128 devices in a mesh: tx: 4 (over z), ty: 32 (over x, y, core).
Axes of the slice: x: 4, y: 4, z: 4, core: 2. Of those that a mesh axis runs over, the one named last changes fastest.
Arguments:
- points: bfloat16 [128, 1024, 256], P(('tx', 'ty')), may hold values from -6 to 6
- counts: int32 [128], P(('tx', 'ty')), may hold values from 512 to 1024, as said below
- owner: int32 [128, 1024], P(('tx', 'ty')), may hold values from 0 to 127, as said below
- zorder: int32 [128, 2048], P(('tx', 'ty')), may hold values from 0 to 2047, as said below
- border: int32 [128, 4, 64], P(('tx', 'ty')), may hold values from 0 to 1023, as said below
- near: int32 [128, 16, 1024], P(('tx', 'ty')), may hold values from 0 to 1279, as said below
- w_near: bfloat16 [256, 256], replicated, may hold values from -0.375 to 0.375
- gain_one: float32 [256], replicated, may hold values from 0.1 to 1.9
- conv_w: bfloat16 [3, 8, 32, 32], replicated, may hold values from -0.625 to 0.625
- gain_two: float32 [256], replicated, may hold values from 0.1 to 1.9
- w_up: bfloat16 [256, 1024], replicated, may hold values from -0.375 to 0.375
- w_down: bfloat16 [1024, 256], replicated, may hold values from -0.1875 to 0.1875
- grad_out: bfloat16 [128, 1024, 256], P(('tx', 'ty')), may hold values from -6 to 6
Outputs:
- out_rows: bfloat16 [128, 1024, 256], P(('tx', 'ty'))
- grad_points: bfloat16 [128, 1024, 256], P(('tx', 'ty'))
- grad_w_near: float32 [256, 256], replicated
- grad_gain_one: float32 [256], replicated
- grad_conv: float32 [3, 8, 32, 32], replicated
- grad_gain_two: float32 [256], replicated
- grad_w_up: float32 [256, 1024], replicated
- grad_w_down: float32 [1024, 256], replicated
The draws below stay inside these ranges and needn't reach their ends.
Inputs may be any that keep to these rules, and one draw needn't show every extreme that they name: `counts`: every tile has at least half of its slots live, and some tile has all of them live. Only live rows count. Among the live rows of one tile at most 16 name the same owner. One particular owner receives exactly 16 live rows from every tile; every other owner receives at most 16 live rows from each tile, so its receive buffer may be partly empty. `zorder`: each owner's entry is a permutation of its 2048 receive slots whose first entries name exactly the filled slots. `border`: each list names distinct live rows of its tile; lists toward a side outside the grid are never read. `near`: indices below 1024 name live rows of the tile; the others name halo rows of blocks whose neighbour tile exists.
All inputs are finite; a program needn't handle non-finite values.
Results may differ from the reference program's by a relative error of at most 0.015.
Values may be sent and summed in bfloat16 or wider, within the bound.
A program may use at most 64 MiB of HBM per device.

```python
import math
import jax
import jax.numpy as jnp
from jax import lax

C = 256
FFN = 1024
GROUPS = 8
PATCH = 1024
K_NEAR = 16
TILE_ROWS = 1024
GW = 32
BORDER = 64
RECV = 2048
TILE_COLS = 4
TILE_LINES = 32
TILES = 128
ALL_ROWS = 131072


def ranked_by(score):
    order = jnp.argsort(score, stable=True).astype(jnp.int32)
    return jnp.zeros(score.shape, jnp.int32).at[order].set(jnp.arange(score.shape[0], dtype=jnp.int32))


def tile_counts(key):
    count_key = jax.random.fold_in(key, 101)
    full_key = jax.random.fold_in(key, 102)
    counts = jax.random.randint(count_key, (TILES,), TILE_ROWS // 2, TILE_ROWS + 1).astype(jnp.int32)
    fullest = jax.random.randint(full_key, (), 0, TILES)
    return counts.at[fullest].set(TILE_ROWS)


def layout_tables(key):
    capacity = RECV // TILES
    counts = tile_counts(key)
    star = jax.random.randint(jax.random.fold_in(key, 103), (), 0, TILES).astype(jnp.int32)
    route_key = jax.random.fold_in(key, 104)
    order_key = jax.random.fold_in(key, 105)
    index = jnp.arange(TILE_ROWS, dtype=jnp.int32)

    def tile_owner(tile_key, count):
        first_key, second_key = jax.random.split(tile_key)
        mixing = jax.random.permutation(first_key, TILE_ROWS).astype(jnp.int32)
        rank = ranked_by(jnp.where(index < count, mixing, TILE_ROWS + mixing))
        others = jax.random.permutation(second_key, TILES - 1).astype(jnp.int32)
        others = others + (others >= star).astype(jnp.int32)
        spread = jnp.take(others, jnp.maximum(rank - capacity, 0) % (TILES - 1))
        return jnp.where(rank < capacity, star, spread).astype(jnp.int32)
    owner = jax.vmap(tile_owner)(jax.random.split(route_key, TILES), counts)
    live = (index[None, :] < counts[:, None]).astype(jnp.int32)
    source = jnp.broadcast_to(jnp.arange(TILES, dtype=jnp.int32)[:, None], owner.shape)
    pair_load = jnp.zeros((TILES, TILES), jnp.int32).at[source, owner].add(live)
    filled = jnp.arange(capacity, dtype=jnp.int32)[None, None, :] < jnp.transpose(pair_load)[:, :, None]
    filled = filled.reshape(TILES, RECV)

    def receiver_order(recv_key, mask):
        mixing = jax.random.permutation(recv_key, RECV).astype(jnp.int32)
        return jnp.argsort(jnp.where(mask, mixing, RECV + mixing), stable=True).astype(jnp.int32)
    zorder = jax.vmap(receiver_order)(jax.random.split(order_key, TILES), filled)
    return (owner, zorder)


def draw_counts(key, part):
    return tile_counts(key)


def draw_owner(key, part):
    return layout_tables(key)[0]


def draw_zorder(key, part):
    return layout_tables(key)[1]


def draw_border(key, part):
    counts = tile_counts(key)
    index = jnp.arange(TILE_ROWS, dtype=jnp.int32)
    list_ids = jnp.arange(4, dtype=jnp.int32)

    def tile_lists(tile_key, count):

        def one_list(list_key, list_id):
            mixing = jax.random.permutation(list_key, TILE_ROWS).astype(jnp.int32)
            mixing = jnp.where((index == count - 1) & (list_id == 0), -1, mixing).astype(jnp.int32)
            order = jnp.argsort(jnp.where(index < count, mixing, TILE_ROWS + mixing), stable=True).astype(jnp.int32)
            return order[:BORDER]
        return jax.vmap(one_list)(jax.random.split(tile_key, 4), list_ids)
    return jax.vmap(tile_lists)(jax.random.split(jax.random.fold_in(key, 201), TILES), counts)


def draw_near(key, part):
    counts = tile_counts(key)
    tile_ids = jnp.arange(TILES, dtype=jnp.int32)
    column = tile_ids // TILE_LINES
    line = tile_ids % TILE_LINES
    present = jnp.stack([column + 1 < TILE_COLS, column > 0, line + 1 < TILE_LINES, line > 0], axis=1)
    slot_index = jnp.arange(K_NEAR, dtype=jnp.int32)[:, None]

    def tile_near(tile_key, count, exists):
        first_key, second_key, third_key, fourth_key = jax.random.split(tile_key, 4)
        inside = jax.random.randint(first_key, (K_NEAR, TILE_ROWS), 0, count).astype(jnp.int32)
        direction = jax.random.randint(second_key, (K_NEAR, TILE_ROWS), 0, 4).astype(jnp.int32)
        offset = jax.random.randint(third_key, (K_NEAR, TILE_ROWS), 0, BORDER).astype(jnp.int32)
        edge_point = jax.random.randint(fourth_key, (1, TILE_ROWS), 0, 4) == 0
        usable = jnp.take(exists, direction) & edge_point & (slot_index < K_NEAR // 2)
        return jnp.where(usable, TILE_ROWS + direction * BORDER + offset, inside).astype(jnp.int32)
    return jax.vmap(tile_near)(jax.random.split(jax.random.fold_in(key, 301), TILES), counts, present)


def shard_levels(stream_key, dims, shards, low, high):
    def one(axis_at, parts):
        steps = jax.random.uniform(jax.random.fold_in(jax.random.fold_in(stream_key, 6), axis_at), (parts,), jnp.float32, low / len(shards), high / len(shards))
        return jnp.repeat(jnp.exp(steps), dims[axis_at] // parts).reshape((-1,) + (1,) * (len(dims) - axis_at - 1))

    level = one(*shards[0])
    for cut in shards[1:]:
        level = level * one(*cut)
    return level


def bell_draw(stream_key, shape, scale, limit, cuts=(), held_as=jnp.bfloat16):
    values = jax.random.normal(stream_key, shape, jnp.float32) * scale
    if len(cuts) > 0:
        values = shard_levels(stream_key, shape, cuts, -0.22, 0.18) * values
    return jnp.clip(values, min=-limit, max=limit).astype(held_as)


def setup_inputs(seed: int = 0) -> dict:
    streams_of = jax.random.split(jax.random.key(seed), 14)
    return {
        "points": bell_draw(streams_of[0], (TILES, TILE_ROWS, C), 1.0, 6.0, ((0, 128),)),
        "counts": draw_counts(jax.random.fold_in(streams_of[13], 71), 0),
        "owner": draw_owner(jax.random.fold_in(streams_of[13], 71), 0),
        "zorder": draw_zorder(jax.random.fold_in(streams_of[13], 71), 0),
        "border": draw_border(jax.random.fold_in(streams_of[13], 71), 0),
        "near": draw_near(jax.random.fold_in(streams_of[13], 71), 0),
        "w_near": bell_draw(streams_of[6], (C, C), C ** -0.5, 0.375),
        "gain_one": jnp.clip(1.0 + 0.18 * jax.random.normal(streams_of[7], (C,), jnp.float32), 0.1, 1.9),
        "conv_w": bell_draw(streams_of[8], (3, GROUPS, GW, GW), (3 * GW) ** -0.5, 0.625),
        "gain_two": jnp.clip(1.0 + 0.18 * jax.random.normal(streams_of[9], (C,), jnp.float32), 0.1, 1.9),
        "w_up": bell_draw(streams_of[10], (C, FFN), C ** -0.5, 0.375),
        "w_down": bell_draw(streams_of[11], (FFN, C), FFN ** -0.5, 0.1875),
        "grad_out": bell_draw(streams_of[12], (TILES, TILE_ROWS, C), 1.0, 6.0, ((0, 128),)),
    }


eps_norm = 1e-06
gelu_coef = 0.7978845608028654
cubic_coef = 0.044715

def gelu_tanh(value):
    inner = gelu_coef * (value + cubic_coef * value * value * value)
    return 0.5 * value * (1.0 + jnp.tanh(inner))

def gelu_slope(value):
    inner = gelu_coef * (value + cubic_coef * value * value * value)
    tangent = jnp.tanh(inner)
    return 0.5 * (1.0 + tangent) + 0.5 * value * (1.0 - tangent * tangent) * gelu_coef * (1.0 + 3.0 * cubic_coef * value * value)

def inverse_rms(value):
    return lax.rsqrt(lax.optimization_barrier(jnp.mean(value * value, axis=-1, keepdims=True)) + eps_norm)

def tile_forward(points_tile, halo_rows, near_tile, w_near):
    extended = jnp.concatenate([points_tile, halo_rows], axis=0)
    count_near = near_tile.shape[0]

    def add_neighbour(index, total):
        return total + jnp.take(extended, near_tile[index], axis=0).astype(jnp.float32)
    total = lax.fori_loop(0, count_near, add_neighbour, jnp.zeros(points_tile.shape, jnp.float32))
    average = (total * (1.0 / count_near)).astype(jnp.bfloat16)
    linear_part = jnp.dot(average, w_near, preferred_element_type=jnp.float32)
    lifted = (points_tile.astype(jnp.float32) + gelu_tanh(linear_part)).astype(jnp.bfloat16)
    return (average, linear_part, lifted)

def tile_backward(lifted_grad, average, linear_part, near_tile, w_near, ext_count):
    count_near = near_tile.shape[0]
    tile_rows = lifted_grad.shape[0]
    act_grad = (lifted_grad.astype(jnp.float32) * gelu_slope(linear_part)).astype(jnp.bfloat16)
    near_grad = lax.dot_general(average, act_grad, (((0,), (0,)), ((), ())), preferred_element_type=jnp.float32)
    spread = lax.dot_general(act_grad, w_near, (((1,), (1,)), ((), ())), preferred_element_type=jnp.float32) * (1.0 / count_near)

    def scatter_neighbour(index, total):
        return total.at[near_tile[index]].add(spread)
    ext_grad = lax.fori_loop(0, count_near, scatter_neighbour, jnp.zeros((ext_count, spread.shape[1]), jnp.float32))
    row_grad = lifted_grad.astype(jnp.float32) + ext_grad[:tile_rows]
    halo_grad = ext_grad[tile_rows:].astype(jnp.bfloat16)
    return (near_grad, row_grad, halo_grad)

def route_ranks(owner_tile, count, tiles):
    tile_rows = owner_tile.shape[0]
    index = jnp.arange(tile_rows, dtype=jnp.int32)
    live = index < count
    score = jnp.where(live, owner_tile * tile_rows + index, tiles * tile_rows + index).astype(jnp.int32)
    order = jnp.argsort(score, stable=True).astype(jnp.int32)
    members = (owner_tile[:, None] == jnp.arange(tiles, dtype=jnp.int32)[None, :]) & live[:, None]
    per_owner = lax.optimization_barrier(jnp.sum(members.astype(jnp.int32), axis=0)).astype(jnp.int32)
    starts = (jnp.cumsum(per_owner) - per_owner).astype(jnp.int32)
    sorted_owner = jnp.take(owner_tile, order)
    ranked = (index - jnp.take(starts, sorted_owner)).astype(jnp.int32)
    rank = jnp.zeros((tile_rows,), jnp.int32).at[order].set(ranked)
    return (rank, live)

def shift_down(rows):
    return jnp.concatenate([jnp.zeros_like(rows[:1]), rows[:-1]], axis=0)

def shift_up(rows):
    return jnp.concatenate([rows[1:], jnp.zeros_like(rows[:1])], axis=0)

def grouped_apply(rows, conv_tap):
    length, width = rows.shape
    split = rows.astype(jnp.float32).reshape(length, conv_tap.shape[0], conv_tap.shape[1])
    return jnp.einsum('pga,gab->pgb', split, conv_tap.astype(jnp.float32)).reshape(length, width)

def grouped_back(rows, conv_tap):
    length, width = rows.shape
    split = rows.astype(jnp.float32).reshape(length, conv_tap.shape[0], conv_tap.shape[1])
    return jnp.einsum('pgb,gab->pga', split, conv_tap.astype(jnp.float32)).reshape(length, width)

def grouped_weight(inputs, outputs, groups, inner):
    length = inputs.shape[0]
    left = inputs.astype(jnp.float32).reshape(length, groups, inner)
    right = outputs.astype(jnp.float32).reshape(length, groups, inner)
    return jnp.einsum('pga,pgb->gab', left, right)

def patch_pass(serial, out_grad, gain_one, conv_w, gain_two, w_up, w_down):
    groups, inner = (conv_w.shape[1], conv_w.shape[2])
    serial_f = serial.astype(jnp.float32)
    scale_one = inverse_rms(serial_f)
    normed = (serial_f * scale_one * gain_one).astype(jnp.bfloat16)
    taps = (shift_down(normed), normed, shift_up(normed))
    mixed = grouped_apply(taps[0], conv_w[0]) + grouped_apply(taps[1], conv_w[1]) + grouped_apply(taps[2], conv_w[2])
    state = serial_f + mixed
    scale_two = inverse_rms(state)
    second = (state * scale_two * gain_two).astype(jnp.bfloat16)
    hidden_pre = jnp.dot(second, w_up, preferred_element_type=jnp.float32)
    hidden = gelu_tanh(hidden_pre).astype(jnp.bfloat16)
    result = (state + jnp.dot(hidden, w_down, preferred_element_type=jnp.float32)).astype(jnp.bfloat16)
    down_grad = lax.dot_general(hidden, out_grad, (((0,), (0,)), ((), ())), preferred_element_type=jnp.float32)
    hidden_grad = lax.dot_general(out_grad, w_down, (((1,), (1,)), ((), ())), preferred_element_type=jnp.float32).astype(jnp.bfloat16)
    pre_grad = (hidden_grad.astype(jnp.float32) * gelu_slope(hidden_pre)).astype(jnp.bfloat16)
    up_grad = lax.dot_general(second, pre_grad, (((0,), (0,)), ((), ())), preferred_element_type=jnp.float32)
    second_grad = lax.dot_general(pre_grad, w_up, (((1,), (1,)), ((), ())), preferred_element_type=jnp.float32).astype(jnp.bfloat16)
    unit_two = state * scale_two
    weighted_two = second_grad.astype(jnp.float32) * gain_two
    gain_two_grad = lax.optimization_barrier(jnp.sum(second_grad.astype(jnp.float32) * unit_two, axis=0))
    state_grad = out_grad.astype(jnp.float32) + scale_two * (weighted_two - unit_two * lax.optimization_barrier(jnp.mean(weighted_two * unit_two, axis=-1, keepdims=True)))
    mixed_grad = state_grad.astype(jnp.bfloat16)
    conv_grad = jnp.stack([grouped_weight(taps[0], mixed_grad, groups, inner), grouped_weight(taps[1], mixed_grad, groups, inner), grouped_weight(taps[2], mixed_grad, groups, inner)], axis=0)
    normed_grad = (shift_up(grouped_back(mixed_grad, conv_w[0])) + grouped_back(mixed_grad, conv_w[1]) + shift_down(grouped_back(mixed_grad, conv_w[2]))).astype(jnp.bfloat16)
    unit_one = serial_f * scale_one
    weighted_one = normed_grad.astype(jnp.float32) * gain_one
    gain_one_grad = lax.optimization_barrier(jnp.sum(normed_grad.astype(jnp.float32) * unit_one, axis=0))
    serial_grad = (state_grad + scale_one * (weighted_one - unit_one * lax.optimization_barrier(jnp.mean(weighted_one * unit_one, axis=-1, keepdims=True)))).astype(jnp.bfloat16)
    return (result, serial_grad, (gain_one_grad, conv_grad, gain_two_grad, up_grad, down_grad))

def gather_halo(sent):
    border_rows, width = (sent.shape[2], sent.shape[3])
    grid = sent.reshape(TILE_COLS, TILE_LINES, 4, border_rows, width)
    zeros_col = jnp.zeros((1, TILE_LINES, border_rows, width), sent.dtype)
    zeros_line = jnp.zeros((TILE_COLS, 1, border_rows, width), sent.dtype)
    from_next_col = jnp.concatenate([grid[1:, :, 0], zeros_col], axis=0)
    from_prev_col = jnp.concatenate([zeros_col, grid[:-1, :, 1]], axis=0)
    from_next_line = jnp.concatenate([grid[:, 1:, 2], zeros_line], axis=1)
    from_prev_line = jnp.concatenate([zeros_line, grid[:, :-1, 3]], axis=1)
    stacked = jnp.stack([from_next_col, from_prev_col, from_next_line, from_prev_line], axis=2)
    return stacked.reshape(TILE_COLS * TILE_LINES, 4 * border_rows, width)

def return_halo(halo_grads, border_rows):
    width = halo_grads.shape[2]
    grid = halo_grads.reshape(TILE_COLS, TILE_LINES, 4, border_rows, width)
    zeros_col = jnp.zeros((1, TILE_LINES, border_rows, width), halo_grads.dtype)
    zeros_line = jnp.zeros((TILE_COLS, 1, border_rows, width), halo_grads.dtype)
    back_zero = jnp.concatenate([zeros_col, grid[:-1, :, 0]], axis=0)
    back_one = jnp.concatenate([grid[1:, :, 1], zeros_col], axis=0)
    back_two = jnp.concatenate([zeros_line, grid[:, :-1, 2]], axis=1)
    back_three = jnp.concatenate([grid[:, 1:, 3], zeros_line], axis=1)
    stacked = jnp.stack([back_zero, back_one, back_two, back_three], axis=2)
    return stacked.reshape(TILE_COLS * TILE_LINES, 4, border_rows, width)

def reference(points, counts, owner, zorder, border, near, w_near, gain_one, conv_w, gain_two, w_up, w_down, grad_out):
    tiles = TILES
    tile_rows = TILE_ROWS
    width = points.shape[2]
    capacity = RECV // tiles
    border_rows = border.shape[2]
    sent = jax.vmap(lambda rows, lists: jnp.take(rows, lists.reshape(-1), axis=0).reshape(4, border_rows, width))(points, border)
    halo = gather_halo(sent)
    lifted = lax.map(lambda item: tile_forward(item[0], item[1], item[2], w_near)[2], (points, halo, near))
    rank, live = jax.vmap(lambda owned, count: route_ranks(owned, count, tiles))(owner, counts)
    source = jnp.arange(tiles, dtype=jnp.int32)[:, None]
    target = jnp.where(live, owner * RECV + source * capacity + rank, tiles * RECV).astype(jnp.int32)
    row_ids = jnp.arange(tiles * tile_rows, dtype=jnp.int32)
    buffer_ids = jnp.full((tiles * RECV,), tiles * tile_rows, jnp.int32).at[target.reshape(-1)].set(row_ids, mode='drop')
    serial_ids = jnp.take_along_axis(buffer_ids.reshape(tiles, RECV), zorder, axis=1).reshape(-1)
    serial = jnp.take(lifted.reshape(-1, width), serial_ids, axis=0, mode='fill', fill_value=0)
    serial_out_grad = jnp.take(grad_out.reshape(-1, width), serial_ids, axis=0, mode='fill', fill_value=0)
    zero_sums = (jnp.zeros((width,), jnp.float32), jnp.zeros(conv_w.shape, jnp.float32), jnp.zeros((width,), jnp.float32), jnp.zeros(w_up.shape, jnp.float32), jnp.zeros(w_down.shape, jnp.float32))

    def patch_step(carry, block):
        result, serial_grad, grads = patch_pass(block[0], block[1], gain_one, conv_w, gain_two, w_up, w_down)
        return (jax.tree.map(lambda left, right: left + right, carry, grads), (result, serial_grad))
    sums, (results, serial_grads) = lax.scan(patch_step, zero_sums, (serial.reshape(-1, PATCH, width), serial_out_grad.reshape(-1, PATCH, width)))
    out_flat = jnp.zeros((tiles * tile_rows, width), jnp.bfloat16).at[serial_ids].set(results.reshape(-1, width), mode='drop')
    lifted_grad = jnp.zeros((tiles * tile_rows, width), jnp.bfloat16).at[serial_ids].set(serial_grads.reshape(-1, width), mode='drop')

    def tile_step(carry, item):
        average, linear_part, unused = tile_forward(item[0], item[1], item[2], w_near)
        near_grad, row_grad, halo_grad = tile_backward(item[3], average, linear_part, item[2], w_near, tile_rows + 4 * border_rows)
        return (carry + near_grad, (row_grad, halo_grad))
    near_sum, (row_grads, halo_grads) = lax.scan(tile_step, jnp.zeros(w_near.shape, jnp.float32), (points, halo, near, lifted_grad.reshape(points.shape)))
    returned = return_halo(halo_grads, border_rows)

    def add_returned(row_grad, lists, back):
        return row_grad.at[lists.reshape(-1)].add(back.reshape(-1, width).astype(jnp.float32))
    row_grads = jax.vmap(add_returned)(row_grads, border, returned)
    scale = 1.0 / math.sqrt(ALL_ROWS)
    return (out_flat.reshape(points.shape), row_grads.astype(jnp.bfloat16), near_sum * scale, sums[0] * scale, sums[1] * scale, sums[2] * scale, sums[3] * scale, sums[4] * scale)
```

```python
import math

import jax
import jax.numpy as jnp
from jax import lax
from jax.sharding import PartitionSpec as P

PATCH = 1024


eps_norm = 1e-06
gelu_coef = 0.7978845608028654
cubic_coef = 0.044715


def shifted(value, axis, steps):
    count = lax.axis_size(axis)
    initial, last = (max(0, -steps), min(count, count - steps))
    return lax.ppermute(value, axis, [(source, source + steps) for source in range(initial, last)])


def gelu_tanh(value):
    inner = gelu_coef * (value + cubic_coef * value * value * value)
    return 0.5 * value * (1.0 + jnp.tanh(inner))


def gelu_slope(value):
    inner = gelu_coef * (value + cubic_coef * value * value * value)
    tangent = jnp.tanh(inner)
    return 0.5 * (1.0 + tangent) + 0.5 * value * (1.0 - tangent * tangent) * gelu_coef * (
        1.0 + 3.0 * cubic_coef * value * value
    )


def inverse_rms(value):
    return lax.rsqrt(jnp.mean(value * value, axis=-1, keepdims=True) + eps_norm)


def near_counts(near_tile, ext_count):
    rows = lax.broadcasted_iota(jnp.int32, (ext_count, near_tile.shape[1]), 0)
    total = jnp.zeros((ext_count, near_tile.shape[1]), jnp.float32)
    for index in range(near_tile.shape[0]):
        total = total + (near_tile[index][None, :] == rows).astype(jnp.float32)
    return total.astype(jnp.bfloat16)


def tile_forward(points_tile, halo_rows, counts_t, w_near, count_near):
    extended = jnp.concatenate([points_tile, halo_rows], axis=0)
    total = lax.dot_general(
        counts_t, extended, (((0,), (0,)), ((), ())), preferred_element_type=jnp.float32
    )
    average = (total * (1.0 / count_near)).astype(jnp.bfloat16)
    linear_part = jnp.dot(average, w_near, preferred_element_type=jnp.float32)
    lifted = (points_tile.astype(jnp.float32) + gelu_tanh(linear_part)).astype(jnp.bfloat16)
    return (average, linear_part, lifted)


def tile_backward(lifted_grad, average, linear_part, counts_t, w_near, count_near):
    tile_rows = lifted_grad.shape[0]
    act_grad = (lifted_grad.astype(jnp.float32) * gelu_slope(linear_part)).astype(jnp.bfloat16)
    near_grad = lax.dot_general(
        average, act_grad, (((0,), (0,)), ((), ())), preferred_element_type=jnp.float32
    )
    spread = lax.dot_general(
        act_grad, w_near, (((1,), (1,)), ((), ())), preferred_element_type=jnp.float32
    ) * (1.0 / count_near)
    spread_hi = spread.astype(jnp.bfloat16)
    spread_lo = (spread - spread_hi.astype(jnp.float32)).astype(jnp.bfloat16)
    ext_grad = jnp.dot(counts_t, spread_hi, preferred_element_type=jnp.float32) + jnp.dot(
        counts_t, spread_lo, preferred_element_type=jnp.float32
    )
    row_grad = lifted_grad.astype(jnp.float32) + ext_grad[:tile_rows]
    halo_grad = ext_grad[tile_rows:].astype(jnp.bfloat16)
    return (near_grad, row_grad, halo_grad)


def route_ranks(owner_tile, count, tiles):
    tile_rows = owner_tile.shape[0]
    index = jnp.arange(tile_rows, dtype=jnp.int32)
    live = index < count
    score = jnp.where(live, owner_tile * tile_rows + index, tiles * tile_rows + index)
    order = jnp.argsort(score, stable=True)
    members = (owner_tile[:, None] == jnp.arange(tiles, dtype=jnp.int32)[None, :]) & live[:, None]
    per_owner = jnp.sum(members.astype(jnp.int32), axis=0)
    starts = jnp.cumsum(per_owner) - per_owner
    sorted_owner = jnp.take(owner_tile, order)
    ranked = index - jnp.take(starts, sorted_owner)
    rank = jnp.zeros((tile_rows,), jnp.int32).at[order].set(ranked)
    return (rank, live)


def shift_down(rows):
    return jnp.concatenate([jnp.zeros_like(rows[:1]), rows[:-1]], axis=0)


def shift_up(rows):
    return jnp.concatenate([rows[1:], jnp.zeros_like(rows[:1])], axis=0)


def block_taps(conv_w):
    groups, inner = (conv_w.shape[1], conv_w.shape[2])
    identity_blocks = jnp.eye(groups, dtype=conv_w.dtype)
    full = jnp.einsum("gh,ogab->ogahb", identity_blocks, conv_w)
    return full.reshape(conv_w.shape[0], groups * inner, groups * inner)


def grouped_weight(inputs, outputs, groups, inner):
    length = inputs.shape[0]
    left = inputs.reshape(length, groups, inner)
    right = outputs.reshape(length, groups, inner)
    return jnp.einsum("pga,pgb->gab", left, right, preferred_element_type=jnp.float32)


def tap_back(rows, tap):
    return lax.dot_general(rows, tap, (((1,), (1,)), ((), ())), preferred_element_type=jnp.float32)


def patch_pass(serial, out_grad, gain_one, conv_w, taps_full, gain_two, w_up, w_down):
    groups, inner = (conv_w.shape[1], conv_w.shape[2])
    serial_f = serial.astype(jnp.float32)
    scale_one = inverse_rms(serial_f)
    normed = (serial_f * scale_one * gain_one).astype(jnp.bfloat16)
    taps = (shift_down(normed), normed, shift_up(normed))
    mixed = (
        jnp.dot(taps[0], taps_full[0], preferred_element_type=jnp.float32)
        + jnp.dot(taps[1], taps_full[1], preferred_element_type=jnp.float32)
        + jnp.dot(taps[2], taps_full[2], preferred_element_type=jnp.float32)
    )
    state = serial_f + mixed
    scale_two = inverse_rms(state)
    second = (state * scale_two * gain_two).astype(jnp.bfloat16)
    hidden_pre = jnp.dot(second, w_up, preferred_element_type=jnp.float32)
    hidden = gelu_tanh(hidden_pre).astype(jnp.bfloat16)
    result = (state + jnp.dot(hidden, w_down, preferred_element_type=jnp.float32)).astype(
        jnp.bfloat16
    )
    down_grad = lax.dot_general(
        hidden, out_grad, (((0,), (0,)), ((), ())), preferred_element_type=jnp.float32
    )
    hidden_grad = lax.dot_general(
        out_grad, w_down, (((1,), (1,)), ((), ())), preferred_element_type=jnp.float32
    ).astype(jnp.bfloat16)
    pre_grad = (hidden_grad.astype(jnp.float32) * gelu_slope(hidden_pre)).astype(jnp.bfloat16)
    up_grad = lax.dot_general(
        second, pre_grad, (((0,), (0,)), ((), ())), preferred_element_type=jnp.float32
    )
    second_grad = lax.dot_general(
        pre_grad, w_up, (((1,), (1,)), ((), ())), preferred_element_type=jnp.float32
    ).astype(jnp.bfloat16)
    unit_two = state * scale_two
    weighted_two = second_grad.astype(jnp.float32) * gain_two
    gain_two_grad = jnp.sum(second_grad.astype(jnp.float32) * unit_two, axis=0)
    state_grad = out_grad.astype(jnp.float32) + scale_two * (
        weighted_two - unit_two * jnp.mean(weighted_two * unit_two, axis=-1, keepdims=True)
    )
    mixed_grad = state_grad.astype(jnp.bfloat16)
    conv_grad = jnp.stack(
        [
            grouped_weight(taps[0], mixed_grad, groups, inner),
            grouped_weight(taps[1], mixed_grad, groups, inner),
            grouped_weight(taps[2], mixed_grad, groups, inner),
        ],
        axis=0,
    )
    normed_grad = (
        shift_up(tap_back(mixed_grad, taps_full[0]))
        + tap_back(mixed_grad, taps_full[1])
        + shift_down(tap_back(mixed_grad, taps_full[2]))
    ).astype(jnp.bfloat16)
    unit_one = serial_f * scale_one
    weighted_one = normed_grad.astype(jnp.float32) * gain_one
    gain_one_grad = jnp.sum(normed_grad.astype(jnp.float32) * unit_one, axis=0)
    serial_grad = (
        state_grad
        + scale_one
        * (weighted_one - unit_one * jnp.mean(weighted_one * unit_one, axis=-1, keepdims=True))
    ).astype(jnp.bfloat16)
    return (result, serial_grad, (gain_one_grad, conv_grad, gain_two_grad, up_grad, down_grad))


def pass_columns(rows, shift_by):
    return shifted(rows, "tx", shift_by)


def pass_lines(rows, shift_by):
    return shifted(rows, "ty", shift_by)


def body(
    points,
    counts,
    owner,
    zorder,
    border,
    near,
    w_near,
    gain_one,
    conv_w,
    gain_two,
    w_up,
    w_down,
    grad_out,
):
    points_tile = points[0]
    tile_rows, width = points_tile.shape
    lists = border[0]
    border_rows = lists.shape[1]
    cols_count = lax.axis_size("tx")
    lines_count = lax.axis_size("ty")
    tiles = cols_count * lines_count
    recv_rows = zorder.shape[1]
    capacity = recv_rows // tiles
    near_tile = near[0]
    owner_tile = owner[0]
    sent = jnp.take(points_tile, lists.reshape(-1), axis=0).reshape(4, border_rows, width)
    halo = jnp.concatenate(
        [
            pass_columns(sent[0], -1),
            pass_columns(sent[1], 1),
            pass_lines(sent[2], -1),
            pass_lines(sent[3], 1),
        ],
        axis=0,
    )
    count_near = near_tile.shape[0]
    counts_t = near_counts(near_tile, tile_rows + 4 * border_rows)
    average, linear_part, lifted = tile_forward(points_tile, halo, counts_t, w_near, count_near)
    rank, live = route_ranks(owner_tile, counts[0], tiles)
    slots = jnp.where(live, owner_tile * capacity + rank, tiles * capacity)
    payload = jnp.concatenate([lifted, grad_out[0]], axis=1)
    outgoing = (
        jnp.zeros((tiles * capacity, 2 * width), jnp.bfloat16).at[slots].set(payload, mode="drop")
    )
    incoming = lax.all_to_all(outgoing, ("tx", "ty"), split_axis=0, concat_axis=0, tiled=True)
    serial_both = jnp.take(incoming, zorder[0], axis=0)
    taps_full = block_taps(conv_w)
    zero_sums = (
        jnp.zeros((width,), jnp.float32),
        jnp.zeros(conv_w.shape, jnp.float32),
        jnp.zeros((width,), jnp.float32),
        jnp.zeros(w_up.shape, jnp.float32),
        jnp.zeros(w_down.shape, jnp.float32),
    )

    def patch_step(carry, block):
        result, serial_grad, grads = patch_pass(
            block[:, :width], block[:, width:], gain_one, conv_w, taps_full, gain_two, w_up, w_down
        )
        return (jax.tree.map(lambda left, right: left + right, carry, grads), (result, serial_grad))

    sums, (results, serial_grads) = lax.scan(
        patch_step, zero_sums, serial_both.reshape(recv_rows // PATCH, PATCH, 2 * width)
    )
    back = jnp.concatenate(
        [results.reshape(recv_rows, width), serial_grads.reshape(recv_rows, width)], axis=1
    )
    back_slots = jnp.zeros_like(back).at[zorder[0]].set(back)
    returned = lax.all_to_all(back_slots, ("tx", "ty"), split_axis=0, concat_axis=0, tiled=True)
    back_rows = jnp.take(returned, slots, axis=0, mode="fill", fill_value=0)
    out_rows = back_rows[:, :width]
    lifted_grad = back_rows[:, width:]
    patch_flat = jnp.concatenate(
        [sums[0], sums[2], sums[1].reshape(-1), sums[3].reshape(-1), sums[4].reshape(-1)]
    )
    patch_total = lax.psum(patch_flat, ("tx", "ty"))
    near_grad, row_grad, halo_grad = tile_backward(
        lifted_grad, average, linear_part, counts_t, w_near, count_near
    )
    came_back = (
        pass_columns(halo_grad[0:border_rows], 1),
        pass_columns(halo_grad[border_rows : 2 * border_rows], -1),
        pass_lines(halo_grad[2 * border_rows : 3 * border_rows], 1),
        pass_lines(halo_grad[3 * border_rows : 4 * border_rows], -1),
    )
    for direction in range(4):
        row_grad = row_grad.at[lists[direction]].add(came_back[direction].astype(jnp.float32))
    near_sum = lax.psum(near_grad, ("tx", "ty"))
    sizes = [width, width, conv_w.size, w_up.size, w_down.size]
    shapes = [(width,), (width,), conv_w.shape, w_up.shape, w_down.shape]
    offsets = [sum(sizes[:index]) for index in range(len(sizes))]
    gain_one_sum, gain_two_sum, conv_sum, up_sum, down_sum = [
        patch_total[start : start + size].reshape(shape)
        for start, size, shape in zip(offsets, sizes, shapes)
    ]
    totals = (gain_one_sum, conv_sum, gain_two_sum, up_sum, down_sum)
    scale = 1.0 / math.sqrt(tiles * tile_rows)
    return (
        out_rows[None],
        row_grad.astype(jnp.bfloat16)[None],
        near_sum * scale,
        totals[0] * scale,
        totals[1] * scale,
        totals[2] * scale,
        totals[3] * scale,
        totals[4] * scale,
    )


def solution(mesh):
    placed = (
        P(("tx", "ty"), None, None),
        P(("tx", "ty")),
        P(("tx", "ty"), None),
        P(("tx", "ty"), None),
        P(("tx", "ty"), None, None),
        P(("tx", "ty"), None, None),
        P(),
        P(),
        P(),
        P(),
        P(),
        P(),
        P(("tx", "ty"), None, None),
    )
    return jax.shard_map(
        body,
        mesh=mesh,
        in_specs=placed,
        out_specs=(
            P(("tx", "ty"), None, None),
            P(("tx", "ty"), None, None),
            P(),
            P(),
            P(),
            P(),
            P(),
            P(),
        ),
        check_vma=False,
    )
```

```python
import math

import jax
import jax.numpy as jnp
from jax import lax
from jax.sharding import PartitionSpec as P

PATCH = 1024


eps_norm = 1e-06
gelu_coef = 0.7978845608028654
cubic_coef = 0.044715


def shifted(value, axis, steps):
    count = lax.axis_size(axis)
    initial, last = (max(0, -steps), min(count, count - steps))
    return lax.ppermute(value, axis, [(source, source + steps) for source in range(initial, last)])


def gelu_tanh(value):
    inner = gelu_coef * (value + cubic_coef * value * value * value)
    return 0.5 * value * (1.0 + jnp.tanh(inner))


def gelu_slope(value):
    inner = gelu_coef * (value + cubic_coef * value * value * value)
    tangent = jnp.tanh(inner)
    return 0.5 * (1.0 + tangent) + 0.5 * value * (1.0 - tangent * tangent) * gelu_coef * (
        1.0 + 3.0 * cubic_coef * value * value
    )


def inverse_rms(value):
    return lax.rsqrt(jnp.mean(value * value, axis=-1, keepdims=True) + eps_norm)


def near_counts(near_tile, ext_count):
    rows = lax.broadcasted_iota(jnp.int32, (ext_count, near_tile.shape[1]), 0)
    total = jnp.zeros((ext_count, near_tile.shape[1]), jnp.float32)
    for index in range(near_tile.shape[0]):
        total = total + (near_tile[index][None, :] == rows).astype(jnp.float32)
    return total.astype(jnp.bfloat16)


def tile_forward(points_tile, halo_rows, counts_t, w_near, count_near):
    extended = jnp.concatenate([points_tile, halo_rows], axis=0)
    total = lax.dot_general(
        counts_t, extended, (((0,), (0,)), ((), ())), preferred_element_type=jnp.float32
    )
    average = (total * (1.0 / count_near)).astype(jnp.bfloat16)
    linear_part = jnp.dot(average, w_near, preferred_element_type=jnp.float32)
    lifted = (points_tile.astype(jnp.float32) + gelu_tanh(linear_part)).astype(jnp.bfloat16)
    return (average, linear_part, lifted)


def tile_backward(lifted_grad, average, linear_part, counts_t, w_near, count_near):
    tile_rows = lifted_grad.shape[0]
    act_grad = (lifted_grad.astype(jnp.float32) * gelu_slope(linear_part)).astype(jnp.bfloat16)
    near_grad = lax.dot_general(
        average, act_grad, (((0,), (0,)), ((), ())), preferred_element_type=jnp.float32
    )
    spread = lax.dot_general(
        act_grad, w_near, (((1,), (1,)), ((), ())), preferred_element_type=jnp.float32
    ) * (1.0 / count_near)
    spread_hi = spread.astype(jnp.bfloat16)
    spread_lo = (spread - spread_hi.astype(jnp.float32)).astype(jnp.bfloat16)
    ext_grad = jnp.dot(counts_t, spread_hi, preferred_element_type=jnp.float32) + jnp.dot(
        counts_t, spread_lo, preferred_element_type=jnp.float32
    )
    row_grad = lifted_grad.astype(jnp.float32) + ext_grad[:tile_rows]
    halo_grad = ext_grad[tile_rows:].astype(jnp.bfloat16)
    return (near_grad, row_grad, halo_grad)


def route_ranks(owner_tile, count, tiles):
    tile_rows = owner_tile.shape[0]
    index = jnp.arange(tile_rows, dtype=jnp.int32)
    live = index < count
    score = jnp.where(live, owner_tile * tile_rows + index, tiles * tile_rows + index)
    order = jnp.argsort(score, stable=True)
    members = (owner_tile[:, None] == jnp.arange(tiles, dtype=jnp.int32)[None, :]) & live[:, None]
    per_owner = jnp.sum(members.astype(jnp.int32), axis=0)
    starts = jnp.cumsum(per_owner) - per_owner
    sorted_owner = jnp.take(owner_tile, order)
    ranked = index - jnp.take(starts, sorted_owner)
    rank = jnp.zeros((tile_rows,), jnp.int32).at[order].set(ranked)
    return (rank, live)


def shift_down(rows):
    patches = rows.reshape(-1, PATCH, rows.shape[-1])
    moved = jnp.concatenate([jnp.zeros_like(patches[:, :1]), patches[:, :-1]], axis=1)
    return moved.reshape(rows.shape)


def shift_up(rows):
    patches = rows.reshape(-1, PATCH, rows.shape[-1])
    moved = jnp.concatenate([patches[:, 1:], jnp.zeros_like(patches[:, :1])], axis=1)
    return moved.reshape(rows.shape)


def block_taps(conv_w):
    groups, inner = (conv_w.shape[1], conv_w.shape[2])
    identity_blocks = jnp.eye(groups, dtype=conv_w.dtype)
    full = jnp.einsum("gh,ogab->ogahb", identity_blocks, conv_w)
    return full.reshape(conv_w.shape[0], groups * inner, groups * inner)


def grouped_weight(inputs, outputs, groups, inner):
    length = inputs.shape[0]
    left = inputs.reshape(length, groups, inner)
    right = outputs.reshape(length, groups, inner)
    return jnp.einsum("pga,pgb->gab", left, right, preferred_element_type=jnp.float32)


def tap_back(rows, tap):
    return lax.dot_general(rows, tap, (((1,), (1,)), ((), ())), preferred_element_type=jnp.float32)


def patch_pass(serial, out_grad, gain_one, conv_w, taps_full, gain_two, w_up, w_down):
    groups, inner = (conv_w.shape[1], conv_w.shape[2])
    serial_f = serial.astype(jnp.float32)
    scale_one = inverse_rms(serial_f)
    normed = (serial_f * scale_one * gain_one).astype(jnp.bfloat16)
    taps = (shift_down(normed), normed, shift_up(normed))
    mixed = (
        jnp.dot(taps[0], taps_full[0], preferred_element_type=jnp.float32)
        + jnp.dot(taps[1], taps_full[1], preferred_element_type=jnp.float32)
        + jnp.dot(taps[2], taps_full[2], preferred_element_type=jnp.float32)
    )
    state = serial_f + mixed
    scale_two = inverse_rms(state)
    second = (state * scale_two * gain_two).astype(jnp.bfloat16)
    hidden_pre = jnp.dot(second, w_up, preferred_element_type=jnp.float32)
    hidden = gelu_tanh(hidden_pre).astype(jnp.bfloat16)
    result = (state + jnp.dot(hidden, w_down, preferred_element_type=jnp.float32)).astype(
        jnp.bfloat16
    )
    down_grad = lax.dot_general(
        hidden, out_grad, (((0,), (0,)), ((), ())), preferred_element_type=jnp.float32
    )
    hidden_grad = lax.dot_general(
        out_grad, w_down, (((1,), (1,)), ((), ())), preferred_element_type=jnp.float32
    ).astype(jnp.bfloat16)
    pre_grad = (hidden_grad.astype(jnp.float32) * gelu_slope(hidden_pre)).astype(jnp.bfloat16)
    up_grad = lax.dot_general(
        second, pre_grad, (((0,), (0,)), ((), ())), preferred_element_type=jnp.float32
    )
    second_grad = lax.dot_general(
        pre_grad, w_up, (((1,), (1,)), ((), ())), preferred_element_type=jnp.float32
    ).astype(jnp.bfloat16)
    unit_two = state * scale_two
    weighted_two = second_grad.astype(jnp.float32) * gain_two
    gain_two_grad = jnp.sum(second_grad.astype(jnp.float32) * unit_two, axis=0)
    state_grad = out_grad.astype(jnp.float32) + scale_two * (
        weighted_two - unit_two * jnp.mean(weighted_two * unit_two, axis=-1, keepdims=True)
    )
    mixed_grad = state_grad.astype(jnp.bfloat16)
    conv_grad = jnp.stack(
        [
            grouped_weight(taps[0], mixed_grad, groups, inner),
            grouped_weight(taps[1], mixed_grad, groups, inner),
            grouped_weight(taps[2], mixed_grad, groups, inner),
        ],
        axis=0,
    )
    normed_grad = (
        shift_up(tap_back(mixed_grad, taps_full[0]))
        + tap_back(mixed_grad, taps_full[1])
        + shift_down(tap_back(mixed_grad, taps_full[2]))
    ).astype(jnp.bfloat16)
    unit_one = serial_f * scale_one
    weighted_one = normed_grad.astype(jnp.float32) * gain_one
    gain_one_grad = jnp.sum(normed_grad.astype(jnp.float32) * unit_one, axis=0)
    serial_grad = (
        state_grad
        + scale_one
        * (weighted_one - unit_one * jnp.mean(weighted_one * unit_one, axis=-1, keepdims=True))
    ).astype(jnp.bfloat16)
    return (result, serial_grad, (gain_one_grad, conv_grad, gain_two_grad, up_grad, down_grad))


def pass_columns(rows, shift_by):
    return shifted(rows, "tx", shift_by)


def pass_lines(rows, shift_by):
    return shifted(rows, "ty", shift_by)


def body(
    points,
    counts,
    owner,
    zorder,
    border,
    near,
    w_near,
    gain_one,
    conv_w,
    gain_two,
    w_up,
    w_down,
    grad_out,
):
    points_tile = points[0]
    tile_rows, width = points_tile.shape
    lists = border[0]
    border_rows = lists.shape[1]
    cols_count = lax.axis_size("tx")
    lines_count = lax.axis_size("ty")
    tiles = cols_count * lines_count
    recv_rows = zorder.shape[1]
    capacity = recv_rows // tiles
    near_tile = near[0]
    owner_tile = owner[0]
    sent = jnp.take(points_tile, lists.reshape(-1), axis=0).reshape(4, border_rows, width)
    halo = jnp.concatenate(
        [
            pass_columns(sent[0], -1),
            pass_columns(sent[1], 1),
            pass_lines(sent[2], -1),
            pass_lines(sent[3], 1),
        ],
        axis=0,
    )
    count_near = near_tile.shape[0]
    counts_t = near_counts(near_tile, tile_rows + 4 * border_rows)
    average, linear_part, lifted = tile_forward(points_tile, halo, counts_t, w_near, count_near)
    rank, live = route_ranks(owner_tile, counts[0], tiles)
    slots = jnp.where(live, owner_tile * capacity + rank, tiles * capacity)
    payload = jnp.concatenate([lifted, grad_out[0]], axis=1)
    outgoing = (
        jnp.zeros((tiles * capacity, 2 * width), jnp.bfloat16).at[slots].set(payload, mode="drop")
    )
    incoming = lax.all_to_all(outgoing, ("tx", "ty"), split_axis=0, concat_axis=0, tiled=True)
    serial_both = jnp.take(incoming, zorder[0], axis=0)
    taps_full = block_taps(conv_w)

    results, serial_grads, sums = patch_pass(
        serial_both[:, :width], serial_both[:, width:], gain_one, conv_w, taps_full, gain_two, w_up, w_down
    )
    back = jnp.concatenate(
        [results.reshape(recv_rows, width), serial_grads.reshape(recv_rows, width)], axis=1
    )
    back_slots = jnp.zeros_like(back).at[zorder[0]].set(back)
    returned = lax.all_to_all(back_slots, ("tx", "ty"), split_axis=0, concat_axis=0, tiled=True)
    back_rows = jnp.take(returned, slots, axis=0, mode="fill", fill_value=0)
    out_rows = back_rows[:, :width]
    lifted_grad = back_rows[:, width:]
    patch_flat = jnp.concatenate(
        [sums[0], sums[2], sums[1].reshape(-1), sums[3].reshape(-1), sums[4].reshape(-1)]
    )
    patch_total = lax.psum(patch_flat, ("tx", "ty"))
    near_grad, row_grad, halo_grad = tile_backward(
        lifted_grad, average, linear_part, counts_t, w_near, count_near
    )
    came_back = (
        pass_columns(halo_grad[0:border_rows], 1),
        pass_columns(halo_grad[border_rows : 2 * border_rows], -1),
        pass_lines(halo_grad[2 * border_rows : 3 * border_rows], 1),
        pass_lines(halo_grad[3 * border_rows : 4 * border_rows], -1),
    )
    for direction in range(4):
        row_grad = row_grad.at[lists[direction]].add(came_back[direction].astype(jnp.float32))
    row_grad, near_grad, patch_total = lax.optimization_barrier((row_grad, near_grad, patch_total))
    near_sum = lax.psum(near_grad, ("tx", "ty"))
    sizes = [width, width, conv_w.size, w_up.size, w_down.size]
    shapes = [(width,), (width,), conv_w.shape, w_up.shape, w_down.shape]
    offsets = [sum(sizes[:index]) for index in range(len(sizes))]
    gain_one_sum, gain_two_sum, conv_sum, up_sum, down_sum = [
        patch_total[start : start + size].reshape(shape)
        for start, size, shape in zip(offsets, sizes, shapes)
    ]
    totals = (gain_one_sum, conv_sum, gain_two_sum, up_sum, down_sum)
    scale = 1.0 / math.sqrt(tiles * tile_rows)
    return (
        out_rows[None],
        row_grad.astype(jnp.bfloat16)[None],
        near_sum * scale,
        totals[0] * scale,
        totals[1] * scale,
        totals[2] * scale,
        totals[3] * scale,
        totals[4] * scale,
    )


def solution(mesh):
    placed = (
        P(("tx", "ty"), None, None),
        P(("tx", "ty")),
        P(("tx", "ty"), None),
        P(("tx", "ty"), None),
        P(("tx", "ty"), None, None),
        P(("tx", "ty"), None, None),
        P(),
        P(),
        P(),
        P(),
        P(),
        P(),
        P(("tx", "ty"), None, None),
    )
    return jax.shard_map(
        body,
        mesh=mesh,
        in_specs=placed,
        out_specs=(
            P(("tx", "ty"), None, None),
            P(("tx", "ty"), None, None),
            P(),
            P(),
            P(),
            P(),
            P(),
            P(),
        ),
        check_vma=False,
    )
```

```python
import math

import jax
import jax.numpy as jnp
from jax import lax
from jax.sharding import PartitionSpec as P

PATCH = 1024


eps_norm = 1e-06
gelu_coef = 0.7978845608028654
cubic_coef = 0.044715


def shifted(value, axis, steps):
    count = lax.axis_size(axis)
    initial, last = (max(0, -steps), min(count, count - steps))
    return lax.ppermute(value, axis, [(source, source + steps) for source in range(initial, last)])


def gelu_tanh(value):
    inner = gelu_coef * (value + cubic_coef * value * value * value)
    return 0.5 * value * (1.0 + jnp.tanh(inner))


def gelu_slope(value):
    inner = gelu_coef * (value + cubic_coef * value * value * value)
    tangent = jnp.tanh(inner)
    return 0.5 * (1.0 + tangent) + 0.5 * value * (1.0 - tangent * tangent) * gelu_coef * (
        1.0 + 3.0 * cubic_coef * value * value
    )


def inverse_rms(value):
    return lax.rsqrt(jnp.mean(value * value, axis=-1, keepdims=True) + eps_norm)


def near_counts(near_tile, ext_count):
    rows = lax.broadcasted_iota(jnp.int32, (ext_count, near_tile.shape[1]), 0)
    total = jnp.zeros((ext_count, near_tile.shape[1]), jnp.float32)
    for index in range(near_tile.shape[0]):
        total = total + (near_tile[index][None, :] == rows).astype(jnp.float32)
    return total.astype(jnp.bfloat16)


def tile_forward(points_tile, halo_rows, counts_t, w_near, count_near):
    extended = jnp.concatenate([points_tile, halo_rows], axis=0)
    total = lax.dot_general(
        counts_t, extended, (((0,), (0,)), ((), ())), preferred_element_type=jnp.float32
    )
    average = (total * (1.0 / count_near)).astype(jnp.bfloat16)
    linear_part = jnp.dot(average, w_near, preferred_element_type=jnp.float32)
    lifted = (points_tile.astype(jnp.float32) + gelu_tanh(linear_part)).astype(jnp.bfloat16)
    return (average, linear_part, lifted)


def tile_backward(lifted_grad, average, linear_part, counts_t, w_near, count_near):
    tile_rows = lifted_grad.shape[0]
    act_grad = (lifted_grad.astype(jnp.float32) * gelu_slope(linear_part)).astype(jnp.bfloat16)
    near_grad = lax.dot_general(
        average, act_grad, (((0,), (0,)), ((), ())), preferred_element_type=jnp.float32
    )
    spread = lax.dot_general(
        act_grad, w_near, (((1,), (1,)), ((), ())), preferred_element_type=jnp.float32
    ) * (1.0 / count_near)
    spread_hi = spread.astype(jnp.bfloat16)
    spread_lo = (spread - spread_hi.astype(jnp.float32)).astype(jnp.bfloat16)
    ext_grad = jnp.dot(counts_t, spread_hi, preferred_element_type=jnp.float32) + jnp.dot(
        counts_t, spread_lo, preferred_element_type=jnp.float32
    )
    row_grad = lifted_grad.astype(jnp.float32) + ext_grad[:tile_rows]
    halo_grad = ext_grad[tile_rows:].astype(jnp.bfloat16)
    return (near_grad, row_grad, halo_grad)


def route_ranks(owner_tile, count, tiles):
    tile_rows = owner_tile.shape[0]
    index = jnp.arange(tile_rows, dtype=jnp.int32)
    live = index < count
    score = jnp.where(live, owner_tile * tile_rows + index, tiles * tile_rows + index)
    order = jnp.argsort(score, stable=True)
    members = (owner_tile[:, None] == jnp.arange(tiles, dtype=jnp.int32)[None, :]) & live[:, None]
    per_owner = jnp.sum(members.astype(jnp.int32), axis=0)
    starts = jnp.cumsum(per_owner) - per_owner
    sorted_owner = jnp.take(owner_tile, order)
    ranked = index - jnp.take(starts, sorted_owner)
    rank = jnp.zeros((tile_rows,), jnp.int32).at[order].set(ranked)
    return (rank, live)


def shift_down(rows):
    patches = rows.reshape(-1, PATCH, rows.shape[-1])
    moved = jnp.concatenate([jnp.zeros_like(patches[:, :1]), patches[:, :-1]], axis=1)
    return moved.reshape(rows.shape)


def shift_up(rows):
    patches = rows.reshape(-1, PATCH, rows.shape[-1])
    moved = jnp.concatenate([patches[:, 1:], jnp.zeros_like(patches[:, :1])], axis=1)
    return moved.reshape(rows.shape)


def block_taps(conv_w):
    groups, inner = (conv_w.shape[1], conv_w.shape[2])
    identity_blocks = jnp.eye(groups, dtype=conv_w.dtype)
    full = jnp.einsum("gh,ogab->ogahb", identity_blocks, conv_w)
    return full.reshape(conv_w.shape[0], groups * inner, groups * inner)


def grouped_weight(inputs, outputs, groups, inner):
    length = inputs.shape[0]
    left = inputs.reshape(length, groups, inner)
    right = outputs.reshape(length, groups, inner)
    return jnp.einsum("pga,pgb->gab", left, right, preferred_element_type=jnp.float32)


def tap_back(rows, tap):
    return lax.dot_general(rows, tap, (((1,), (1,)), ((), ())), preferred_element_type=jnp.float32)


def patch_pass(serial, out_grad, gain_one, conv_w, taps_full, gain_two, w_up, w_down):
    groups, inner = (conv_w.shape[1], conv_w.shape[2])
    serial_f = serial.astype(jnp.float32)
    scale_one = inverse_rms(serial_f)
    normed = (serial_f * scale_one * gain_one).astype(jnp.bfloat16)
    taps = (shift_down(normed), normed, shift_up(normed))
    mixed = (
        jnp.dot(taps[0], taps_full[0], preferred_element_type=jnp.float32)
        + jnp.dot(taps[1], taps_full[1], preferred_element_type=jnp.float32)
        + jnp.dot(taps[2], taps_full[2], preferred_element_type=jnp.float32)
    )
    state = serial_f + mixed
    scale_two = inverse_rms(state)
    second = (state * scale_two * gain_two).astype(jnp.bfloat16)
    hidden_pre = jnp.dot(second, w_up, preferred_element_type=jnp.float32)
    hidden = gelu_tanh(hidden_pre).astype(jnp.bfloat16)
    result = (state + jnp.dot(hidden, w_down, preferred_element_type=jnp.float32)).astype(
        jnp.bfloat16
    )
    down_grad = lax.dot_general(
        hidden, out_grad, (((0,), (0,)), ((), ())), preferred_element_type=jnp.float32
    )
    hidden_grad = lax.dot_general(
        out_grad, w_down, (((1,), (1,)), ((), ())), preferred_element_type=jnp.float32
    ).astype(jnp.bfloat16)
    pre_grad = (hidden_grad.astype(jnp.float32) * gelu_slope(hidden_pre)).astype(jnp.bfloat16)
    up_grad = lax.dot_general(
        second, pre_grad, (((0,), (0,)), ((), ())), preferred_element_type=jnp.float32
    )
    second_grad = lax.dot_general(
        pre_grad, w_up, (((1,), (1,)), ((), ())), preferred_element_type=jnp.float32
    ).astype(jnp.bfloat16)
    unit_two = state * scale_two
    weighted_two = second_grad.astype(jnp.float32) * gain_two
    gain_two_grad = jnp.sum(second_grad.astype(jnp.float32) * unit_two, axis=0)
    state_grad = out_grad.astype(jnp.float32) + scale_two * (
        weighted_two - unit_two * jnp.mean(weighted_two * unit_two, axis=-1, keepdims=True)
    )
    mixed_grad = state_grad.astype(jnp.bfloat16)
    conv_grad = jnp.stack(
        [
            grouped_weight(taps[0], mixed_grad, groups, inner),
            grouped_weight(taps[1], mixed_grad, groups, inner),
            grouped_weight(taps[2], mixed_grad, groups, inner),
        ],
        axis=0,
    )
    normed_grad = (
        shift_up(tap_back(mixed_grad, taps_full[0]))
        + tap_back(mixed_grad, taps_full[1])
        + shift_down(tap_back(mixed_grad, taps_full[2]))
    ).astype(jnp.bfloat16)
    unit_one = serial_f * scale_one
    weighted_one = normed_grad.astype(jnp.float32) * gain_one
    gain_one_grad = jnp.sum(normed_grad.astype(jnp.float32) * unit_one, axis=0)
    serial_grad = (
        state_grad
        + scale_one
        * (weighted_one - unit_one * jnp.mean(weighted_one * unit_one, axis=-1, keepdims=True))
    ).astype(jnp.bfloat16)
    return (result, serial_grad, (gain_one_grad, conv_grad, gain_two_grad, up_grad, down_grad))


def all_sum(flat, axes):
    devices = lax.axis_size(axes)
    chunk = -(-flat.shape[0] // (devices * 128)) * 128
    padded = jnp.pad(flat, (0, devices * chunk - flat.shape[0])).reshape(devices, chunk)
    pieces = lax.all_to_all(padded, axes, split_axis=0, concat_axis=0, tiled=True)
    part = jnp.sum(pieces, axis=0)
    spread = jnp.broadcast_to(part[None], (devices, chunk))
    whole = lax.all_to_all(spread, axes, split_axis=0, concat_axis=0, tiled=True)
    return whole.reshape(-1)[: flat.shape[0]]


def pass_columns(rows, shift_by):
    return shifted(rows, "tx", shift_by)


def pass_lines(rows, shift_by):
    return shifted(rows, "ty", shift_by)


def body(
    points,
    counts,
    owner,
    zorder,
    border,
    near,
    w_near,
    gain_one,
    conv_w,
    gain_two,
    w_up,
    w_down,
    grad_out,
):
    points_tile = points[0]
    tile_rows, width = points_tile.shape
    lists = border[0]
    border_rows = lists.shape[1]
    cols_count = lax.axis_size("tx")
    lines_count = lax.axis_size("ty")
    tiles = cols_count * lines_count
    recv_rows = zorder.shape[1]
    capacity = recv_rows // tiles
    near_tile = near[0]
    owner_tile = owner[0]
    sent = jnp.take(points_tile, lists.reshape(-1), axis=0).reshape(4, border_rows, width)
    halo = jnp.concatenate(
        [
            pass_columns(sent[0], -1),
            pass_columns(sent[1], 1),
            pass_lines(sent[2], -1),
            pass_lines(sent[3], 1),
        ],
        axis=0,
    )
    count_near = near_tile.shape[0]
    counts_t = near_counts(near_tile, tile_rows + 4 * border_rows)
    average, linear_part, lifted = tile_forward(points_tile, halo, counts_t, w_near, count_near)
    rank, live = route_ranks(owner_tile, counts[0], tiles)
    slots = jnp.where(live, owner_tile * capacity + rank, tiles * capacity)
    payload = jnp.concatenate([lifted, grad_out[0]], axis=1)
    outgoing = (
        jnp.zeros((tiles * capacity, 2 * width), jnp.bfloat16).at[slots].set(payload, mode="drop")
    )
    incoming = lax.all_to_all(outgoing, ("tx", "ty"), split_axis=0, concat_axis=0, tiled=True)
    serial_both = jnp.take(incoming, zorder[0], axis=0)
    taps_full = block_taps(conv_w)

    results, serial_grads, sums = patch_pass(
        serial_both[:, :width], serial_both[:, width:], gain_one, conv_w, taps_full, gain_two, w_up, w_down
    )
    back = jnp.concatenate(
        [results.reshape(recv_rows, width), serial_grads.reshape(recv_rows, width)], axis=1
    )
    back_slots = jnp.zeros_like(back).at[zorder[0]].set(back)
    returned = lax.all_to_all(back_slots, ("tx", "ty"), split_axis=0, concat_axis=0, tiled=True)
    back_rows = jnp.take(returned, slots, axis=0, mode="fill", fill_value=0)
    out_rows = back_rows[:, :width]
    lifted_grad = back_rows[:, width:]
    patch_flat = jnp.concatenate(
        [sums[0], sums[2], sums[1].reshape(-1), sums[3].reshape(-1), sums[4].reshape(-1)]
    )
    near_grad, row_grad, halo_grad = tile_backward(
        lifted_grad, average, linear_part, counts_t, w_near, count_near
    )
    came_back = (
        pass_columns(halo_grad[0:border_rows], 1),
        pass_columns(halo_grad[border_rows : 2 * border_rows], -1),
        pass_lines(halo_grad[2 * border_rows : 3 * border_rows], 1),
        pass_lines(halo_grad[3 * border_rows : 4 * border_rows], -1),
    )
    for direction in range(4):
        row_grad = row_grad.at[lists[direction]].add(came_back[direction].astype(jnp.float32))
    grads_total = all_sum(jnp.concatenate([near_grad.reshape(-1), patch_flat]), ("tx", "ty"))
    near_sum = grads_total[: near_grad.size].reshape(near_grad.shape)
    patch_total = grads_total[near_grad.size :]
    sizes = [width, width, conv_w.size, w_up.size, w_down.size]
    shapes = [(width,), (width,), conv_w.shape, w_up.shape, w_down.shape]
    offsets = [sum(sizes[:index]) for index in range(len(sizes))]
    gain_one_sum, gain_two_sum, conv_sum, up_sum, down_sum = [
        patch_total[start : start + size].reshape(shape)
        for start, size, shape in zip(offsets, sizes, shapes)
    ]
    totals = (gain_one_sum, conv_sum, gain_two_sum, up_sum, down_sum)
    scale = 1.0 / math.sqrt(tiles * tile_rows)
    return (
        out_rows[None],
        row_grad.astype(jnp.bfloat16)[None],
        near_sum * scale,
        totals[0] * scale,
        totals[1] * scale,
        totals[2] * scale,
        totals[3] * scale,
        totals[4] * scale,
    )


def solution(mesh):
    placed = (
        P(("tx", "ty"), None, None),
        P(("tx", "ty")),
        P(("tx", "ty"), None),
        P(("tx", "ty"), None),
        P(("tx", "ty"), None, None),
        P(("tx", "ty"), None, None),
        P(),
        P(),
        P(),
        P(),
        P(),
        P(),
        P(("tx", "ty"), None, None),
    )
    return jax.shard_map(
        body,
        mesh=mesh,
        in_specs=placed,
        out_specs=(
            P(("tx", "ty"), None, None),
            P(("tx", "ty"), None, None),
            P(),
            P(),
            P(),
            P(),
            P(),
            P(),
        ),
        check_vma=False,
    )
```

```python
import math

import jax
import jax.numpy as jnp
from jax import lax
from jax.experimental import pallas as pl
from jax.experimental.pallas import tpu as pltpu
from jax.sharding import PartitionSpec as P

PATCH = 1024


eps_norm = 1e-06
gelu_coef = 0.7978845608028654
cubic_coef = 0.044715


def shifted(value, axis, steps):
    count = lax.axis_size(axis)
    initial, last = (max(0, -steps), min(count, count - steps))
    return lax.ppermute(value, axis, [(source, source + steps) for source in range(initial, last)])


def gelu_tanh(value):
    inner = gelu_coef * (value + cubic_coef * value * value * value)
    return 0.5 * value * (1.0 + jnp.tanh(inner))


def gelu_slope(value):
    inner = gelu_coef * (value + cubic_coef * value * value * value)
    tangent = jnp.tanh(inner)
    return 0.5 * (1.0 + tangent) + 0.5 * value * (1.0 - tangent * tangent) * gelu_coef * (
        1.0 + 3.0 * cubic_coef * value * value
    )


def inverse_rms(value):
    return lax.rsqrt(jnp.mean(value * value, axis=-1, keepdims=True) + eps_norm)


def near_counts(near_tile, ext_count):
    rows = lax.broadcasted_iota(jnp.int32, (ext_count, near_tile.shape[1]), 0)
    total = jnp.zeros((ext_count, near_tile.shape[1]), jnp.float32)
    for index in range(near_tile.shape[0]):
        total = total + (near_tile[index][None, :] == rows).astype(jnp.float32)
    return total.astype(jnp.bfloat16)


def tile_forward(points_tile, halo_rows, counts_t, w_near, count_near):
    extended = jnp.concatenate([points_tile, halo_rows], axis=0)
    total = lax.dot_general(
        counts_t, extended, (((0,), (0,)), ((), ())), preferred_element_type=jnp.float32
    )
    average = (total * (1.0 / count_near)).astype(jnp.bfloat16)
    linear_part = jnp.dot(average, w_near, preferred_element_type=jnp.float32)
    lifted = (points_tile.astype(jnp.float32) + gelu_tanh(linear_part)).astype(jnp.bfloat16)
    return (average, linear_part, lifted)


def tile_backward(lifted_grad, average, linear_part, counts_t, w_near, count_near):
    tile_rows = lifted_grad.shape[0]
    act_grad = (lifted_grad.astype(jnp.float32) * gelu_slope(linear_part)).astype(jnp.bfloat16)
    near_grad = lax.dot_general(
        average, act_grad, (((0,), (0,)), ((), ())), preferred_element_type=jnp.float32
    )
    spread = lax.dot_general(
        act_grad, w_near, (((1,), (1,)), ((), ())), preferred_element_type=jnp.float32
    ) * (1.0 / count_near)
    spread_hi = spread.astype(jnp.bfloat16)
    spread_lo = (spread - spread_hi.astype(jnp.float32)).astype(jnp.bfloat16)
    ext_grad = jnp.dot(counts_t, spread_hi, preferred_element_type=jnp.float32) + jnp.dot(
        counts_t, spread_lo, preferred_element_type=jnp.float32
    )
    row_grad = lifted_grad.astype(jnp.float32) + ext_grad[:tile_rows]
    halo_grad = ext_grad[tile_rows:].astype(jnp.bfloat16)
    return (near_grad, row_grad, halo_grad)


def route_ranks(owner_tile, count, tiles):
    tile_rows = owner_tile.shape[0]
    index = jnp.arange(tile_rows, dtype=jnp.int32)
    live = index < count
    score = jnp.where(live, owner_tile * tile_rows + index, tiles * tile_rows + index)
    order = jnp.argsort(score, stable=True)
    members = (owner_tile[:, None] == jnp.arange(tiles, dtype=jnp.int32)[None, :]) & live[:, None]
    per_owner = jnp.sum(members.astype(jnp.int32), axis=0)
    starts = jnp.cumsum(per_owner) - per_owner
    sorted_owner = jnp.take(owner_tile, order)
    ranked = index - jnp.take(starts, sorted_owner)
    rank = jnp.zeros((tile_rows,), jnp.int32).at[order].set(ranked)
    return (rank, live)


def shift_down(rows):
    patches = rows.reshape(-1, PATCH, rows.shape[-1])
    moved = jnp.concatenate([jnp.zeros_like(patches[:, :1]), patches[:, :-1]], axis=1)
    return moved.reshape(rows.shape)


def shift_up(rows):
    patches = rows.reshape(-1, PATCH, rows.shape[-1])
    moved = jnp.concatenate([patches[:, 1:], jnp.zeros_like(patches[:, :1])], axis=1)
    return moved.reshape(rows.shape)


def block_taps(conv_w):
    groups, inner = (conv_w.shape[1], conv_w.shape[2])
    identity_blocks = jnp.eye(groups, dtype=conv_w.dtype)
    full = jnp.einsum("gh,ogab->ogahb", identity_blocks, conv_w)
    return full.reshape(conv_w.shape[0], groups * inner, groups * inner)


def grouped_weight(inputs, outputs, groups, inner):
    length = inputs.shape[0]
    left = inputs.reshape(length, groups, inner)
    right = outputs.reshape(length, groups, inner)
    return jnp.einsum("pga,pgb->gab", left, right, preferred_element_type=jnp.float32)


def tap_back(rows, tap):
    return lax.dot_general(rows, tap, (((1,), (1,)), ((), ())), preferred_element_type=jnp.float32)


def mlp_kernel(
    second_ref, grad_ref, state_ref, up_ref, down_ref, result_ref, sgrad_ref, upg_ref, downg_ref
):
    @pl.when(pl.program_id(0) == 0)
    def _():
        upg_ref[...] = jnp.zeros_like(upg_ref)
        downg_ref[...] = jnp.zeros_like(downg_ref)

    second = second_ref[...]
    out_grad = grad_ref[...]
    hidden_pre = jnp.dot(second, up_ref[...], preferred_element_type=jnp.float32)
    inner = gelu_coef * (hidden_pre + cubic_coef * hidden_pre * hidden_pre * hidden_pre)
    tangent = jnp.tanh(inner)
    hidden = (0.5 * hidden_pre * (1.0 + tangent)).astype(jnp.bfloat16)
    result_ref[...] = (
        state_ref[...] + jnp.dot(hidden, down_ref[...], preferred_element_type=jnp.float32)
    ).astype(jnp.bfloat16)
    downg_ref[...] += lax.dot_general(
        hidden, out_grad, (((0,), (0,)), ((), ())), preferred_element_type=jnp.float32
    )
    hidden_grad = lax.dot_general(
        out_grad, down_ref[...], (((1,), (1,)), ((), ())), preferred_element_type=jnp.float32
    ).astype(jnp.bfloat16)
    slope = 0.5 * (1.0 + tangent) + 0.5 * hidden_pre * (1.0 - tangent * tangent) * gelu_coef * (
        1.0 + 3.0 * cubic_coef * hidden_pre * hidden_pre
    )
    pre_grad = (hidden_grad.astype(jnp.float32) * slope).astype(jnp.bfloat16)
    upg_ref[...] += lax.dot_general(
        second, pre_grad, (((0,), (0,)), ((), ())), preferred_element_type=jnp.float32
    )
    sgrad_ref[...] = lax.dot_general(
        pre_grad, up_ref[...], (((1,), (1,)), ((), ())), preferred_element_type=jnp.float32
    ).astype(jnp.bfloat16)


def mlp_pass(second, out_grad, state, w_up, w_down, block_rows=256):
    rows, width = second.shape
    ffn = w_up.shape[1]
    row_block = pl.BlockSpec((block_rows, width), lambda step: (step, 0))
    whole = lambda shape: pl.BlockSpec(shape, lambda step: (0, 0))
    flops = 2 * rows * width * ffn * 6
    return pl.pallas_call(
        mlp_kernel,
        grid=(rows // block_rows,),
        in_specs=[row_block, row_block, row_block, whole((width, ffn)), whole((ffn, width))],
        out_specs=[row_block, row_block, whole((width, ffn)), whole((ffn, width))],
        out_shape=[
            jax.ShapeDtypeStruct((rows, width), jnp.bfloat16),
            jax.ShapeDtypeStruct((rows, width), jnp.bfloat16),
            jax.ShapeDtypeStruct((width, ffn), jnp.float32),
            jax.ShapeDtypeStruct((ffn, width), jnp.float32),
        ],
        compiler_params=pltpu.CompilerParams(dimension_semantics=("arbitrary",)),
        cost_estimate=pl.CostEstimate(
            flops=flops, transcendentals=rows * ffn, bytes_accessed=rows * width * 10 + 4 * width * ffn * 3
        ),
    )(second, out_grad, state, w_up, w_down)


def patch_pass(serial, out_grad, gain_one, conv_w, taps_full, gain_two, w_up, w_down):
    groups, inner = (conv_w.shape[1], conv_w.shape[2])
    serial_f = serial.astype(jnp.float32)
    scale_one = inverse_rms(serial_f)
    normed = (serial_f * scale_one * gain_one).astype(jnp.bfloat16)
    taps = (shift_down(normed), normed, shift_up(normed))
    mixed = (
        jnp.dot(taps[0], taps_full[0], preferred_element_type=jnp.float32)
        + jnp.dot(taps[1], taps_full[1], preferred_element_type=jnp.float32)
        + jnp.dot(taps[2], taps_full[2], preferred_element_type=jnp.float32)
    )
    state = serial_f + mixed
    scale_two = inverse_rms(state)
    second = (state * scale_two * gain_two).astype(jnp.bfloat16)
    result, second_grad, up_grad, down_grad = mlp_pass(second, out_grad, state, w_up, w_down)
    unit_two = state * scale_two
    weighted_two = second_grad.astype(jnp.float32) * gain_two
    gain_two_grad = jnp.sum(second_grad.astype(jnp.float32) * unit_two, axis=0)
    state_grad = out_grad.astype(jnp.float32) + scale_two * (
        weighted_two - unit_two * jnp.mean(weighted_two * unit_two, axis=-1, keepdims=True)
    )
    mixed_grad = state_grad.astype(jnp.bfloat16)
    conv_grad = jnp.stack(
        [
            grouped_weight(taps[0], mixed_grad, groups, inner),
            grouped_weight(taps[1], mixed_grad, groups, inner),
            grouped_weight(taps[2], mixed_grad, groups, inner),
        ],
        axis=0,
    )
    normed_grad = (
        shift_up(tap_back(mixed_grad, taps_full[0]))
        + tap_back(mixed_grad, taps_full[1])
        + shift_down(tap_back(mixed_grad, taps_full[2]))
    ).astype(jnp.bfloat16)
    unit_one = serial_f * scale_one
    weighted_one = normed_grad.astype(jnp.float32) * gain_one
    gain_one_grad = jnp.sum(normed_grad.astype(jnp.float32) * unit_one, axis=0)
    serial_grad = (
        state_grad
        + scale_one
        * (weighted_one - unit_one * jnp.mean(weighted_one * unit_one, axis=-1, keepdims=True))
    ).astype(jnp.bfloat16)
    return (result, serial_grad, (gain_one_grad, conv_grad, gain_two_grad, up_grad, down_grad))


def all_sum(flat, axes):
    devices = lax.axis_size(axes)
    chunk = -(-flat.shape[0] // (devices * 128)) * 128
    padded = jnp.pad(flat, (0, devices * chunk - flat.shape[0])).reshape(devices, chunk)
    pieces = lax.all_to_all(padded, axes, split_axis=0, concat_axis=0, tiled=True)
    part = jnp.sum(pieces, axis=0)
    spread = jnp.broadcast_to(part[None], (devices, chunk))
    whole = lax.all_to_all(spread, axes, split_axis=0, concat_axis=0, tiled=True)
    return whole.reshape(-1)[: flat.shape[0]]


def pass_columns(rows, shift_by):
    return shifted(rows, "tx", shift_by)


def pass_lines(rows, shift_by):
    return shifted(rows, "ty", shift_by)


def body(
    points,
    counts,
    owner,
    zorder,
    border,
    near,
    w_near,
    gain_one,
    conv_w,
    gain_two,
    w_up,
    w_down,
    grad_out,
):
    points_tile = points[0]
    tile_rows, width = points_tile.shape
    lists = border[0]
    border_rows = lists.shape[1]
    cols_count = lax.axis_size("tx")
    lines_count = lax.axis_size("ty")
    tiles = cols_count * lines_count
    recv_rows = zorder.shape[1]
    capacity = recv_rows // tiles
    near_tile = near[0]
    owner_tile = owner[0]
    sent = jnp.take(points_tile, lists.reshape(-1), axis=0).reshape(4, border_rows, width)
    halo = jnp.concatenate(
        [
            pass_columns(sent[0], -1),
            pass_columns(sent[1], 1),
            pass_lines(sent[2], -1),
            pass_lines(sent[3], 1),
        ],
        axis=0,
    )
    count_near = near_tile.shape[0]
    counts_t = near_counts(near_tile, tile_rows + 4 * border_rows)
    average, linear_part, lifted = tile_forward(points_tile, halo, counts_t, w_near, count_near)
    rank, live = route_ranks(owner_tile, counts[0], tiles)
    slots = jnp.where(live, owner_tile * capacity + rank, tiles * capacity)
    payload = jnp.concatenate([lifted, grad_out[0]], axis=1)
    outgoing = (
        jnp.zeros((tiles * capacity, 2 * width), jnp.bfloat16).at[slots].set(payload, mode="drop")
    )
    incoming = lax.all_to_all(outgoing, ("tx", "ty"), split_axis=0, concat_axis=0, tiled=True)
    serial_both = jnp.take(incoming, zorder[0], axis=0)
    taps_full = block_taps(conv_w)

    results, serial_grads, sums = patch_pass(
        serial_both[:, :width], serial_both[:, width:], gain_one, conv_w, taps_full, gain_two, w_up, w_down
    )
    back = jnp.concatenate(
        [results.reshape(recv_rows, width), serial_grads.reshape(recv_rows, width)], axis=1
    )
    back_slots = jnp.zeros_like(back).at[zorder[0]].set(back)
    returned = lax.all_to_all(back_slots, ("tx", "ty"), split_axis=0, concat_axis=0, tiled=True)
    back_rows = jnp.take(returned, slots, axis=0, mode="fill", fill_value=0)
    out_rows = back_rows[:, :width]
    lifted_grad = back_rows[:, width:]
    patch_flat = jnp.concatenate(
        [sums[0], sums[2], sums[1].reshape(-1), sums[3].reshape(-1), sums[4].reshape(-1)]
    )
    near_grad, row_grad, halo_grad = tile_backward(
        lifted_grad, average, linear_part, counts_t, w_near, count_near
    )
    came_back = (
        pass_columns(halo_grad[0:border_rows], 1),
        pass_columns(halo_grad[border_rows : 2 * border_rows], -1),
        pass_lines(halo_grad[2 * border_rows : 3 * border_rows], 1),
        pass_lines(halo_grad[3 * border_rows : 4 * border_rows], -1),
    )
    for direction in range(4):
        row_grad = row_grad.at[lists[direction]].add(came_back[direction].astype(jnp.float32))
    grads_total = all_sum(jnp.concatenate([near_grad.reshape(-1), patch_flat]), ("tx", "ty"))
    near_sum = grads_total[: near_grad.size].reshape(near_grad.shape)
    patch_total = grads_total[near_grad.size :]
    sizes = [width, width, conv_w.size, w_up.size, w_down.size]
    shapes = [(width,), (width,), conv_w.shape, w_up.shape, w_down.shape]
    offsets = [sum(sizes[:index]) for index in range(len(sizes))]
    gain_one_sum, gain_two_sum, conv_sum, up_sum, down_sum = [
        patch_total[start : start + size].reshape(shape)
        for start, size, shape in zip(offsets, sizes, shapes)
    ]
    totals = (gain_one_sum, conv_sum, gain_two_sum, up_sum, down_sum)
    scale = 1.0 / math.sqrt(tiles * tile_rows)
    return (
        out_rows[None],
        row_grad.astype(jnp.bfloat16)[None],
        near_sum * scale,
        totals[0] * scale,
        totals[1] * scale,
        totals[2] * scale,
        totals[3] * scale,
        totals[4] * scale,
    )


def solution(mesh):
    placed = (
        P(("tx", "ty"), None, None),
        P(("tx", "ty")),
        P(("tx", "ty"), None),
        P(("tx", "ty"), None),
        P(("tx", "ty"), None, None),
        P(("tx", "ty"), None, None),
        P(),
        P(),
        P(),
        P(),
        P(),
        P(),
        P(("tx", "ty"), None, None),
    )
    return jax.shard_map(
        body,
        mesh=mesh,
        in_specs=placed,
        out_specs=(
            P(("tx", "ty"), None, None),
            P(("tx", "ty"), None, None),
            P(),
            P(),
            P(),
            P(),
            P(),
            P(),
        ),
        check_vma=False,
    )
```

```python
import math

import jax
import jax.numpy as jnp
from jax import lax
from jax.experimental import pallas as pl
from jax.experimental.pallas import tpu as pltpu
from jax.sharding import Mesh, PartitionSpec as P

PATCH = 1024
LINES = ("tyc", "core")
ALL = ("tx",) + LINES


eps_norm = 1e-06
gelu_coef = 0.7978845608028654
cubic_coef = 0.044715


def shifted(value, axis, steps):
    count = lax.axis_size(axis)
    initial, last = (max(0, -steps), min(count, count - steps))
    return lax.ppermute(value, axis, [(source, source + steps) for source in range(initial, last)])


def gelu_tanh(value):
    inner = gelu_coef * (value + cubic_coef * value * value * value)
    return 0.5 * value * (1.0 + jnp.tanh(inner))


def gelu_slope(value):
    inner = gelu_coef * (value + cubic_coef * value * value * value)
    tangent = jnp.tanh(inner)
    return 0.5 * (1.0 + tangent) + 0.5 * value * (1.0 - tangent * tangent) * gelu_coef * (
        1.0 + 3.0 * cubic_coef * value * value
    )


def inverse_rms(value):
    return lax.rsqrt(jnp.mean(value * value, axis=-1, keepdims=True) + eps_norm)


def near_counts(near_tile, ext_count):
    rows = lax.broadcasted_iota(jnp.int32, (ext_count, near_tile.shape[1]), 0)
    total = jnp.zeros((ext_count, near_tile.shape[1]), jnp.float32)
    for index in range(near_tile.shape[0]):
        total = total + (near_tile[index][None, :] == rows).astype(jnp.float32)
    return total.astype(jnp.bfloat16)


def tile_forward(points_tile, halo_rows, counts_t, w_near, count_near):
    extended = jnp.concatenate([points_tile, halo_rows], axis=0)
    total = lax.dot_general(
        counts_t, extended, (((0,), (0,)), ((), ())), preferred_element_type=jnp.float32
    )
    average = (total * (1.0 / count_near)).astype(jnp.bfloat16)
    linear_part = jnp.dot(average, w_near, preferred_element_type=jnp.float32)
    lifted = (points_tile.astype(jnp.float32) + gelu_tanh(linear_part)).astype(jnp.bfloat16)
    return (average, linear_part, lifted)


def tile_backward(lifted_grad, average, linear_part, counts_t, w_near, count_near):
    tile_rows = lifted_grad.shape[0]
    act_grad = (lifted_grad.astype(jnp.float32) * gelu_slope(linear_part)).astype(jnp.bfloat16)
    near_grad = lax.dot_general(
        average, act_grad, (((0,), (0,)), ((), ())), preferred_element_type=jnp.float32
    )
    spread = lax.dot_general(
        act_grad, w_near, (((1,), (1,)), ((), ())), preferred_element_type=jnp.float32
    ) * (1.0 / count_near)
    spread_hi = spread.astype(jnp.bfloat16)
    spread_lo = (spread - spread_hi.astype(jnp.float32)).astype(jnp.bfloat16)
    ext_grad = jnp.dot(counts_t, spread_hi, preferred_element_type=jnp.float32) + jnp.dot(
        counts_t, spread_lo, preferred_element_type=jnp.float32
    )
    row_grad = lifted_grad.astype(jnp.float32) + ext_grad[:tile_rows]
    halo_grad = ext_grad[tile_rows:].astype(jnp.bfloat16)
    return (near_grad, row_grad, halo_grad)


def route_ranks(owner_tile, count, tiles):
    tile_rows = owner_tile.shape[0]
    index = jnp.arange(tile_rows, dtype=jnp.int32)
    live = index < count
    score = jnp.where(live, owner_tile * tile_rows + index, tiles * tile_rows + index)
    order = jnp.argsort(score, stable=True)
    members = (owner_tile[:, None] == jnp.arange(tiles, dtype=jnp.int32)[None, :]) & live[:, None]
    per_owner = jnp.sum(members.astype(jnp.int32), axis=0)
    starts = jnp.cumsum(per_owner) - per_owner
    sorted_owner = jnp.take(owner_tile, order)
    ranked = index - jnp.take(starts, sorted_owner)
    rank = jnp.zeros((tile_rows,), jnp.int32).at[order].set(ranked)
    return (rank, live)


def shift_down(rows):
    patches = rows.reshape(-1, PATCH, rows.shape[-1])
    moved = jnp.concatenate([jnp.zeros_like(patches[:, :1]), patches[:, :-1]], axis=1)
    return moved.reshape(rows.shape)


def shift_up(rows):
    patches = rows.reshape(-1, PATCH, rows.shape[-1])
    moved = jnp.concatenate([patches[:, 1:], jnp.zeros_like(patches[:, :1])], axis=1)
    return moved.reshape(rows.shape)


def block_taps(conv_w):
    groups, inner = (conv_w.shape[1], conv_w.shape[2])
    identity_blocks = jnp.eye(groups, dtype=conv_w.dtype)
    full = jnp.einsum("gh,ogab->ogahb", identity_blocks, conv_w)
    return full.reshape(conv_w.shape[0], groups * inner, groups * inner)


def grouped_weight(inputs, outputs, groups, inner):
    length = inputs.shape[0]
    left = inputs.reshape(length, groups, inner)
    right = outputs.reshape(length, groups, inner)
    return jnp.einsum("pga,pgb->gab", left, right, preferred_element_type=jnp.float32)


def tap_back(rows, tap):
    return lax.dot_general(rows, tap, (((1,), (1,)), ((), ())), preferred_element_type=jnp.float32)


def mlp_kernel(
    second_ref, grad_ref, state_ref, up_ref, down_ref, result_ref, sgrad_ref, upg_ref, downg_ref
):
    @pl.when(pl.program_id(0) == 0)
    def _():
        upg_ref[...] = jnp.zeros_like(upg_ref)
        downg_ref[...] = jnp.zeros_like(downg_ref)

    second = second_ref[...]
    out_grad = grad_ref[...]
    hidden_pre = jnp.dot(second, up_ref[...], preferred_element_type=jnp.float32)
    inner = gelu_coef * (hidden_pre + cubic_coef * hidden_pre * hidden_pre * hidden_pre)
    tangent = jnp.tanh(inner)
    hidden = (0.5 * hidden_pre * (1.0 + tangent)).astype(jnp.bfloat16)
    result_ref[...] = (
        state_ref[...] + jnp.dot(hidden, down_ref[...], preferred_element_type=jnp.float32)
    ).astype(jnp.bfloat16)
    downg_ref[...] += lax.dot_general(
        hidden, out_grad, (((0,), (0,)), ((), ())), preferred_element_type=jnp.float32
    )
    hidden_grad = lax.dot_general(
        out_grad, down_ref[...], (((1,), (1,)), ((), ())), preferred_element_type=jnp.float32
    ).astype(jnp.bfloat16)
    slope = 0.5 * (1.0 + tangent) + 0.5 * hidden_pre * (1.0 - tangent * tangent) * gelu_coef * (
        1.0 + 3.0 * cubic_coef * hidden_pre * hidden_pre
    )
    pre_grad = (hidden_grad.astype(jnp.float32) * slope).astype(jnp.bfloat16)
    upg_ref[...] += lax.dot_general(
        second, pre_grad, (((0,), (0,)), ((), ())), preferred_element_type=jnp.float32
    )
    sgrad_ref[...] = lax.dot_general(
        pre_grad, up_ref[...], (((1,), (1,)), ((), ())), preferred_element_type=jnp.float32
    ).astype(jnp.bfloat16)


def mlp_pass(second, out_grad, state, w_up, w_down, block_rows=256):
    rows, width = second.shape
    ffn = w_up.shape[1]
    row_block = pl.BlockSpec((block_rows, width), lambda step: (step, 0))
    whole = lambda shape: pl.BlockSpec(shape, lambda step: (0, 0))
    flops = 2 * rows * width * ffn * 6
    return pl.pallas_call(
        mlp_kernel,
        grid=(rows // block_rows,),
        in_specs=[row_block, row_block, row_block, whole((width, ffn)), whole((ffn, width))],
        out_specs=[row_block, row_block, whole((width, ffn)), whole((ffn, width))],
        out_shape=[
            jax.ShapeDtypeStruct((rows, width), jnp.bfloat16),
            jax.ShapeDtypeStruct((rows, width), jnp.bfloat16),
            jax.ShapeDtypeStruct((width, ffn), jnp.float32),
            jax.ShapeDtypeStruct((ffn, width), jnp.float32),
        ],
        compiler_params=pltpu.CompilerParams(dimension_semantics=("arbitrary",)),
        cost_estimate=pl.CostEstimate(
            flops=flops, transcendentals=rows * ffn, bytes_accessed=rows * width * 10 + 4 * width * ffn * 3
        ),
    )(second, out_grad, state, w_up, w_down)


def patch_pass(serial, out_grad, gain_one, conv_w, taps_full, gain_two, w_up, w_down):
    groups, inner = (conv_w.shape[1], conv_w.shape[2])
    serial_f = serial.astype(jnp.float32)
    scale_one = inverse_rms(serial_f)
    normed = (serial_f * scale_one * gain_one).astype(jnp.bfloat16)
    taps = (shift_down(normed), normed, shift_up(normed))
    mixed = (
        jnp.dot(taps[0], taps_full[0], preferred_element_type=jnp.float32)
        + jnp.dot(taps[1], taps_full[1], preferred_element_type=jnp.float32)
        + jnp.dot(taps[2], taps_full[2], preferred_element_type=jnp.float32)
    )
    state = serial_f + mixed
    scale_two = inverse_rms(state)
    second = (state * scale_two * gain_two).astype(jnp.bfloat16)
    result, second_grad, up_grad, down_grad = mlp_pass(second, out_grad, state, w_up, w_down)
    unit_two = state * scale_two
    weighted_two = second_grad.astype(jnp.float32) * gain_two
    gain_two_grad = jnp.sum(second_grad.astype(jnp.float32) * unit_two, axis=0)
    state_grad = out_grad.astype(jnp.float32) + scale_two * (
        weighted_two - unit_two * jnp.mean(weighted_two * unit_two, axis=-1, keepdims=True)
    )
    mixed_grad = state_grad.astype(jnp.bfloat16)
    conv_grad = jnp.stack(
        [
            grouped_weight(taps[0], mixed_grad, groups, inner),
            grouped_weight(taps[1], mixed_grad, groups, inner),
            grouped_weight(taps[2], mixed_grad, groups, inner),
        ],
        axis=0,
    )
    normed_grad = (
        shift_up(tap_back(mixed_grad, taps_full[0]))
        + tap_back(mixed_grad, taps_full[1])
        + shift_down(tap_back(mixed_grad, taps_full[2]))
    ).astype(jnp.bfloat16)
    unit_one = serial_f * scale_one
    weighted_one = normed_grad.astype(jnp.float32) * gain_one
    gain_one_grad = jnp.sum(normed_grad.astype(jnp.float32) * unit_one, axis=0)
    serial_grad = (
        state_grad
        + scale_one
        * (weighted_one - unit_one * jnp.mean(weighted_one * unit_one, axis=-1, keepdims=True))
    ).astype(jnp.bfloat16)
    return (result, serial_grad, (gain_one_grad, conv_grad, gain_two_grad, up_grad, down_grad))


def all_sum(flat, axes):
    devices = lax.axis_size(axes)
    chunk = -(-flat.shape[0] // (devices * 128)) * 128
    padded = jnp.pad(flat, (0, devices * chunk - flat.shape[0])).reshape(devices, chunk)
    pieces = lax.all_to_all(padded, axes, split_axis=0, concat_axis=0, tiled=True)
    part = jnp.sum(pieces, axis=0)
    spread = jnp.broadcast_to(part[None], (devices, chunk))
    whole = lax.all_to_all(spread, axes, split_axis=0, concat_axis=0, tiled=True)
    return whole.reshape(-1)[: flat.shape[0]]


def pair_sum(flat, group):
    devices = lax.axis_size(group)
    chunk = -(-flat.shape[0] // (2 * devices * 128)) * 128
    halves = jnp.pad(flat, (0, 2 * devices * chunk - flat.shape[0])).reshape(2, devices * chunk)
    core = lax.axis_index("core")
    swap = [(0, 1), (1, 0)]
    mine = jnp.where(core == 0, halves[0], halves[1])
    theirs = jnp.where(core == 0, halves[1], halves[0])
    half_sum = mine + lax.ppermute(theirs, "core", swap)
    total = all_sum(half_sum, group)
    other = lax.ppermute(total, "core", swap)
    whole = jnp.where(core == 0, jnp.concatenate([total, other]), jnp.concatenate([other, total]))
    return whole[: flat.shape[0]]


def pass_columns(rows, shift_by):
    return shifted(rows, "tx", shift_by)


def pass_lines(rows, shift_by):
    return shifted(rows, LINES, shift_by)


def body(
    points,
    counts,
    owner,
    zorder,
    border,
    near,
    w_near,
    gain_one,
    conv_w,
    gain_two,
    w_up,
    w_down,
    grad_out,
):
    points_tile = points[0]
    tile_rows, width = points_tile.shape
    lists = border[0]
    border_rows = lists.shape[1]
    cols_count = lax.axis_size("tx")
    lines_count = lax.axis_size(LINES)
    tiles = cols_count * lines_count
    recv_rows = zorder.shape[1]
    capacity = recv_rows // tiles
    near_tile = near[0]
    owner_tile = owner[0]
    sent = jnp.take(points_tile, lists.reshape(-1), axis=0).reshape(4, border_rows, width)
    halo = jnp.concatenate(
        [
            pass_columns(sent[0], -1),
            pass_columns(sent[1], 1),
            pass_lines(sent[2], -1),
            pass_lines(sent[3], 1),
        ],
        axis=0,
    )
    count_near = near_tile.shape[0]
    counts_t = near_counts(near_tile, tile_rows + 4 * border_rows)
    average, linear_part, lifted = tile_forward(points_tile, halo, counts_t, w_near, count_near)
    rank, live = route_ranks(owner_tile, counts[0], tiles)
    slots = jnp.where(live, owner_tile * capacity + rank, tiles * capacity)
    payload = jnp.concatenate([lifted, grad_out[0]], axis=1)
    outgoing = (
        jnp.zeros((tiles * capacity, 2 * width), jnp.bfloat16).at[slots].set(payload, mode="drop")
    )
    incoming = lax.all_to_all(outgoing, ALL, split_axis=0, concat_axis=0, tiled=True)
    serial_both = jnp.take(incoming, zorder[0], axis=0)
    taps_full = block_taps(conv_w)

    results, serial_grads, sums = patch_pass(
        serial_both[:, :width], serial_both[:, width:], gain_one, conv_w, taps_full, gain_two, w_up, w_down
    )
    back = jnp.concatenate(
        [results.reshape(recv_rows, width), serial_grads.reshape(recv_rows, width)], axis=1
    )
    back_slots = jnp.zeros_like(back).at[zorder[0]].set(back)
    returned = lax.all_to_all(back_slots, ALL, split_axis=0, concat_axis=0, tiled=True)
    back_rows = jnp.take(returned, slots, axis=0, mode="fill", fill_value=0)
    out_rows = back_rows[:, :width]
    lifted_grad = back_rows[:, width:]
    patch_flat = jnp.concatenate(
        [sums[0], sums[2], sums[1].reshape(-1), sums[3].reshape(-1), sums[4].reshape(-1)]
    )
    near_grad, row_grad, halo_grad = tile_backward(
        lifted_grad, average, linear_part, counts_t, w_near, count_near
    )
    came_back = (
        pass_columns(halo_grad[0:border_rows], 1),
        pass_columns(halo_grad[border_rows : 2 * border_rows], -1),
        pass_lines(halo_grad[2 * border_rows : 3 * border_rows], 1),
        pass_lines(halo_grad[3 * border_rows : 4 * border_rows], -1),
    )
    for direction in range(4):
        row_grad = row_grad.at[lists[direction]].add(came_back[direction].astype(jnp.float32))
    grads_total = pair_sum(jnp.concatenate([near_grad.reshape(-1), patch_flat]), ("tx", "tyc"))
    near_sum = grads_total[: near_grad.size].reshape(near_grad.shape)
    patch_total = grads_total[near_grad.size :]
    sizes = [width, width, conv_w.size, w_up.size, w_down.size]
    shapes = [(width,), (width,), conv_w.shape, w_up.shape, w_down.shape]
    offsets = [sum(sizes[:index]) for index in range(len(sizes))]
    gain_one_sum, gain_two_sum, conv_sum, up_sum, down_sum = [
        patch_total[start : start + size].reshape(shape)
        for start, size, shape in zip(offsets, sizes, shapes)
    ]
    totals = (gain_one_sum, conv_sum, gain_two_sum, up_sum, down_sum)
    scale = 1.0 / math.sqrt(tiles * tile_rows)
    return (
        out_rows[None],
        row_grad.astype(jnp.bfloat16)[None],
        near_sum * scale,
        totals[0] * scale,
        totals[1] * scale,
        totals[2] * scale,
        totals[3] * scale,
        totals[4] * scale,
    )


def solution(mesh):
    placed = (
        P(ALL, None, None),
        P(ALL),
        P(ALL, None),
        P(ALL, None),
        P(ALL, None, None),
        P(ALL, None, None),
        P(),
        P(),
        P(),
        P(),
        P(),
        P(),
        P(ALL, None, None),
    )
    return jax.shard_map(
        body,
        mesh=Mesh(mesh.devices.reshape(mesh.shape["tx"], -1, 2), ALL),
        in_specs=placed,
        out_specs=(
            P(ALL, None, None),
            P(ALL, None, None),
            P(),
            P(),
            P(),
            P(),
            P(),
            P(),
        ),
        check_vma=False,
    )
```

```python
import math

import jax
import jax.numpy as jnp
from jax import lax
from jax.experimental import pallas as pl
from jax.experimental.pallas import tpu as pltpu
from jax.sharding import Mesh, PartitionSpec as P

PATCH = 1024
LINES = ("tyc", "core")
ALL = ("tx",) + LINES


eps_norm = 1e-06
gelu_coef = 0.7978845608028654
cubic_coef = 0.044715


def shifted(value, axis, steps):
    count = lax.axis_size(axis)
    initial, last = (max(0, -steps), min(count, count - steps))
    return lax.ppermute(value, axis, [(source, source + steps) for source in range(initial, last)])


def gelu_tanh(value):
    inner = gelu_coef * (value + cubic_coef * value * value * value)
    return 0.5 * value * (1.0 + jnp.tanh(inner))


def gelu_slope(value):
    inner = gelu_coef * (value + cubic_coef * value * value * value)
    tangent = jnp.tanh(inner)
    return 0.5 * (1.0 + tangent) + 0.5 * value * (1.0 - tangent * tangent) * gelu_coef * (
        1.0 + 3.0 * cubic_coef * value * value
    )


def inverse_rms(value):
    return lax.rsqrt(jnp.mean(value * value, axis=-1, keepdims=True) + eps_norm)


def near_counts(near_tile, ext_count):
    rows = lax.broadcasted_iota(jnp.int32, (ext_count, near_tile.shape[1]), 0)
    total = jnp.zeros((ext_count, near_tile.shape[1]), jnp.float32)
    for index in range(near_tile.shape[0]):
        total = total + (near_tile[index][None, :] == rows).astype(jnp.float32)
    return total.astype(jnp.bfloat16)


def tile_forward(points_tile, halo_rows, counts_t, w_near, count_near):
    extended = jnp.concatenate([points_tile, halo_rows], axis=0)
    total = lax.dot_general(
        counts_t, extended, (((0,), (0,)), ((), ())), preferred_element_type=jnp.float32
    )
    average = (total * (1.0 / count_near)).astype(jnp.bfloat16)
    linear_part = jnp.dot(average, w_near, preferred_element_type=jnp.float32)
    lifted = (points_tile.astype(jnp.float32) + gelu_tanh(linear_part)).astype(jnp.bfloat16)
    return (average, linear_part, lifted)


def tile_backward(lifted_grad, average, linear_part, counts_t, w_near, count_near):
    tile_rows = lifted_grad.shape[0]
    act_grad = (lifted_grad.astype(jnp.float32) * gelu_slope(linear_part)).astype(jnp.bfloat16)
    near_grad = lax.dot_general(
        average, act_grad, (((0,), (0,)), ((), ())), preferred_element_type=jnp.float32
    )
    spread = lax.dot_general(
        act_grad, w_near, (((1,), (1,)), ((), ())), preferred_element_type=jnp.float32
    ) * (1.0 / count_near)
    spread_hi = spread.astype(jnp.bfloat16)
    spread_lo = (spread - spread_hi.astype(jnp.float32)).astype(jnp.bfloat16)
    ext_grad = jnp.dot(counts_t, spread_hi, preferred_element_type=jnp.float32) + jnp.dot(
        counts_t, spread_lo, preferred_element_type=jnp.float32
    )
    row_grad = lifted_grad.astype(jnp.float32) + ext_grad[:tile_rows]
    halo_grad = ext_grad[tile_rows:].astype(jnp.bfloat16)
    return (near_grad, row_grad, halo_grad)


def route_ranks(owner_tile, count, tiles):
    tile_rows = owner_tile.shape[0]
    index = jnp.arange(tile_rows, dtype=jnp.int32)
    live = index < count
    score = jnp.where(live, owner_tile * tile_rows + index, tiles * tile_rows + index)
    order = jnp.argsort(score, stable=True)
    members = (owner_tile[:, None] == jnp.arange(tiles, dtype=jnp.int32)[None, :]) & live[:, None]
    per_owner = jnp.sum(members.astype(jnp.int32), axis=0)
    starts = jnp.cumsum(per_owner) - per_owner
    sorted_owner = jnp.take(owner_tile, order)
    ranked = index - jnp.take(starts, sorted_owner)
    rank = jnp.zeros((tile_rows,), jnp.int32).at[order].set(ranked)
    return (rank, live)


def route_slots(owner_tile, count, tiles, capacity):
    tile_rows = owner_tile.shape[0]
    live = jnp.arange(tile_rows, dtype=jnp.int32) < count
    owner_ids = lax.broadcasted_iota(jnp.int32, (tile_rows, tiles), 1)
    members = ((owner_tile[:, None] == owner_ids) & live[:, None]).astype(jnp.bfloat16)
    before = (
        lax.broadcasted_iota(jnp.int32, (tile_rows, tile_rows), 1)
        < lax.broadcasted_iota(jnp.int32, (tile_rows, tile_rows), 0)
    ).astype(jnp.bfloat16)
    prefix = jnp.dot(before, members, preferred_element_type=jnp.float32)
    rank = jnp.sum(prefix * members.astype(jnp.float32), axis=1).astype(jnp.int32)
    return jnp.where(live, owner_tile * capacity + rank, tiles * capacity)


def one_hot_rows(ids, size):
    return (lax.broadcasted_iota(jnp.int32, (size, ids.shape[0]), 0) == ids[None, :]).astype(
        jnp.bfloat16
    )


def move_rows(picks, rows, transpose):
    dims = (((0,), (0,)), ((), ())) if transpose else (((1,), (0,)), ((), ()))
    return lax.dot_general(picks, rows, dims, preferred_element_type=jnp.float32).astype(rows.dtype)


def shift_down(rows):
    patches = rows.reshape(-1, PATCH, rows.shape[-1])
    moved = jnp.concatenate([jnp.zeros_like(patches[:, :1]), patches[:, :-1]], axis=1)
    return moved.reshape(rows.shape)


def shift_up(rows):
    patches = rows.reshape(-1, PATCH, rows.shape[-1])
    moved = jnp.concatenate([patches[:, 1:], jnp.zeros_like(patches[:, :1])], axis=1)
    return moved.reshape(rows.shape)


def block_taps(conv_w):
    groups, inner = (conv_w.shape[1], conv_w.shape[2])
    identity_blocks = jnp.eye(groups, dtype=conv_w.dtype)
    full = jnp.einsum("gh,ogab->ogahb", identity_blocks, conv_w)
    return full.reshape(conv_w.shape[0], groups * inner, groups * inner)


def grouped_weight(inputs, outputs, groups, inner):
    length = inputs.shape[0]
    left = inputs.reshape(length, groups, inner)
    right = outputs.reshape(length, groups, inner)
    return jnp.einsum("pga,pgb->gab", left, right, preferred_element_type=jnp.float32)


def tap_back(rows, tap):
    return lax.dot_general(rows, tap, (((1,), (1,)), ((), ())), preferred_element_type=jnp.float32)


def mlp_kernel(
    second_ref, grad_ref, state_ref, up_ref, down_ref, result_ref, sgrad_ref, upg_ref, downg_ref
):
    @pl.when(pl.program_id(0) == 0)
    def _():
        upg_ref[...] = jnp.zeros_like(upg_ref)
        downg_ref[...] = jnp.zeros_like(downg_ref)

    second = second_ref[...]
    out_grad = grad_ref[...]
    hidden_pre = jnp.dot(second, up_ref[...], preferred_element_type=jnp.float32)
    inner = gelu_coef * (hidden_pre + cubic_coef * hidden_pre * hidden_pre * hidden_pre)
    tangent = jnp.tanh(inner)
    hidden = (0.5 * hidden_pre * (1.0 + tangent)).astype(jnp.bfloat16)
    result_ref[...] = (
        state_ref[...] + jnp.dot(hidden, down_ref[...], preferred_element_type=jnp.float32)
    ).astype(jnp.bfloat16)
    downg_ref[...] += lax.dot_general(
        hidden, out_grad, (((0,), (0,)), ((), ())), preferred_element_type=jnp.float32
    )
    hidden_grad = lax.dot_general(
        out_grad, down_ref[...], (((1,), (1,)), ((), ())), preferred_element_type=jnp.float32
    ).astype(jnp.bfloat16)
    slope = 0.5 * (1.0 + tangent) + 0.5 * hidden_pre * (1.0 - tangent * tangent) * gelu_coef * (
        1.0 + 3.0 * cubic_coef * hidden_pre * hidden_pre
    )
    pre_grad = (hidden_grad.astype(jnp.float32) * slope).astype(jnp.bfloat16)
    upg_ref[...] += lax.dot_general(
        second, pre_grad, (((0,), (0,)), ((), ())), preferred_element_type=jnp.float32
    )
    sgrad_ref[...] = lax.dot_general(
        pre_grad, up_ref[...], (((1,), (1,)), ((), ())), preferred_element_type=jnp.float32
    ).astype(jnp.bfloat16)


def mlp_pass(second, out_grad, state, w_up, w_down, block_rows=256):
    rows, width = second.shape
    ffn = w_up.shape[1]
    row_block = pl.BlockSpec((block_rows, width), lambda step: (step, 0))
    whole = lambda shape: pl.BlockSpec(shape, lambda step: (0, 0))
    flops = 2 * rows * width * ffn * 6
    return pl.pallas_call(
        mlp_kernel,
        grid=(rows // block_rows,),
        in_specs=[row_block, row_block, row_block, whole((width, ffn)), whole((ffn, width))],
        out_specs=[row_block, row_block, whole((width, ffn)), whole((ffn, width))],
        out_shape=[
            jax.ShapeDtypeStruct((rows, width), jnp.bfloat16),
            jax.ShapeDtypeStruct((rows, width), jnp.bfloat16),
            jax.ShapeDtypeStruct((width, ffn), jnp.float32),
            jax.ShapeDtypeStruct((ffn, width), jnp.float32),
        ],
        compiler_params=pltpu.CompilerParams(dimension_semantics=("arbitrary",)),
        cost_estimate=pl.CostEstimate(
            flops=flops, transcendentals=rows * ffn, bytes_accessed=rows * width * 10 + 4 * width * ffn * 3
        ),
    )(second, out_grad, state, w_up, w_down)


def patch_pass(serial, out_grad, gain_one, conv_w, taps_full, gain_two, w_up, w_down):
    groups, inner = (conv_w.shape[1], conv_w.shape[2])
    serial_f = serial.astype(jnp.float32)
    scale_one = inverse_rms(serial_f)
    normed = (serial_f * scale_one * gain_one).astype(jnp.bfloat16)
    taps = (shift_down(normed), normed, shift_up(normed))
    mixed = (
        jnp.dot(taps[0], taps_full[0], preferred_element_type=jnp.float32)
        + jnp.dot(taps[1], taps_full[1], preferred_element_type=jnp.float32)
        + jnp.dot(taps[2], taps_full[2], preferred_element_type=jnp.float32)
    )
    state = serial_f + mixed
    scale_two = inverse_rms(state)
    second = (state * scale_two * gain_two).astype(jnp.bfloat16)
    result, second_grad, up_grad, down_grad = mlp_pass(second, out_grad, state, w_up, w_down)
    unit_two = state * scale_two
    weighted_two = second_grad.astype(jnp.float32) * gain_two
    gain_two_grad = jnp.sum(second_grad.astype(jnp.float32) * unit_two, axis=0)
    state_grad = out_grad.astype(jnp.float32) + scale_two * (
        weighted_two - unit_two * jnp.mean(weighted_two * unit_two, axis=-1, keepdims=True)
    )
    mixed_grad = state_grad.astype(jnp.bfloat16)
    conv_grad = jnp.stack(
        [
            grouped_weight(taps[0], mixed_grad, groups, inner),
            grouped_weight(taps[1], mixed_grad, groups, inner),
            grouped_weight(taps[2], mixed_grad, groups, inner),
        ],
        axis=0,
    )
    normed_grad = (
        shift_up(tap_back(mixed_grad, taps_full[0]))
        + tap_back(mixed_grad, taps_full[1])
        + shift_down(tap_back(mixed_grad, taps_full[2]))
    ).astype(jnp.bfloat16)
    unit_one = serial_f * scale_one
    weighted_one = normed_grad.astype(jnp.float32) * gain_one
    gain_one_grad = jnp.sum(normed_grad.astype(jnp.float32) * unit_one, axis=0)
    serial_grad = (
        state_grad
        + scale_one
        * (weighted_one - unit_one * jnp.mean(weighted_one * unit_one, axis=-1, keepdims=True))
    ).astype(jnp.bfloat16)
    return (result, serial_grad, (gain_one_grad, conv_grad, gain_two_grad, up_grad, down_grad))


def all_sum(flat, axes):
    devices = lax.axis_size(axes)
    chunk = -(-flat.shape[0] // (devices * 128)) * 128
    padded = jnp.pad(flat, (0, devices * chunk - flat.shape[0])).reshape(devices, chunk)
    pieces = lax.all_to_all(padded, axes, split_axis=0, concat_axis=0, tiled=True)
    part = jnp.sum(pieces, axis=0)
    spread = jnp.broadcast_to(part[None], (devices, chunk))
    whole = lax.all_to_all(spread, axes, split_axis=0, concat_axis=0, tiled=True)
    return whole.reshape(-1)[: flat.shape[0]]


def pair_sum(flat, group):
    devices = lax.axis_size(group)
    chunk = -(-flat.shape[0] // (2 * devices * 128)) * 128
    halves = jnp.pad(flat, (0, 2 * devices * chunk - flat.shape[0])).reshape(2, devices * chunk)
    core = lax.axis_index("core")
    swap = [(0, 1), (1, 0)]
    mine = jnp.where(core == 0, halves[0], halves[1])
    theirs = jnp.where(core == 0, halves[1], halves[0])
    half_sum = mine + lax.ppermute(theirs, "core", swap)
    total = all_sum(half_sum, group)
    other = lax.ppermute(total, "core", swap)
    whole = jnp.where(core == 0, jnp.concatenate([total, other]), jnp.concatenate([other, total]))
    return whole[: flat.shape[0]]


def pass_columns(rows, shift_by):
    return shifted(rows, "tx", shift_by)


def pass_lines(rows, shift_by):
    return shifted(rows, LINES, shift_by)


def body(
    points,
    counts,
    owner,
    zorder,
    border,
    near,
    w_near,
    gain_one,
    conv_w,
    gain_two,
    w_up,
    w_down,
    grad_out,
):
    points_tile = points[0]
    tile_rows, width = points_tile.shape
    lists = border[0]
    border_rows = lists.shape[1]
    cols_count = lax.axis_size("tx")
    lines_count = lax.axis_size(LINES)
    tiles = cols_count * lines_count
    recv_rows = zorder.shape[1]
    capacity = recv_rows // tiles
    near_tile = near[0]
    owner_tile = owner[0]
    sent = jnp.take(points_tile, lists.reshape(-1), axis=0).reshape(4, border_rows, width)
    halo = jnp.concatenate(
        [
            pass_columns(sent[0], -1),
            pass_columns(sent[1], 1),
            pass_lines(sent[2], -1),
            pass_lines(sent[3], 1),
        ],
        axis=0,
    )
    count_near = near_tile.shape[0]
    counts_t = near_counts(near_tile, tile_rows + 4 * border_rows)
    average, linear_part, lifted = tile_forward(points_tile, halo, counts_t, w_near, count_near)
    slots = route_slots(owner_tile, counts[0], tiles, capacity)
    slot_picks = one_hot_rows(slots, tiles * capacity)
    order_picks = one_hot_rows(zorder[0], recv_rows).T
    payload = jnp.concatenate([lifted, grad_out[0]], axis=1)
    outgoing = move_rows(slot_picks, payload, False)
    incoming = lax.all_to_all(outgoing, ALL, split_axis=0, concat_axis=0, tiled=True)
    serial_both = move_rows(order_picks, incoming, False)
    taps_full = block_taps(conv_w)

    results, serial_grads, sums = patch_pass(
        serial_both[:, :width], serial_both[:, width:], gain_one, conv_w, taps_full, gain_two, w_up, w_down
    )
    back = jnp.concatenate(
        [results.reshape(recv_rows, width), serial_grads.reshape(recv_rows, width)], axis=1
    )
    back_slots = move_rows(order_picks, back, True)
    returned = lax.all_to_all(back_slots, ALL, split_axis=0, concat_axis=0, tiled=True)
    back_rows = move_rows(slot_picks, returned, True)
    out_rows = back_rows[:, :width]
    lifted_grad = back_rows[:, width:]
    patch_flat = jnp.concatenate(
        [sums[0], sums[2], sums[1].reshape(-1), sums[3].reshape(-1), sums[4].reshape(-1)]
    )
    near_grad, row_grad, halo_grad = tile_backward(
        lifted_grad, average, linear_part, counts_t, w_near, count_near
    )
    came_back = (
        pass_columns(halo_grad[0:border_rows], 1),
        pass_columns(halo_grad[border_rows : 2 * border_rows], -1),
        pass_lines(halo_grad[2 * border_rows : 3 * border_rows], 1),
        pass_lines(halo_grad[3 * border_rows : 4 * border_rows], -1),
    )
    for direction in range(4):
        row_grad = row_grad.at[lists[direction]].add(came_back[direction].astype(jnp.float32))
    grads_total = pair_sum(jnp.concatenate([near_grad.reshape(-1), patch_flat]), ("tx", "tyc"))
    near_sum = grads_total[: near_grad.size].reshape(near_grad.shape)
    patch_total = grads_total[near_grad.size :]
    sizes = [width, width, conv_w.size, w_up.size, w_down.size]
    shapes = [(width,), (width,), conv_w.shape, w_up.shape, w_down.shape]
    offsets = [sum(sizes[:index]) for index in range(len(sizes))]
    gain_one_sum, gain_two_sum, conv_sum, up_sum, down_sum = [
        patch_total[start : start + size].reshape(shape)
        for start, size, shape in zip(offsets, sizes, shapes)
    ]
    totals = (gain_one_sum, conv_sum, gain_two_sum, up_sum, down_sum)
    scale = 1.0 / math.sqrt(tiles * tile_rows)
    return (
        out_rows[None],
        row_grad.astype(jnp.bfloat16)[None],
        near_sum * scale,
        totals[0] * scale,
        totals[1] * scale,
        totals[2] * scale,
        totals[3] * scale,
        totals[4] * scale,
    )


def solution(mesh):
    placed = (
        P(ALL, None, None),
        P(ALL),
        P(ALL, None),
        P(ALL, None),
        P(ALL, None, None),
        P(ALL, None, None),
        P(),
        P(),
        P(),
        P(),
        P(),
        P(),
        P(ALL, None, None),
    )
    return jax.shard_map(
        body,
        mesh=Mesh(mesh.devices.reshape(mesh.shape["tx"], -1, 2), ALL),
        in_specs=placed,
        out_specs=(
            P(ALL, None, None),
            P(ALL, None, None),
            P(),
            P(),
            P(),
            P(),
            P(),
            P(),
        ),
        check_vma=False,
    )
```

```python
import math

import jax
import jax.numpy as jnp
from jax import lax
from jax.experimental import pallas as pl
from jax.experimental.pallas import tpu as pltpu
from jax.sharding import Mesh, PartitionSpec as P

PATCH = 1024
LINES = ("tyc", "core")
ALL = ("tx",) + LINES


eps_norm = 1e-06
gelu_coef = 0.7978845608028654
cubic_coef = 0.044715


def shifted(value, axis, steps):
    count = lax.axis_size(axis)
    initial, last = (max(0, -steps), min(count, count - steps))
    return lax.ppermute(value, axis, [(source, source + steps) for source in range(initial, last)])


def gelu_tanh(value):
    inner = gelu_coef * (value + cubic_coef * value * value * value)
    return 0.5 * value * (1.0 + jnp.tanh(inner))


def gelu_slope(value):
    inner = gelu_coef * (value + cubic_coef * value * value * value)
    tangent = jnp.tanh(inner)
    return 0.5 * (1.0 + tangent) + 0.5 * value * (1.0 - tangent * tangent) * gelu_coef * (
        1.0 + 3.0 * cubic_coef * value * value
    )


def inverse_rms(value):
    return lax.rsqrt(jnp.mean(value * value, axis=-1, keepdims=True) + eps_norm)


def near_counts(near_tile, ext_count):
    rows = lax.broadcasted_iota(jnp.int32, (ext_count, near_tile.shape[1]), 0)
    total = jnp.zeros((ext_count, near_tile.shape[1]), jnp.float32)
    for index in range(near_tile.shape[0]):
        total = total + (near_tile[index][None, :] == rows).astype(jnp.float32)
    return total.astype(jnp.bfloat16)


def tile_forward(points_tile, halo_rows, counts_t, w_near, count_near):
    extended = jnp.concatenate([points_tile, halo_rows], axis=0)
    total = lax.dot_general(
        counts_t, extended, (((0,), (0,)), ((), ())), preferred_element_type=jnp.float32
    )
    average = (total * (1.0 / count_near)).astype(jnp.bfloat16)
    linear_part = jnp.dot(average, w_near, preferred_element_type=jnp.float32)
    lifted = (points_tile.astype(jnp.float32) + gelu_tanh(linear_part)).astype(jnp.bfloat16)
    return (average, linear_part, lifted)


def tile_backward(lifted_grad, average, linear_part, counts_t, w_near, count_near):
    tile_rows = lifted_grad.shape[0]
    act_grad = (lifted_grad.astype(jnp.float32) * gelu_slope(linear_part)).astype(jnp.bfloat16)
    near_grad = lax.dot_general(
        average, act_grad, (((0,), (0,)), ((), ())), preferred_element_type=jnp.float32
    )
    spread = lax.dot_general(
        act_grad, w_near, (((1,), (1,)), ((), ())), preferred_element_type=jnp.float32
    ) * (1.0 / count_near)
    spread_hi = spread.astype(jnp.bfloat16)
    spread_lo = (spread - spread_hi.astype(jnp.float32)).astype(jnp.bfloat16)
    ext_grad = jnp.dot(counts_t, spread_hi, preferred_element_type=jnp.float32) + jnp.dot(
        counts_t, spread_lo, preferred_element_type=jnp.float32
    )
    row_grad = lifted_grad.astype(jnp.float32) + ext_grad[:tile_rows]
    halo_grad = ext_grad[tile_rows:].astype(jnp.bfloat16)
    return (near_grad, row_grad, halo_grad)


def route_ranks(owner_tile, count, tiles):
    tile_rows = owner_tile.shape[0]
    index = jnp.arange(tile_rows, dtype=jnp.int32)
    live = index < count
    score = jnp.where(live, owner_tile * tile_rows + index, tiles * tile_rows + index)
    order = jnp.argsort(score, stable=True)
    members = (owner_tile[:, None] == jnp.arange(tiles, dtype=jnp.int32)[None, :]) & live[:, None]
    per_owner = jnp.sum(members.astype(jnp.int32), axis=0)
    starts = jnp.cumsum(per_owner) - per_owner
    sorted_owner = jnp.take(owner_tile, order)
    ranked = index - jnp.take(starts, sorted_owner)
    rank = jnp.zeros((tile_rows,), jnp.int32).at[order].set(ranked)
    return (rank, live)


def route_slots(owner_tile, count, tiles, capacity):
    tile_rows = owner_tile.shape[0]
    live = jnp.arange(tile_rows, dtype=jnp.int32) < count
    owner_ids = lax.broadcasted_iota(jnp.int32, (tile_rows, tiles), 1)
    members = ((owner_tile[:, None] == owner_ids) & live[:, None]).astype(jnp.bfloat16)
    before = (
        lax.broadcasted_iota(jnp.int32, (tile_rows, tile_rows), 1)
        < lax.broadcasted_iota(jnp.int32, (tile_rows, tile_rows), 0)
    ).astype(jnp.bfloat16)
    prefix = jnp.dot(before, members, preferred_element_type=jnp.float32)
    rank = jnp.sum(prefix * members.astype(jnp.float32), axis=1).astype(jnp.int32)
    return jnp.where(live, owner_tile * capacity + rank, tiles * capacity)


def one_hot_rows(ids, size):
    return (lax.broadcasted_iota(jnp.int32, (size, ids.shape[0]), 0) == ids[None, :]).astype(
        jnp.bfloat16
    )


def move_rows(picks, rows, transpose):
    dims = (((0,), (0,)), ((), ())) if transpose else (((1,), (0,)), ((), ()))
    return lax.dot_general(picks, rows, dims, preferred_element_type=jnp.float32).astype(rows.dtype)


def shift_down(rows):
    patches = rows.reshape(-1, PATCH, rows.shape[-1])
    moved = jnp.concatenate([jnp.zeros_like(patches[:, :1]), patches[:, :-1]], axis=1)
    return moved.reshape(rows.shape)


def shift_up(rows):
    patches = rows.reshape(-1, PATCH, rows.shape[-1])
    moved = jnp.concatenate([patches[:, 1:], jnp.zeros_like(patches[:, :1])], axis=1)
    return moved.reshape(rows.shape)


def block_taps(conv_w):
    groups, inner = (conv_w.shape[1], conv_w.shape[2])
    identity_blocks = jnp.eye(groups, dtype=conv_w.dtype)
    full = jnp.einsum("gh,ogab->ogahb", identity_blocks, conv_w)
    return full.reshape(conv_w.shape[0], groups * inner, groups * inner)


def grouped_weight(inputs, outputs, groups, inner):
    length = inputs.shape[0]
    left = inputs.reshape(length, groups, inner)
    right = outputs.reshape(length, groups, inner)
    return jnp.einsum("pga,pgb->gab", left, right, preferred_element_type=jnp.float32)


def tap_back(rows, tap):
    return lax.dot_general(rows, tap, (((1,), (1,)), ((), ())), preferred_element_type=jnp.float32)


def mlp_kernel(
    second_ref, grad_ref, state_ref, up_ref, down_ref, result_ref, sgrad_ref, upg_ref, downg_ref
):
    @pl.when(pl.program_id(0) == 0)
    def _():
        upg_ref[...] = jnp.zeros_like(upg_ref)
        downg_ref[...] = jnp.zeros_like(downg_ref)

    second = second_ref[...]
    out_grad = grad_ref[...]
    hidden_pre = jnp.dot(second, up_ref[...], preferred_element_type=jnp.float32)
    inner = gelu_coef * (hidden_pre + cubic_coef * hidden_pre * hidden_pre * hidden_pre)
    tangent = jnp.tanh(inner)
    hidden = (0.5 * hidden_pre * (1.0 + tangent)).astype(jnp.bfloat16)
    result_ref[...] = (
        state_ref[...] + jnp.dot(hidden, down_ref[...], preferred_element_type=jnp.float32)
    ).astype(jnp.bfloat16)
    downg_ref[...] += lax.dot_general(
        hidden, out_grad, (((0,), (0,)), ((), ())), preferred_element_type=jnp.float32
    )
    hidden_grad = lax.dot_general(
        out_grad, down_ref[...], (((1,), (1,)), ((), ())), preferred_element_type=jnp.float32
    ).astype(jnp.bfloat16)
    slope = 0.5 * (1.0 + tangent) + 0.5 * hidden_pre * (1.0 - tangent * tangent) * gelu_coef * (
        1.0 + 3.0 * cubic_coef * hidden_pre * hidden_pre
    )
    pre_grad = (hidden_grad.astype(jnp.float32) * slope).astype(jnp.bfloat16)
    upg_ref[...] += lax.dot_general(
        second, pre_grad, (((0,), (0,)), ((), ())), preferred_element_type=jnp.float32
    )
    sgrad_ref[...] = lax.dot_general(
        pre_grad, up_ref[...], (((1,), (1,)), ((), ())), preferred_element_type=jnp.float32
    ).astype(jnp.bfloat16)


def mlp_pass(second, out_grad, state, w_up, w_down, block_rows=256):
    rows, width = second.shape
    ffn = w_up.shape[1]
    row_block = pl.BlockSpec((block_rows, width), lambda step: (step, 0))
    whole = lambda shape: pl.BlockSpec(shape, lambda step: (0, 0))
    flops = 2 * rows * width * ffn * 6
    return pl.pallas_call(
        mlp_kernel,
        grid=(rows // block_rows,),
        in_specs=[row_block, row_block, row_block, whole((width, ffn)), whole((ffn, width))],
        out_specs=[row_block, row_block, whole((width, ffn)), whole((ffn, width))],
        out_shape=[
            jax.ShapeDtypeStruct((rows, width), jnp.bfloat16),
            jax.ShapeDtypeStruct((rows, width), jnp.bfloat16),
            jax.ShapeDtypeStruct((width, ffn), jnp.float32),
            jax.ShapeDtypeStruct((ffn, width), jnp.float32),
        ],
        compiler_params=pltpu.CompilerParams(dimension_semantics=("arbitrary",)),
        cost_estimate=pl.CostEstimate(
            flops=flops, transcendentals=rows * ffn, bytes_accessed=rows * width * 10 + 4 * width * ffn * 3
        ),
    )(second, out_grad, state, w_up, w_down)


def patch_pass(serial, out_grad, gain_one, conv_w, taps_full, gain_two, w_up, w_down):
    groups, inner = (conv_w.shape[1], conv_w.shape[2])
    serial_f = serial.astype(jnp.float32)
    scale_one = inverse_rms(serial_f)
    normed = (serial_f * scale_one * gain_one).astype(jnp.bfloat16)
    taps = (shift_down(normed), normed, shift_up(normed))
    mixed = (
        jnp.dot(taps[0], taps_full[0], preferred_element_type=jnp.float32)
        + jnp.dot(taps[1], taps_full[1], preferred_element_type=jnp.float32)
        + jnp.dot(taps[2], taps_full[2], preferred_element_type=jnp.float32)
    )
    state = serial_f + mixed
    scale_two = inverse_rms(state)
    second = (state * scale_two * gain_two).astype(jnp.bfloat16)
    result, second_grad, up_grad, down_grad = mlp_pass(second, out_grad, state, w_up, w_down)
    unit_two = state * scale_two
    weighted_two = second_grad.astype(jnp.float32) * gain_two
    gain_two_grad = jnp.sum(second_grad.astype(jnp.float32) * unit_two, axis=0)
    state_grad = out_grad.astype(jnp.float32) + scale_two * (
        weighted_two - unit_two * jnp.mean(weighted_two * unit_two, axis=-1, keepdims=True)
    )
    mixed_grad = state_grad.astype(jnp.bfloat16)
    conv_grad = jnp.stack(
        [
            grouped_weight(taps[0], mixed_grad, groups, inner),
            grouped_weight(taps[1], mixed_grad, groups, inner),
            grouped_weight(taps[2], mixed_grad, groups, inner),
        ],
        axis=0,
    )
    normed_grad = (
        shift_up(tap_back(mixed_grad, taps_full[0]))
        + tap_back(mixed_grad, taps_full[1])
        + shift_down(tap_back(mixed_grad, taps_full[2]))
    ).astype(jnp.bfloat16)
    unit_one = serial_f * scale_one
    weighted_one = normed_grad.astype(jnp.float32) * gain_one
    gain_one_grad = jnp.sum(normed_grad.astype(jnp.float32) * unit_one, axis=0)
    serial_grad = (
        state_grad
        + scale_one
        * (weighted_one - unit_one * jnp.mean(weighted_one * unit_one, axis=-1, keepdims=True))
    ).astype(jnp.bfloat16)
    return (result, serial_grad, (gain_one_grad, conv_grad, gain_two_grad, up_grad, down_grad))


def all_sum(flat, axes):
    devices = lax.axis_size(axes)
    chunk = -(-flat.shape[0] // (devices * 128)) * 128
    padded = jnp.pad(flat, (0, devices * chunk - flat.shape[0])).reshape(devices, chunk)
    pieces = lax.all_to_all(padded, axes, split_axis=0, concat_axis=0, tiled=True)
    part = jnp.sum(pieces, axis=0)
    spread = jnp.broadcast_to(part[None], (devices, chunk))
    whole = lax.all_to_all(spread, axes, split_axis=0, concat_axis=0, tiled=True)
    return whole.reshape(-1)[: flat.shape[0]]


def pair_sum(flat, group):
    devices = lax.axis_size(group)
    chunk = -(-flat.shape[0] // (2 * devices * 128)) * 128
    halves = jnp.pad(flat, (0, 2 * devices * chunk - flat.shape[0])).reshape(2, devices * chunk)
    core = lax.axis_index("core")
    swap = [(0, 1), (1, 0)]
    mine = jnp.where(core == 0, halves[0], halves[1])
    theirs = jnp.where(core == 0, halves[1], halves[0])
    half_sum = mine + lax.ppermute(theirs, "core", swap)
    total = all_sum(half_sum, group)
    other = lax.ppermute(total, "core", swap)
    whole = jnp.where(core == 0, jnp.concatenate([total, other]), jnp.concatenate([other, total]))
    return whole[: flat.shape[0]]


def pass_columns(rows, shift_by):
    return shifted(rows, "tx", shift_by)


def pass_lines(rows, shift_by):
    return shifted(rows, LINES, shift_by)


def body(
    points,
    counts,
    owner,
    zorder,
    border,
    near,
    w_near,
    gain_one,
    conv_w,
    gain_two,
    w_up,
    w_down,
    grad_out,
):
    points_tile = points[0]
    tile_rows, width = points_tile.shape
    lists = border[0]
    border_rows = lists.shape[1]
    cols_count = lax.axis_size("tx")
    lines_count = lax.axis_size(LINES)
    tiles = cols_count * lines_count
    recv_rows = zorder.shape[1]
    capacity = recv_rows // tiles
    near_tile = near[0]
    owner_tile = owner[0]
    sent = jnp.take(points_tile, lists.reshape(-1), axis=0).reshape(4, border_rows, width)
    halo = jnp.concatenate(
        [
            pass_columns(sent[0], -1),
            pass_columns(sent[1], 1),
            pass_lines(sent[2], -1),
            pass_lines(sent[3], 1),
        ],
        axis=0,
    )
    count_near = near_tile.shape[0]
    counts_t = near_counts(near_tile, tile_rows + 4 * border_rows)
    average, linear_part, lifted = tile_forward(points_tile, halo, counts_t, w_near, count_near)
    slots = route_slots(owner_tile, counts[0], tiles, capacity)
    slot_picks = one_hot_rows(slots, tiles * capacity)
    order_picks = one_hot_rows(zorder[0], recv_rows).T
    grad_incoming = lax.all_to_all(
        move_rows(slot_picks, grad_out[0], False), ALL, split_axis=0, concat_axis=0, tiled=True
    )
    lifted_incoming = lax.all_to_all(
        move_rows(slot_picks, lifted, False), ALL, split_axis=0, concat_axis=0, tiled=True
    )
    incoming = jnp.concatenate([lifted_incoming, grad_incoming], axis=1)
    serial_both = move_rows(order_picks, incoming, False)
    taps_full = block_taps(conv_w)

    results, serial_grads, sums = patch_pass(
        serial_both[:, :width], serial_both[:, width:], gain_one, conv_w, taps_full, gain_two, w_up, w_down
    )
    grad_returned = lax.all_to_all(
        move_rows(order_picks, serial_grads.reshape(recv_rows, width), True),
        ALL, split_axis=0, concat_axis=0, tiled=True,
    )
    lifted_grad = move_rows(slot_picks, grad_returned, True)
    result_returned = lax.all_to_all(
        move_rows(order_picks, results.reshape(recv_rows, width), True),
        ALL, split_axis=0, concat_axis=0, tiled=True,
    )
    out_rows = move_rows(slot_picks, result_returned, True)
    patch_flat = jnp.concatenate(
        [sums[0], sums[2], sums[1].reshape(-1), sums[3].reshape(-1), sums[4].reshape(-1)]
    )
    near_grad, row_grad, halo_grad = tile_backward(
        lifted_grad, average, linear_part, counts_t, w_near, count_near
    )
    came_back = (
        pass_columns(halo_grad[0:border_rows], 1),
        pass_columns(halo_grad[border_rows : 2 * border_rows], -1),
        pass_lines(halo_grad[2 * border_rows : 3 * border_rows], 1),
        pass_lines(halo_grad[3 * border_rows : 4 * border_rows], -1),
    )
    for direction in range(4):
        row_grad = row_grad.at[lists[direction]].add(came_back[direction].astype(jnp.float32))
    grads_total = pair_sum(jnp.concatenate([near_grad.reshape(-1), patch_flat]), ("tx", "tyc"))
    near_sum = grads_total[: near_grad.size].reshape(near_grad.shape)
    patch_total = grads_total[near_grad.size :]
    sizes = [width, width, conv_w.size, w_up.size, w_down.size]
    shapes = [(width,), (width,), conv_w.shape, w_up.shape, w_down.shape]
    offsets = [sum(sizes[:index]) for index in range(len(sizes))]
    gain_one_sum, gain_two_sum, conv_sum, up_sum, down_sum = [
        patch_total[start : start + size].reshape(shape)
        for start, size, shape in zip(offsets, sizes, shapes)
    ]
    totals = (gain_one_sum, conv_sum, gain_two_sum, up_sum, down_sum)
    scale = 1.0 / math.sqrt(tiles * tile_rows)
    return (
        out_rows[None],
        row_grad.astype(jnp.bfloat16)[None],
        near_sum * scale,
        totals[0] * scale,
        totals[1] * scale,
        totals[2] * scale,
        totals[3] * scale,
        totals[4] * scale,
    )


def solution(mesh):
    placed = (
        P(ALL, None, None),
        P(ALL),
        P(ALL, None),
        P(ALL, None),
        P(ALL, None, None),
        P(ALL, None, None),
        P(),
        P(),
        P(),
        P(),
        P(),
        P(),
        P(ALL, None, None),
    )
    return jax.shard_map(
        body,
        mesh=Mesh(mesh.devices.reshape(mesh.shape["tx"], -1, 2), ALL),
        in_specs=placed,
        out_specs=(
            P(ALL, None, None),
            P(ALL, None, None),
            P(),
            P(),
            P(),
            P(),
            P(),
            P(),
        ),
        check_vma=False,
    )
```

```python
import math

import jax
import jax.numpy as jnp
from jax import lax
from jax.experimental import pallas as pl
from jax.experimental.pallas import tpu as pltpu
from jax.sharding import Mesh, PartitionSpec as P

PATCH = 1024
LINES = ("tyc", "core")
ALL = ("tx",) + LINES


eps_norm = 1e-06
gelu_coef = 0.7978845608028654
cubic_coef = 0.044715


def shifted(value, axis, steps):
    count = lax.axis_size(axis)
    initial, last = (max(0, -steps), min(count, count - steps))
    return lax.ppermute(value, axis, [(source, source + steps) for source in range(initial, last)])


def gelu_tanh(value):
    inner = gelu_coef * (value + cubic_coef * value * value * value)
    return 0.5 * value * (1.0 + jnp.tanh(inner))


def gelu_slope(value):
    inner = gelu_coef * (value + cubic_coef * value * value * value)
    tangent = jnp.tanh(inner)
    return 0.5 * (1.0 + tangent) + 0.5 * value * (1.0 - tangent * tangent) * gelu_coef * (
        1.0 + 3.0 * cubic_coef * value * value
    )


def inverse_rms(value):
    return lax.rsqrt(jnp.mean(value * value, axis=-1, keepdims=True) + eps_norm)


def near_counts(near_tile, ext_count):
    rows = lax.broadcasted_iota(jnp.int32, (ext_count, near_tile.shape[1]), 0)
    total = jnp.zeros((ext_count, near_tile.shape[1]), jnp.float32)
    for index in range(near_tile.shape[0]):
        total = total + (near_tile[index][None, :] == rows).astype(jnp.float32)
    return total.astype(jnp.bfloat16)


def tile_forward(points_tile, halo_rows, counts_t, w_near, count_near):
    extended = jnp.concatenate([points_tile, halo_rows], axis=0)
    total = lax.dot_general(
        counts_t, extended, (((0,), (0,)), ((), ())), preferred_element_type=jnp.float32
    )
    average = (total * (1.0 / count_near)).astype(jnp.bfloat16)
    linear_part = jnp.dot(average, w_near, preferred_element_type=jnp.float32)
    lifted = (points_tile.astype(jnp.float32) + gelu_tanh(linear_part)).astype(jnp.bfloat16)
    return (average, linear_part, lifted)


def tile_backward(lifted_grad, average, linear_part, counts_t, w_near, count_near):
    tile_rows = lifted_grad.shape[0]
    act_grad = (lifted_grad.astype(jnp.float32) * gelu_slope(linear_part)).astype(jnp.bfloat16)
    near_grad = lax.dot_general(
        average, act_grad, (((0,), (0,)), ((), ())), preferred_element_type=jnp.float32
    )
    spread = lax.dot_general(
        act_grad, w_near, (((1,), (1,)), ((), ())), preferred_element_type=jnp.float32
    ) * (1.0 / count_near)
    spread_hi = spread.astype(jnp.bfloat16)
    spread_lo = (spread - spread_hi.astype(jnp.float32)).astype(jnp.bfloat16)
    ext_grad = jnp.dot(counts_t, spread_hi, preferred_element_type=jnp.float32) + jnp.dot(
        counts_t, spread_lo, preferred_element_type=jnp.float32
    )
    row_grad = lifted_grad.astype(jnp.float32) + ext_grad[:tile_rows]
    halo_grad = ext_grad[tile_rows:].astype(jnp.bfloat16)
    return (near_grad, row_grad, halo_grad)


def route_ranks(owner_tile, count, tiles):
    tile_rows = owner_tile.shape[0]
    index = jnp.arange(tile_rows, dtype=jnp.int32)
    live = index < count
    score = jnp.where(live, owner_tile * tile_rows + index, tiles * tile_rows + index)
    order = jnp.argsort(score, stable=True)
    members = (owner_tile[:, None] == jnp.arange(tiles, dtype=jnp.int32)[None, :]) & live[:, None]
    per_owner = jnp.sum(members.astype(jnp.int32), axis=0)
    starts = jnp.cumsum(per_owner) - per_owner
    sorted_owner = jnp.take(owner_tile, order)
    ranked = index - jnp.take(starts, sorted_owner)
    rank = jnp.zeros((tile_rows,), jnp.int32).at[order].set(ranked)
    return (rank, live)


def route_slots(owner_tile, count, tiles, capacity):
    tile_rows = owner_tile.shape[0]
    live = jnp.arange(tile_rows, dtype=jnp.int32) < count
    owner_ids = lax.broadcasted_iota(jnp.int32, (tile_rows, tiles), 1)
    members = ((owner_tile[:, None] == owner_ids) & live[:, None]).astype(jnp.bfloat16)
    before = (
        lax.broadcasted_iota(jnp.int32, (tile_rows, tile_rows), 1)
        < lax.broadcasted_iota(jnp.int32, (tile_rows, tile_rows), 0)
    ).astype(jnp.bfloat16)
    prefix = jnp.dot(before, members, preferred_element_type=jnp.float32)
    rank = jnp.sum(prefix * members.astype(jnp.float32), axis=1).astype(jnp.int32)
    return jnp.where(live, owner_tile * capacity + rank, tiles * capacity)


def one_hot_rows(ids, size):
    return (lax.broadcasted_iota(jnp.int32, (size, ids.shape[0]), 0) == ids[None, :]).astype(
        jnp.bfloat16
    )


def move_rows(picks, rows, transpose):
    dims = (((0,), (0,)), ((), ())) if transpose else (((1,), (0,)), ((), ()))
    return lax.dot_general(picks, rows, dims, preferred_element_type=jnp.float32).astype(rows.dtype)


def shift_down(rows):
    patches = rows.reshape(-1, PATCH, rows.shape[-1])
    moved = jnp.concatenate([jnp.zeros_like(patches[:, :1]), patches[:, :-1]], axis=1)
    return moved.reshape(rows.shape)


def shift_up(rows):
    patches = rows.reshape(-1, PATCH, rows.shape[-1])
    moved = jnp.concatenate([patches[:, 1:], jnp.zeros_like(patches[:, :1])], axis=1)
    return moved.reshape(rows.shape)


def block_taps(conv_w):
    groups, inner = (conv_w.shape[1], conv_w.shape[2])
    identity_blocks = jnp.eye(groups, dtype=conv_w.dtype)
    full = jnp.einsum("gh,ogab->ogahb", identity_blocks, conv_w)
    return full.reshape(conv_w.shape[0], groups * inner, groups * inner)


def grouped_weight(inputs, outputs, groups, inner):
    length = inputs.shape[0]
    left = inputs.reshape(length, groups, inner)
    right = outputs.reshape(length, groups, inner)
    return jnp.einsum("pga,pgb->gab", left, right, preferred_element_type=jnp.float32)


def tap_back(rows, tap):
    return lax.dot_general(rows, tap, (((1,), (1,)), ((), ())), preferred_element_type=jnp.float32)


def mlp_kernel(
    second_ref, grad_ref, state_ref, up_ref, down_ref, result_ref, sgrad_ref, upg_ref, downg_ref
):
    @pl.when(pl.program_id(0) == 0)
    def _():
        upg_ref[...] = jnp.zeros_like(upg_ref)
        downg_ref[...] = jnp.zeros_like(downg_ref)

    second = second_ref[...]
    out_grad = grad_ref[...]
    hidden_pre = jnp.dot(second, up_ref[...], preferred_element_type=jnp.float32)
    inner = gelu_coef * (hidden_pre + cubic_coef * hidden_pre * hidden_pre * hidden_pre)
    tangent = jnp.tanh(inner)
    hidden = (0.5 * hidden_pre * (1.0 + tangent)).astype(jnp.bfloat16)
    result_ref[...] = (
        state_ref[...] + jnp.dot(hidden, down_ref[...], preferred_element_type=jnp.float32)
    ).astype(jnp.bfloat16)
    downg_ref[...] += lax.dot_general(
        hidden, out_grad, (((0,), (0,)), ((), ())), preferred_element_type=jnp.float32
    )
    hidden_grad = lax.dot_general(
        out_grad, down_ref[...], (((1,), (1,)), ((), ())), preferred_element_type=jnp.float32
    ).astype(jnp.bfloat16)
    slope = 0.5 * (1.0 + tangent) + 0.5 * hidden_pre * (1.0 - tangent * tangent) * gelu_coef * (
        1.0 + 3.0 * cubic_coef * hidden_pre * hidden_pre
    )
    pre_grad = (hidden_grad.astype(jnp.float32) * slope).astype(jnp.bfloat16)
    upg_ref[...] += lax.dot_general(
        second, pre_grad, (((0,), (0,)), ((), ())), preferred_element_type=jnp.float32
    )
    sgrad_ref[...] = lax.dot_general(
        pre_grad, up_ref[...], (((1,), (1,)), ((), ())), preferred_element_type=jnp.float32
    ).astype(jnp.bfloat16)


def mlp_pass(second, out_grad, state, w_up, w_down, block_rows=512):
    rows, width = second.shape
    ffn = w_up.shape[1]
    row_block = pl.BlockSpec((block_rows, width), lambda step: (step, 0))
    whole = lambda shape: pl.BlockSpec(shape, lambda step: (0, 0))
    flops = 2 * rows * width * ffn * 6
    return pl.pallas_call(
        mlp_kernel,
        grid=(rows // block_rows,),
        in_specs=[row_block, row_block, row_block, whole((width, ffn)), whole((ffn, width))],
        out_specs=[row_block, row_block, whole((width, ffn)), whole((ffn, width))],
        out_shape=[
            jax.ShapeDtypeStruct((rows, width), jnp.bfloat16),
            jax.ShapeDtypeStruct((rows, width), jnp.bfloat16),
            jax.ShapeDtypeStruct((width, ffn), jnp.float32),
            jax.ShapeDtypeStruct((ffn, width), jnp.float32),
        ],
        compiler_params=pltpu.CompilerParams(dimension_semantics=("arbitrary",)),
        cost_estimate=pl.CostEstimate(
            flops=flops, transcendentals=rows * ffn, bytes_accessed=rows * width * 10 + 4 * width * ffn * 3
        ),
    )(second, out_grad, state, w_up, w_down)


def patch_pass(serial, out_grad, gain_one, conv_w, taps_full, gain_two, w_up, w_down):
    groups, inner = (conv_w.shape[1], conv_w.shape[2])
    serial_f = serial.astype(jnp.float32)
    scale_one = inverse_rms(serial_f)
    normed = (serial_f * scale_one * gain_one).astype(jnp.bfloat16)
    taps = (shift_down(normed), normed, shift_up(normed))
    mixed = (
        jnp.dot(taps[0], taps_full[0], preferred_element_type=jnp.float32)
        + jnp.dot(taps[1], taps_full[1], preferred_element_type=jnp.float32)
        + jnp.dot(taps[2], taps_full[2], preferred_element_type=jnp.float32)
    )
    state = serial_f + mixed
    scale_two = inverse_rms(state)
    second = (state * scale_two * gain_two).astype(jnp.bfloat16)
    result, second_grad, up_grad, down_grad = mlp_pass(second, out_grad, state, w_up, w_down)
    unit_two = state * scale_two
    weighted_two = second_grad.astype(jnp.float32) * gain_two
    gain_two_grad = jnp.sum(second_grad.astype(jnp.float32) * unit_two, axis=0)
    state_grad = out_grad.astype(jnp.float32) + scale_two * (
        weighted_two - unit_two * jnp.mean(weighted_two * unit_two, axis=-1, keepdims=True)
    )
    mixed_grad = state_grad.astype(jnp.bfloat16)
    conv_grad = jnp.stack(
        [
            grouped_weight(taps[0], mixed_grad, groups, inner),
            grouped_weight(taps[1], mixed_grad, groups, inner),
            grouped_weight(taps[2], mixed_grad, groups, inner),
        ],
        axis=0,
    )
    normed_grad = (
        shift_up(tap_back(mixed_grad, taps_full[0]))
        + tap_back(mixed_grad, taps_full[1])
        + shift_down(tap_back(mixed_grad, taps_full[2]))
    ).astype(jnp.bfloat16)
    unit_one = serial_f * scale_one
    weighted_one = normed_grad.astype(jnp.float32) * gain_one
    gain_one_grad = jnp.sum(normed_grad.astype(jnp.float32) * unit_one, axis=0)
    serial_grad = (
        state_grad
        + scale_one
        * (weighted_one - unit_one * jnp.mean(weighted_one * unit_one, axis=-1, keepdims=True))
    ).astype(jnp.bfloat16)
    return (result, serial_grad, (gain_one_grad, conv_grad, gain_two_grad, up_grad, down_grad))


def all_sum(flat, axes):
    devices = lax.axis_size(axes)
    chunk = -(-flat.shape[0] // (devices * 128)) * 128
    padded = jnp.pad(flat, (0, devices * chunk - flat.shape[0])).reshape(devices, chunk)
    pieces = lax.all_to_all(padded, axes, split_axis=0, concat_axis=0, tiled=True)
    part = jnp.sum(pieces, axis=0)
    spread = jnp.broadcast_to(part[None], (devices, chunk))
    whole = lax.all_to_all(spread, axes, split_axis=0, concat_axis=0, tiled=True)
    return whole.reshape(-1)[: flat.shape[0]]


def pair_sum(flat, group):
    devices = lax.axis_size(group)
    chunk = -(-flat.shape[0] // (2 * devices * 128)) * 128
    halves = jnp.pad(flat, (0, 2 * devices * chunk - flat.shape[0])).reshape(2, devices * chunk)
    core = lax.axis_index("core")
    swap = [(0, 1), (1, 0)]
    mine = jnp.where(core == 0, halves[0], halves[1])
    theirs = jnp.where(core == 0, halves[1], halves[0])
    half_sum = mine + lax.ppermute(theirs, "core", swap)
    total = all_sum(half_sum, group)
    other = lax.ppermute(total, "core", swap)
    whole = jnp.where(core == 0, jnp.concatenate([total, other]), jnp.concatenate([other, total]))
    return whole[: flat.shape[0]]


def pass_columns(rows, shift_by):
    return shifted(rows, "tx", shift_by)


def pass_lines(rows, shift_by):
    return shifted(rows, LINES, shift_by)


def body(
    points,
    counts,
    owner,
    zorder,
    border,
    near,
    w_near,
    gain_one,
    conv_w,
    gain_two,
    w_up,
    w_down,
    grad_out,
):
    points_tile = points[0]
    tile_rows, width = points_tile.shape
    lists = border[0]
    border_rows = lists.shape[1]
    cols_count = lax.axis_size("tx")
    lines_count = lax.axis_size(LINES)
    tiles = cols_count * lines_count
    recv_rows = zorder.shape[1]
    capacity = recv_rows // tiles
    near_tile = near[0]
    owner_tile = owner[0]
    sent = jnp.take(points_tile, lists.reshape(-1), axis=0).reshape(4, border_rows, width)
    halo = jnp.concatenate(
        [
            pass_columns(sent[0], -1),
            pass_columns(sent[1], 1),
            pass_lines(sent[2], -1),
            pass_lines(sent[3], 1),
        ],
        axis=0,
    )
    count_near = near_tile.shape[0]
    counts_t = near_counts(near_tile, tile_rows + 4 * border_rows)
    average, linear_part, lifted = tile_forward(points_tile, halo, counts_t, w_near, count_near)
    slots = route_slots(owner_tile, counts[0], tiles, capacity)
    slot_picks = one_hot_rows(slots, tiles * capacity)
    order_picks = one_hot_rows(zorder[0], recv_rows).T
    payload = jnp.concatenate([lifted, grad_out[0]], axis=1)
    outgoing = move_rows(slot_picks, payload, False)
    incoming = lax.all_to_all(outgoing, ALL, split_axis=0, concat_axis=0, tiled=True)
    serial_both = move_rows(order_picks, incoming, False)
    taps_full = block_taps(conv_w)

    results, serial_grads, sums = patch_pass(
        serial_both[:, :width], serial_both[:, width:], gain_one, conv_w, taps_full, gain_two, w_up, w_down
    )
    back = jnp.concatenate(
        [results.reshape(recv_rows, width), serial_grads.reshape(recv_rows, width)], axis=1
    )
    back_slots = move_rows(order_picks, back, True)
    returned = lax.all_to_all(back_slots, ALL, split_axis=0, concat_axis=0, tiled=True)
    back_rows = move_rows(slot_picks, returned, True)
    out_rows = back_rows[:, :width]
    lifted_grad = back_rows[:, width:]
    patch_flat = jnp.concatenate(
        [sums[0], sums[2], sums[1].reshape(-1), sums[3].reshape(-1), sums[4].reshape(-1)]
    )
    near_grad, row_grad, halo_grad = tile_backward(
        lifted_grad, average, linear_part, counts_t, w_near, count_near
    )
    came_back = (
        pass_columns(halo_grad[0:border_rows], 1),
        pass_columns(halo_grad[border_rows : 2 * border_rows], -1),
        pass_lines(halo_grad[2 * border_rows : 3 * border_rows], 1),
        pass_lines(halo_grad[3 * border_rows : 4 * border_rows], -1),
    )
    for direction in range(4):
        row_grad = row_grad.at[lists[direction]].add(came_back[direction].astype(jnp.float32))
    grads_total = pair_sum(jnp.concatenate([near_grad.reshape(-1), patch_flat]), ("tx", "tyc"))
    near_sum = grads_total[: near_grad.size].reshape(near_grad.shape)
    patch_total = grads_total[near_grad.size :]
    sizes = [width, width, conv_w.size, w_up.size, w_down.size]
    shapes = [(width,), (width,), conv_w.shape, w_up.shape, w_down.shape]
    offsets = [sum(sizes[:index]) for index in range(len(sizes))]
    gain_one_sum, gain_two_sum, conv_sum, up_sum, down_sum = [
        patch_total[start : start + size].reshape(shape)
        for start, size, shape in zip(offsets, sizes, shapes)
    ]
    totals = (gain_one_sum, conv_sum, gain_two_sum, up_sum, down_sum)
    scale = 1.0 / math.sqrt(tiles * tile_rows)
    return (
        out_rows[None],
        row_grad.astype(jnp.bfloat16)[None],
        near_sum * scale,
        totals[0] * scale,
        totals[1] * scale,
        totals[2] * scale,
        totals[3] * scale,
        totals[4] * scale,
    )


def solution(mesh):
    placed = (
        P(ALL, None, None),
        P(ALL),
        P(ALL, None),
        P(ALL, None),
        P(ALL, None, None),
        P(ALL, None, None),
        P(),
        P(),
        P(),
        P(),
        P(),
        P(),
        P(ALL, None, None),
    )
    return jax.shard_map(
        body,
        mesh=Mesh(mesh.devices.reshape(mesh.shape["tx"], -1, 2), ALL),
        in_specs=placed,
        out_specs=(
            P(ALL, None, None),
            P(ALL, None, None),
            P(),
            P(),
            P(),
            P(),
            P(),
            P(),
        ),
        check_vma=False,
    )
```

```python
import functools
import math

import jax
import jax.numpy as jnp
from jax import lax
from jax.experimental import pallas as pl
from jax.experimental.pallas import tpu as pltpu
from jax.sharding import Mesh, PartitionSpec as P

PATCH = 1024
LINES = ("tyc", "core")
ALL = ("tx",) + LINES


eps_norm = 1e-06
gelu_coef = 0.7978845608028654
cubic_coef = 0.044715


def shifted(value, axis, steps):
    count = lax.axis_size(axis)
    initial, last = (max(0, -steps), min(count, count - steps))
    return lax.ppermute(value, axis, [(source, source + steps) for source in range(initial, last)])


def gelu_tanh(value):
    inner = gelu_coef * (value + cubic_coef * value * value * value)
    return 0.5 * value * (1.0 + jnp.tanh(inner))


def gelu_slope(value):
    inner = gelu_coef * (value + cubic_coef * value * value * value)
    tangent = jnp.tanh(inner)
    return 0.5 * (1.0 + tangent) + 0.5 * value * (1.0 - tangent * tangent) * gelu_coef * (
        1.0 + 3.0 * cubic_coef * value * value
    )


def inverse_rms(value):
    return lax.rsqrt(jnp.mean(value * value, axis=-1, keepdims=True) + eps_norm)


def near_counts(near_tile, ext_count):
    rows = lax.broadcasted_iota(jnp.int32, (ext_count, near_tile.shape[1]), 0)
    total = jnp.zeros((ext_count, near_tile.shape[1]), jnp.float32)
    for index in range(near_tile.shape[0]):
        total = total + (near_tile[index][None, :] == rows).astype(jnp.float32)
    return total.astype(jnp.bfloat16)


def tile_forward(points_tile, halo_rows, counts_t, w_near, count_near):
    extended = jnp.concatenate([points_tile, halo_rows], axis=0)
    total = lax.dot_general(
        counts_t, extended, (((0,), (0,)), ((), ())), preferred_element_type=jnp.float32
    )
    average = (total * (1.0 / count_near)).astype(jnp.bfloat16)
    linear_part = jnp.dot(average, w_near, preferred_element_type=jnp.float32)
    lifted = (points_tile.astype(jnp.float32) + gelu_tanh(linear_part)).astype(jnp.bfloat16)
    return (average, linear_part, lifted)


def tile_backward(lifted_grad, average, linear_part, counts_t, w_near, count_near):
    tile_rows = lifted_grad.shape[0]
    act_grad = (lifted_grad.astype(jnp.float32) * gelu_slope(linear_part)).astype(jnp.bfloat16)
    near_grad = lax.dot_general(
        average, act_grad, (((0,), (0,)), ((), ())), preferred_element_type=jnp.float32
    )
    spread = lax.dot_general(
        act_grad, w_near, (((1,), (1,)), ((), ())), preferred_element_type=jnp.float32
    ) * (1.0 / count_near)
    spread_hi = spread.astype(jnp.bfloat16)
    spread_lo = (spread - spread_hi.astype(jnp.float32)).astype(jnp.bfloat16)
    ext_grad = jnp.dot(counts_t, spread_hi, preferred_element_type=jnp.float32) + jnp.dot(
        counts_t, spread_lo, preferred_element_type=jnp.float32
    )
    row_grad = lifted_grad.astype(jnp.float32) + ext_grad[:tile_rows]
    halo_grad = ext_grad[tile_rows:].astype(jnp.bfloat16)
    return (near_grad, row_grad, halo_grad)


def route_ranks(owner_tile, count, tiles):
    tile_rows = owner_tile.shape[0]
    index = jnp.arange(tile_rows, dtype=jnp.int32)
    live = index < count
    score = jnp.where(live, owner_tile * tile_rows + index, tiles * tile_rows + index)
    order = jnp.argsort(score, stable=True)
    members = (owner_tile[:, None] == jnp.arange(tiles, dtype=jnp.int32)[None, :]) & live[:, None]
    per_owner = jnp.sum(members.astype(jnp.int32), axis=0)
    starts = jnp.cumsum(per_owner) - per_owner
    sorted_owner = jnp.take(owner_tile, order)
    ranked = index - jnp.take(starts, sorted_owner)
    rank = jnp.zeros((tile_rows,), jnp.int32).at[order].set(ranked)
    return (rank, live)


def route_slots(owner_tile, count, tiles, capacity):
    tile_rows = owner_tile.shape[0]
    live = jnp.arange(tile_rows, dtype=jnp.int32) < count
    owner_ids = lax.broadcasted_iota(jnp.int32, (tile_rows, tiles), 1)
    members = ((owner_tile[:, None] == owner_ids) & live[:, None]).astype(jnp.bfloat16)
    before = (
        lax.broadcasted_iota(jnp.int32, (tile_rows, tile_rows), 1)
        < lax.broadcasted_iota(jnp.int32, (tile_rows, tile_rows), 0)
    ).astype(jnp.bfloat16)
    prefix = jnp.dot(before, members, preferred_element_type=jnp.float32)
    rank = jnp.sum(prefix * members.astype(jnp.float32), axis=1).astype(jnp.int32)
    return jnp.where(live, owner_tile * capacity + rank, tiles * capacity)


def one_hot_rows(ids, size):
    return (lax.broadcasted_iota(jnp.int32, (size, ids.shape[0]), 0) == ids[None, :]).astype(
        jnp.bfloat16
    )


def move_rows(picks, rows, transpose):
    dims = (((0,), (0,)), ((), ())) if transpose else (((1,), (0,)), ((), ()))
    return lax.dot_general(picks, rows, dims, preferred_element_type=jnp.float32).astype(rows.dtype)


def shift_down(rows):
    patches = rows.reshape(-1, PATCH, rows.shape[-1])
    moved = jnp.concatenate([jnp.zeros_like(patches[:, :1]), patches[:, :-1]], axis=1)
    return moved.reshape(rows.shape)


def shift_up(rows):
    patches = rows.reshape(-1, PATCH, rows.shape[-1])
    moved = jnp.concatenate([patches[:, 1:], jnp.zeros_like(patches[:, :1])], axis=1)
    return moved.reshape(rows.shape)


def block_taps(conv_w):
    groups, inner = (conv_w.shape[1], conv_w.shape[2])
    identity_blocks = jnp.eye(groups, dtype=conv_w.dtype)
    full = jnp.einsum("gh,ogab->ogahb", identity_blocks, conv_w)
    return full.reshape(conv_w.shape[0], groups * inner, groups * inner)


def grouped_weight(inputs, outputs, groups, inner):
    length = inputs.shape[0]
    left = inputs.reshape(length, groups, inner)
    right = outputs.reshape(length, groups, inner)
    return jnp.einsum("pga,pgb->gab", left, right, preferred_element_type=jnp.float32)


def tap_back(rows, tap):
    return lax.dot_general(rows, tap, (((1,), (1,)), ((), ())), preferred_element_type=jnp.float32)


def mlp_kernel(
    second_ref, grad_ref, state_ref, up_ref, down_ref, result_ref, sgrad_ref, upg_ref, downg_ref
):
    @pl.when(pl.program_id(0) == 0)
    def _():
        upg_ref[...] = jnp.zeros_like(upg_ref)
        downg_ref[...] = jnp.zeros_like(downg_ref)

    second = second_ref[...]
    out_grad = grad_ref[...]
    hidden_pre = jnp.dot(second, up_ref[...], preferred_element_type=jnp.float32)
    inner = gelu_coef * (hidden_pre + cubic_coef * hidden_pre * hidden_pre * hidden_pre)
    tangent = jnp.tanh(inner)
    hidden = (0.5 * hidden_pre * (1.0 + tangent)).astype(jnp.bfloat16)
    result_ref[...] = (
        state_ref[...] + jnp.dot(hidden, down_ref[...], preferred_element_type=jnp.float32)
    ).astype(jnp.bfloat16)
    downg_ref[...] += lax.dot_general(
        hidden, out_grad, (((0,), (0,)), ((), ())), preferred_element_type=jnp.float32
    )
    hidden_grad = lax.dot_general(
        out_grad, down_ref[...], (((1,), (1,)), ((), ())), preferred_element_type=jnp.float32
    ).astype(jnp.bfloat16)
    slope = 0.5 * (1.0 + tangent) + 0.5 * hidden_pre * (1.0 - tangent * tangent) * gelu_coef * (
        1.0 + 3.0 * cubic_coef * hidden_pre * hidden_pre
    )
    pre_grad = (hidden_grad.astype(jnp.float32) * slope).astype(jnp.bfloat16)
    upg_ref[...] += lax.dot_general(
        second, pre_grad, (((0,), (0,)), ((), ())), preferred_element_type=jnp.float32
    )
    sgrad_ref[...] = lax.dot_general(
        pre_grad, up_ref[...], (((1,), (1,)), ((), ())), preferred_element_type=jnp.float32
    ).astype(jnp.bfloat16)


def mlp_pass(second, out_grad, state, w_up, w_down, block_rows=512):
    rows, width = second.shape
    ffn = w_up.shape[1]
    row_block = pl.BlockSpec((block_rows, width), lambda step: (step, 0))
    whole = lambda shape: pl.BlockSpec(shape, lambda step: (0, 0))
    flops = 2 * rows * width * ffn * 6
    return pl.pallas_call(
        mlp_kernel,
        grid=(rows // block_rows,),
        in_specs=[row_block, row_block, row_block, whole((width, ffn)), whole((ffn, width))],
        out_specs=[row_block, row_block, whole((width, ffn)), whole((ffn, width))],
        out_shape=[
            jax.ShapeDtypeStruct((rows, width), jnp.bfloat16),
            jax.ShapeDtypeStruct((rows, width), jnp.bfloat16),
            jax.ShapeDtypeStruct((width, ffn), jnp.float32),
            jax.ShapeDtypeStruct((ffn, width), jnp.float32),
        ],
        compiler_params=pltpu.CompilerParams(dimension_semantics=("arbitrary",)),
        cost_estimate=pl.CostEstimate(
            flops=flops, transcendentals=rows * ffn, bytes_accessed=rows * width * 10 + 4 * width * ffn * 3
        ),
    )(second, out_grad, state, w_up, w_down)


def patch_pass(serial, out_grad, gain_one, conv_w, taps_full, gain_two, w_up, w_down):
    groups, inner = (conv_w.shape[1], conv_w.shape[2])
    serial_f = serial.astype(jnp.float32)
    scale_one = inverse_rms(serial_f)
    normed = (serial_f * scale_one * gain_one).astype(jnp.bfloat16)
    taps = (shift_down(normed), normed, shift_up(normed))
    mixed = (
        jnp.dot(taps[0], taps_full[0], preferred_element_type=jnp.float32)
        + jnp.dot(taps[1], taps_full[1], preferred_element_type=jnp.float32)
        + jnp.dot(taps[2], taps_full[2], preferred_element_type=jnp.float32)
    )
    state = serial_f + mixed
    scale_two = inverse_rms(state)
    second = (state * scale_two * gain_two).astype(jnp.bfloat16)
    result, second_grad, up_grad, down_grad = mlp_pass(second, out_grad, state, w_up, w_down)
    unit_two = state * scale_two
    weighted_two = second_grad.astype(jnp.float32) * gain_two
    gain_two_grad = jnp.sum(second_grad.astype(jnp.float32) * unit_two, axis=0)
    state_grad = out_grad.astype(jnp.float32) + scale_two * (
        weighted_two - unit_two * jnp.mean(weighted_two * unit_two, axis=-1, keepdims=True)
    )
    mixed_grad = state_grad.astype(jnp.bfloat16)
    conv_grad = jnp.stack(
        [
            grouped_weight(taps[0], mixed_grad, groups, inner),
            grouped_weight(taps[1], mixed_grad, groups, inner),
            grouped_weight(taps[2], mixed_grad, groups, inner),
        ],
        axis=0,
    )
    normed_grad = (
        shift_up(tap_back(mixed_grad, taps_full[0]))
        + tap_back(mixed_grad, taps_full[1])
        + shift_down(tap_back(mixed_grad, taps_full[2]))
    ).astype(jnp.bfloat16)
    unit_one = serial_f * scale_one
    weighted_one = normed_grad.astype(jnp.float32) * gain_one
    gain_one_grad = jnp.sum(normed_grad.astype(jnp.float32) * unit_one, axis=0)
    serial_grad = (
        state_grad
        + scale_one
        * (weighted_one - unit_one * jnp.mean(weighted_one * unit_one, axis=-1, keepdims=True))
    ).astype(jnp.bfloat16)
    return (result, serial_grad, (gain_one_grad, conv_grad, gain_two_grad, up_grad, down_grad))


def all_sum(flat, axes):
    devices = lax.axis_size(axes)
    chunk = -(-flat.shape[0] // (devices * 128)) * 128
    padded = jnp.pad(flat, (0, devices * chunk - flat.shape[0])).reshape(devices, chunk)
    pieces = lax.all_to_all(padded, axes, split_axis=0, concat_axis=0, tiled=True)
    part = jnp.sum(pieces, axis=0)
    spread = jnp.broadcast_to(part[None], (devices, chunk))
    whole = lax.all_to_all(spread, axes, split_axis=0, concat_axis=0, tiled=True)
    return whole.reshape(-1)[: flat.shape[0]]


MESH_ID = pl.DeviceIdType.MESH


def exchange_kernel(sizes, x_ref, out_ref, send_sem, recv_sem, local_sem):
    cols, pairs, cores = sizes
    devices = cols * pairs * cores
    rows = x_ref.shape[0] // devices
    me = (lax.axis_index("tx") * pairs + lax.axis_index("tyc")) * cores + lax.axis_index("core")

    def device(index):
        return (index // (pairs * cores), (index // cores) % pairs, index % cores)

    barrier = pltpu.get_barrier_semaphore()

    def greet(step, carry):
        target = lax.rem(me + step, devices)
        pl.semaphore_signal(barrier, 1, device_id=device(target), device_id_type=MESH_ID)
        return carry

    lax.fori_loop(1, devices, greet, 0)
    pl.semaphore_wait(barrier, devices - 1)
    local = pltpu.make_async_copy(
        x_ref.at[pl.ds(me * rows, rows)], out_ref.at[pl.ds(me * rows, rows)], local_sem
    )
    local.start()

    def send(step, carry):
        target = lax.rem(me + step, devices)
        pltpu.make_async_remote_copy(
            src_ref=x_ref.at[pl.ds(target * rows, rows)],
            dst_ref=out_ref.at[pl.ds(me * rows, rows)],
            send_sem=send_sem,
            recv_sem=recv_sem,
            device_id=device(target),
            device_id_type=MESH_ID,
        ).start()
        return carry

    lax.fori_loop(1, devices, send, 0)
    span = (devices - 1) * rows
    pltpu.make_async_copy(x_ref.at[pl.ds(0, span)], out_ref.at[pl.ds(0, span)], send_sem).wait()
    pltpu.make_async_copy(x_ref.at[pl.ds(0, span)], out_ref.at[pl.ds(0, span)], recv_sem).wait()
    local.wait()


def exchange(x, sizes, tag):
    return pl.pallas_call(
        functools.partial(exchange_kernel, sizes),
        out_shape=jax.ShapeDtypeStruct(x.shape, x.dtype),
        in_specs=[pl.BlockSpec(memory_space=pl.ANY)],
        out_specs=pl.BlockSpec(memory_space=pl.ANY),
        scratch_shapes=[pltpu.SemaphoreType.DMA, pltpu.SemaphoreType.DMA, pltpu.SemaphoreType.DMA],
        compiler_params=pltpu.CompilerParams(collective_id=tag, has_side_effects=True),
    )(x)


def pair_sum(flat, group):
    devices = lax.axis_size(group)
    chunk = -(-flat.shape[0] // (2 * devices * 128)) * 128
    halves = jnp.pad(flat, (0, 2 * devices * chunk - flat.shape[0])).reshape(2, devices * chunk)
    core = lax.axis_index("core")
    swap = [(0, 1), (1, 0)]
    mine = jnp.where(core == 0, halves[0], halves[1])
    theirs = jnp.where(core == 0, halves[1], halves[0])
    half_sum = mine + lax.ppermute(theirs, "core", swap)
    total = all_sum(half_sum, group)
    other = lax.ppermute(total, "core", swap)
    whole = jnp.where(core == 0, jnp.concatenate([total, other]), jnp.concatenate([other, total]))
    return whole[: flat.shape[0]]


def pass_columns(rows, shift_by):
    return shifted(rows, "tx", shift_by)


def pass_lines(rows, shift_by):
    return shifted(rows, LINES, shift_by)


def body(
    points,
    counts,
    owner,
    zorder,
    border,
    near,
    w_near,
    gain_one,
    conv_w,
    gain_two,
    w_up,
    w_down,
    grad_out,
):
    points_tile = points[0]
    tile_rows, width = points_tile.shape
    lists = border[0]
    border_rows = lists.shape[1]
    cols_count = lax.axis_size("tx")
    lines_count = lax.axis_size(LINES)
    tiles = cols_count * lines_count
    recv_rows = zorder.shape[1]
    capacity = recv_rows // tiles
    near_tile = near[0]
    owner_tile = owner[0]
    sent = jnp.take(points_tile, lists.reshape(-1), axis=0).reshape(4, border_rows, width)
    halo = jnp.concatenate(
        [
            pass_columns(sent[0], -1),
            pass_columns(sent[1], 1),
            pass_lines(sent[2], -1),
            pass_lines(sent[3], 1),
        ],
        axis=0,
    )
    count_near = near_tile.shape[0]
    counts_t = near_counts(near_tile, tile_rows + 4 * border_rows)
    average, linear_part, lifted = tile_forward(points_tile, halo, counts_t, w_near, count_near)
    slots = route_slots(owner_tile, counts[0], tiles, capacity)
    slot_picks = one_hot_rows(slots, tiles * capacity)
    order_picks = one_hot_rows(zorder[0], recv_rows).T
    payload = jnp.concatenate([lifted, grad_out[0]], axis=1)
    outgoing = move_rows(slot_picks, payload, False)
    sizes = tuple(lax.axis_size(name) for name in ALL)
    incoming = exchange(outgoing, sizes, 0)
    serial_both = move_rows(order_picks, incoming, False)
    taps_full = block_taps(conv_w)

    results, serial_grads, sums = patch_pass(
        serial_both[:, :width], serial_both[:, width:], gain_one, conv_w, taps_full, gain_two, w_up, w_down
    )
    back = jnp.concatenate(
        [results.reshape(recv_rows, width), serial_grads.reshape(recv_rows, width)], axis=1
    )
    back_slots = move_rows(order_picks, back, True)
    returned = exchange(back_slots, sizes, 1)
    back_rows = move_rows(slot_picks, returned, True)
    out_rows = back_rows[:, :width]
    lifted_grad = back_rows[:, width:]
    patch_flat = jnp.concatenate(
        [sums[0], sums[2], sums[1].reshape(-1), sums[3].reshape(-1), sums[4].reshape(-1)]
    )
    near_grad, row_grad, halo_grad = tile_backward(
        lifted_grad, average, linear_part, counts_t, w_near, count_near
    )
    came_back = (
        pass_columns(halo_grad[0:border_rows], 1),
        pass_columns(halo_grad[border_rows : 2 * border_rows], -1),
        pass_lines(halo_grad[2 * border_rows : 3 * border_rows], 1),
        pass_lines(halo_grad[3 * border_rows : 4 * border_rows], -1),
    )
    for direction in range(4):
        row_grad = row_grad.at[lists[direction]].add(came_back[direction].astype(jnp.float32))
    grads_total = pair_sum(jnp.concatenate([near_grad.reshape(-1), patch_flat]), ("tx", "tyc"))
    near_sum = grads_total[: near_grad.size].reshape(near_grad.shape)
    patch_total = grads_total[near_grad.size :]
    sizes = [width, width, conv_w.size, w_up.size, w_down.size]
    shapes = [(width,), (width,), conv_w.shape, w_up.shape, w_down.shape]
    offsets = [sum(sizes[:index]) for index in range(len(sizes))]
    gain_one_sum, gain_two_sum, conv_sum, up_sum, down_sum = [
        patch_total[start : start + size].reshape(shape)
        for start, size, shape in zip(offsets, sizes, shapes)
    ]
    totals = (gain_one_sum, conv_sum, gain_two_sum, up_sum, down_sum)
    scale = 1.0 / math.sqrt(tiles * tile_rows)
    return (
        out_rows[None],
        row_grad.astype(jnp.bfloat16)[None],
        near_sum * scale,
        totals[0] * scale,
        totals[1] * scale,
        totals[2] * scale,
        totals[3] * scale,
        totals[4] * scale,
    )


def solution(mesh):
    placed = (
        P(ALL, None, None),
        P(ALL),
        P(ALL, None),
        P(ALL, None),
        P(ALL, None, None),
        P(ALL, None, None),
        P(),
        P(),
        P(),
        P(),
        P(),
        P(),
        P(ALL, None, None),
    )
    return jax.shard_map(
        body,
        mesh=Mesh(mesh.devices.reshape(mesh.shape["tx"], -1, 2), ALL),
        in_specs=placed,
        out_specs=(
            P(ALL, None, None),
            P(ALL, None, None),
            P(),
            P(),
            P(),
            P(),
            P(),
            P(),
        ),
        check_vma=False,
    )
```

```python
import math

import jax
import jax.numpy as jnp
from jax import lax
from jax.experimental import pallas as pl
from jax.experimental.pallas import tpu as pltpu
from jax.sharding import Mesh, PartitionSpec as P

PATCH = 1024
LINES = ("tyc", "core")
ALL = ("tx",) + LINES


eps_norm = 1e-06
gelu_coef = 0.7978845608028654
cubic_coef = 0.044715


def shifted(value, axis, steps):
    count = lax.axis_size(axis)
    initial, last = (max(0, -steps), min(count, count - steps))
    return lax.ppermute(value, axis, [(source, source + steps) for source in range(initial, last)])


def gelu_tanh(value):
    inner = gelu_coef * (value + cubic_coef * value * value * value)
    return 0.5 * value * (1.0 + jnp.tanh(inner))


def gelu_slope(value):
    inner = gelu_coef * (value + cubic_coef * value * value * value)
    tangent = jnp.tanh(inner)
    return 0.5 * (1.0 + tangent) + 0.5 * value * (1.0 - tangent * tangent) * gelu_coef * (
        1.0 + 3.0 * cubic_coef * value * value
    )


def inverse_rms(value):
    return lax.rsqrt(jnp.mean(value * value, axis=-1, keepdims=True) + eps_norm)


def near_counts(near_tile, ext_count):
    rows = lax.broadcasted_iota(jnp.int32, (ext_count, near_tile.shape[1]), 0)
    total = jnp.zeros((ext_count, near_tile.shape[1]), jnp.float32)
    for index in range(near_tile.shape[0]):
        total = total + (near_tile[index][None, :] == rows).astype(jnp.float32)
    return total.astype(jnp.bfloat16)


def tile_forward(points_tile, halo_rows, counts_t, w_near, count_near):
    extended = jnp.concatenate([points_tile, halo_rows], axis=0)
    total = lax.dot_general(
        counts_t, extended, (((0,), (0,)), ((), ())), preferred_element_type=jnp.float32
    )
    average = (total * (1.0 / count_near)).astype(jnp.bfloat16)
    linear_part = jnp.dot(average, w_near, preferred_element_type=jnp.float32)
    lifted = (points_tile.astype(jnp.float32) + gelu_tanh(linear_part)).astype(jnp.bfloat16)
    return (average, linear_part, lifted)


def tile_backward(lifted_grad, average, linear_part, counts_t, w_near, count_near):
    tile_rows = lifted_grad.shape[0]
    act_grad = (lifted_grad.astype(jnp.float32) * gelu_slope(linear_part)).astype(jnp.bfloat16)
    near_grad = lax.dot_general(
        average, act_grad, (((0,), (0,)), ((), ())), preferred_element_type=jnp.float32
    )
    spread = lax.dot_general(
        act_grad, w_near, (((1,), (1,)), ((), ())), preferred_element_type=jnp.float32
    ) * (1.0 / count_near)
    spread_hi = spread.astype(jnp.bfloat16)
    spread_lo = (spread - spread_hi.astype(jnp.float32)).astype(jnp.bfloat16)
    ext_grad = jnp.dot(counts_t, spread_hi, preferred_element_type=jnp.float32) + jnp.dot(
        counts_t, spread_lo, preferred_element_type=jnp.float32
    )
    row_grad = lifted_grad.astype(jnp.float32) + ext_grad[:tile_rows]
    halo_grad = ext_grad[tile_rows:].astype(jnp.bfloat16)
    return (near_grad, row_grad, halo_grad)


def route_ranks(owner_tile, count, tiles):
    tile_rows = owner_tile.shape[0]
    index = jnp.arange(tile_rows, dtype=jnp.int32)
    live = index < count
    score = jnp.where(live, owner_tile * tile_rows + index, tiles * tile_rows + index)
    order = jnp.argsort(score, stable=True)
    members = (owner_tile[:, None] == jnp.arange(tiles, dtype=jnp.int32)[None, :]) & live[:, None]
    per_owner = jnp.sum(members.astype(jnp.int32), axis=0)
    starts = jnp.cumsum(per_owner) - per_owner
    sorted_owner = jnp.take(owner_tile, order)
    ranked = index - jnp.take(starts, sorted_owner)
    rank = jnp.zeros((tile_rows,), jnp.int32).at[order].set(ranked)
    return (rank, live)


def route_slots(owner_tile, count, tiles, capacity):
    tile_rows = owner_tile.shape[0]
    live = jnp.arange(tile_rows, dtype=jnp.int32) < count
    owner_ids = lax.broadcasted_iota(jnp.int32, (tile_rows, tiles), 1)
    members = ((owner_tile[:, None] == owner_ids) & live[:, None]).astype(jnp.bfloat16)
    before = (
        lax.broadcasted_iota(jnp.int32, (tile_rows, tile_rows), 1)
        < lax.broadcasted_iota(jnp.int32, (tile_rows, tile_rows), 0)
    ).astype(jnp.bfloat16)
    prefix = jnp.dot(before, members, preferred_element_type=jnp.float32)
    rank = jnp.sum(prefix * members.astype(jnp.float32), axis=1).astype(jnp.int32)
    return jnp.where(live, owner_tile * capacity + rank, tiles * capacity)


def one_hot_rows(ids, size):
    return (lax.broadcasted_iota(jnp.int32, (size, ids.shape[0]), 0) == ids[None, :]).astype(
        jnp.bfloat16
    )


def move_rows(picks, rows, transpose):
    dims = (((0,), (0,)), ((), ())) if transpose else (((1,), (0,)), ((), ()))
    return lax.dot_general(picks, rows, dims, preferred_element_type=jnp.float32).astype(rows.dtype)


def shift_down(rows):
    patches = rows.reshape(-1, PATCH, rows.shape[-1])
    moved = jnp.concatenate([jnp.zeros_like(patches[:, :1]), patches[:, :-1]], axis=1)
    return moved.reshape(rows.shape)


def shift_up(rows):
    patches = rows.reshape(-1, PATCH, rows.shape[-1])
    moved = jnp.concatenate([patches[:, 1:], jnp.zeros_like(patches[:, :1])], axis=1)
    return moved.reshape(rows.shape)


def block_taps(conv_w):
    groups, inner = (conv_w.shape[1], conv_w.shape[2])
    identity_blocks = jnp.eye(groups, dtype=conv_w.dtype)
    full = jnp.einsum("gh,ogab->ogahb", identity_blocks, conv_w)
    return full.reshape(conv_w.shape[0], groups * inner, groups * inner)


def grouped_weight(inputs, outputs, groups, inner):
    length = inputs.shape[0]
    left = inputs.reshape(length, groups, inner)
    right = outputs.reshape(length, groups, inner)
    return jnp.einsum("pga,pgb->gab", left, right, preferred_element_type=jnp.float32)


def tap_back(rows, tap):
    return lax.dot_general(rows, tap, (((1,), (1,)), ((), ())), preferred_element_type=jnp.float32)


def mlp_kernel(
    second_ref, grad_ref, state_ref, up_ref, down_ref, result_ref, sgrad_ref, upg_ref, downg_ref
):
    @pl.when(pl.program_id(0) == 0)
    def _():
        upg_ref[...] = jnp.zeros_like(upg_ref)
        downg_ref[...] = jnp.zeros_like(downg_ref)

    second = second_ref[...]
    out_grad = grad_ref[...]
    hidden_pre = jnp.dot(second, up_ref[...], preferred_element_type=jnp.float32)
    inner = gelu_coef * (hidden_pre + cubic_coef * hidden_pre * hidden_pre * hidden_pre)
    tangent = jnp.tanh(inner)
    hidden = (0.5 * hidden_pre * (1.0 + tangent)).astype(jnp.bfloat16)
    result_ref[...] = (
        state_ref[...] + jnp.dot(hidden, down_ref[...], preferred_element_type=jnp.float32)
    ).astype(jnp.bfloat16)
    downg_ref[...] += lax.dot_general(
        hidden, out_grad, (((0,), (0,)), ((), ())), preferred_element_type=jnp.float32
    )
    hidden_grad = lax.dot_general(
        out_grad, down_ref[...], (((1,), (1,)), ((), ())), preferred_element_type=jnp.float32
    ).astype(jnp.bfloat16)
    slope = 0.5 * (1.0 + tangent) + 0.5 * hidden_pre * (1.0 - tangent * tangent) * gelu_coef * (
        1.0 + 3.0 * cubic_coef * hidden_pre * hidden_pre
    )
    pre_grad = (hidden_grad.astype(jnp.float32) * slope).astype(jnp.bfloat16)
    upg_ref[...] += lax.dot_general(
        second, pre_grad, (((0,), (0,)), ((), ())), preferred_element_type=jnp.float32
    )
    sgrad_ref[...] = lax.dot_general(
        pre_grad, up_ref[...], (((1,), (1,)), ((), ())), preferred_element_type=jnp.float32
    ).astype(jnp.bfloat16)


def mlp_pass(second, out_grad, state, w_up, w_down, block_rows=512):
    rows, width = second.shape
    ffn = w_up.shape[1]
    row_block = pl.BlockSpec((block_rows, width), lambda step: (step, 0))
    whole = lambda shape: pl.BlockSpec(shape, lambda step: (0, 0))
    flops = 2 * rows * width * ffn * 6
    return pl.pallas_call(
        mlp_kernel,
        grid=(rows // block_rows,),
        in_specs=[row_block, row_block, row_block, whole((width, ffn)), whole((ffn, width))],
        out_specs=[row_block, row_block, whole((width, ffn)), whole((ffn, width))],
        out_shape=[
            jax.ShapeDtypeStruct((rows, width), jnp.bfloat16),
            jax.ShapeDtypeStruct((rows, width), jnp.bfloat16),
            jax.ShapeDtypeStruct((width, ffn), jnp.float32),
            jax.ShapeDtypeStruct((ffn, width), jnp.float32),
        ],
        compiler_params=pltpu.CompilerParams(dimension_semantics=("arbitrary",)),
        cost_estimate=pl.CostEstimate(
            flops=flops, transcendentals=rows * ffn, bytes_accessed=rows * width * 10 + 4 * width * ffn * 3
        ),
    )(second, out_grad, state, w_up, w_down)


def patch_pass(serial, out_grad, gain_one, conv_w, taps_full, gain_two, w_up, w_down):
    groups, inner = (conv_w.shape[1], conv_w.shape[2])
    serial_f = serial.astype(jnp.float32)
    scale_one = inverse_rms(serial_f)
    normed = (serial_f * scale_one * gain_one).astype(jnp.bfloat16)
    taps = (shift_down(normed), normed, shift_up(normed))
    mixed = (
        jnp.dot(taps[0], taps_full[0], preferred_element_type=jnp.float32)
        + jnp.dot(taps[1], taps_full[1], preferred_element_type=jnp.float32)
        + jnp.dot(taps[2], taps_full[2], preferred_element_type=jnp.float32)
    )
    state = serial_f + mixed
    scale_two = inverse_rms(state)
    second = (state * scale_two * gain_two).astype(jnp.bfloat16)
    result, second_grad, up_grad, down_grad = mlp_pass(second, out_grad, state, w_up, w_down)
    unit_two = state * scale_two
    weighted_two = second_grad.astype(jnp.float32) * gain_two
    gain_two_grad = jnp.sum(second_grad.astype(jnp.float32) * unit_two, axis=0)
    state_grad = out_grad.astype(jnp.float32) + scale_two * (
        weighted_two - unit_two * jnp.mean(weighted_two * unit_two, axis=-1, keepdims=True)
    )
    mixed_grad = state_grad.astype(jnp.bfloat16)
    conv_grad = jnp.stack(
        [
            grouped_weight(taps[0], mixed_grad, groups, inner),
            grouped_weight(taps[1], mixed_grad, groups, inner),
            grouped_weight(taps[2], mixed_grad, groups, inner),
        ],
        axis=0,
    )
    normed_grad = (
        shift_up(tap_back(mixed_grad, taps_full[0]))
        + tap_back(mixed_grad, taps_full[1])
        + shift_down(tap_back(mixed_grad, taps_full[2]))
    ).astype(jnp.bfloat16)
    unit_one = serial_f * scale_one
    weighted_one = normed_grad.astype(jnp.float32) * gain_one
    gain_one_grad = jnp.sum(normed_grad.astype(jnp.float32) * unit_one, axis=0)
    serial_grad = (
        state_grad
        + scale_one
        * (weighted_one - unit_one * jnp.mean(weighted_one * unit_one, axis=-1, keepdims=True))
    ).astype(jnp.bfloat16)
    return (result, serial_grad, (gain_one_grad, conv_grad, gain_two_grad, up_grad, down_grad))


def all_sum(flat, axes):
    devices = lax.axis_size(axes)
    chunk = -(-flat.shape[0] // (devices * 1024)) * 1024
    padded = jnp.pad(flat, (0, devices * chunk - flat.shape[0])).reshape(devices, chunk // 128, 128)
    pieces = lax.all_to_all(padded, axes, split_axis=0, concat_axis=0, tiled=True)
    part = jnp.sum(pieces, axis=0)
    spread = jnp.broadcast_to(part[None], (devices,) + part.shape)
    whole = lax.all_to_all(spread, axes, split_axis=0, concat_axis=0, tiled=True)
    return whole.reshape(-1)[: flat.shape[0]]


def pair_sum(flat, group):
    devices = lax.axis_size(group)
    chunk = -(-flat.shape[0] // (2 * devices * 1024)) * 1024
    halves = jnp.pad(flat, (0, 2 * devices * chunk - flat.shape[0])).reshape(2, devices * chunk)
    core = lax.axis_index("core")
    swap = [(0, 1), (1, 0)]
    mine = jnp.where(core == 0, halves[0], halves[1])
    theirs = jnp.where(core == 0, halves[1], halves[0])
    half_sum = mine + lax.ppermute(theirs, "core", swap)
    total = all_sum(half_sum, group)
    other = lax.ppermute(total, "core", swap)
    whole = jnp.where(core == 0, jnp.concatenate([total, other]), jnp.concatenate([other, total]))
    return whole[: flat.shape[0]]


def pass_columns(rows, shift_by):
    return shifted(rows, "tx", shift_by)


def pass_lines(rows, shift_by):
    return shifted(rows, LINES, shift_by)


def body(
    points,
    counts,
    owner,
    zorder,
    border,
    near,
    w_near,
    gain_one,
    conv_w,
    gain_two,
    w_up,
    w_down,
    grad_out,
):
    points_tile = points[0]
    tile_rows, width = points_tile.shape
    lists = border[0]
    border_rows = lists.shape[1]
    cols_count = lax.axis_size("tx")
    lines_count = lax.axis_size(LINES)
    tiles = cols_count * lines_count
    recv_rows = zorder.shape[1]
    capacity = recv_rows // tiles
    near_tile = near[0]
    owner_tile = owner[0]
    sent = jnp.take(points_tile, lists.reshape(-1), axis=0).reshape(4, border_rows, width)
    halo = jnp.concatenate(
        [
            pass_columns(sent[0], -1),
            pass_columns(sent[1], 1),
            pass_lines(sent[2], -1),
            pass_lines(sent[3], 1),
        ],
        axis=0,
    )
    count_near = near_tile.shape[0]
    counts_t = near_counts(near_tile, tile_rows + 4 * border_rows)
    average, linear_part, lifted = tile_forward(points_tile, halo, counts_t, w_near, count_near)
    slots = route_slots(owner_tile, counts[0], tiles, capacity)
    slot_picks = one_hot_rows(slots, tiles * capacity)
    order_picks = one_hot_rows(zorder[0], recv_rows).T
    payload = jnp.concatenate([lifted, grad_out[0]], axis=1)
    outgoing = move_rows(slot_picks, payload, False)
    incoming = lax.all_to_all(outgoing, ALL, split_axis=0, concat_axis=0, tiled=True)
    serial_both = move_rows(order_picks, incoming, False)
    taps_full = block_taps(conv_w)

    results, serial_grads, sums = patch_pass(
        serial_both[:, :width], serial_both[:, width:], gain_one, conv_w, taps_full, gain_two, w_up, w_down
    )
    back = jnp.concatenate(
        [results.reshape(recv_rows, width), serial_grads.reshape(recv_rows, width)], axis=1
    )
    back_slots = move_rows(order_picks, back, True)
    returned = lax.all_to_all(back_slots, ALL, split_axis=0, concat_axis=0, tiled=True)
    back_rows = move_rows(slot_picks, returned, True)
    out_rows = back_rows[:, :width]
    lifted_grad = back_rows[:, width:]
    patch_flat = jnp.concatenate(
        [sums[0], sums[2], sums[1].reshape(-1), sums[3].reshape(-1), sums[4].reshape(-1)]
    )
    near_grad, row_grad, halo_grad = tile_backward(
        lifted_grad, average, linear_part, counts_t, w_near, count_near
    )
    came_back = (
        pass_columns(halo_grad[0:border_rows], 1),
        pass_columns(halo_grad[border_rows : 2 * border_rows], -1),
        pass_lines(halo_grad[2 * border_rows : 3 * border_rows], 1),
        pass_lines(halo_grad[3 * border_rows : 4 * border_rows], -1),
    )
    for direction in range(4):
        row_grad = row_grad.at[lists[direction]].add(came_back[direction].astype(jnp.float32))
    grads_total = pair_sum(jnp.concatenate([near_grad.reshape(-1), patch_flat]), ("tx", "tyc"))
    near_sum = grads_total[: near_grad.size].reshape(near_grad.shape)
    patch_total = grads_total[near_grad.size :]
    sizes = [width, width, conv_w.size, w_up.size, w_down.size]
    shapes = [(width,), (width,), conv_w.shape, w_up.shape, w_down.shape]
    offsets = [sum(sizes[:index]) for index in range(len(sizes))]
    gain_one_sum, gain_two_sum, conv_sum, up_sum, down_sum = [
        patch_total[start : start + size].reshape(shape)
        for start, size, shape in zip(offsets, sizes, shapes)
    ]
    totals = (gain_one_sum, conv_sum, gain_two_sum, up_sum, down_sum)
    scale = 1.0 / math.sqrt(tiles * tile_rows)
    return (
        out_rows[None],
        row_grad.astype(jnp.bfloat16)[None],
        near_sum * scale,
        totals[0] * scale,
        totals[1] * scale,
        totals[2] * scale,
        totals[3] * scale,
        totals[4] * scale,
    )


def solution(mesh):
    placed = (
        P(ALL, None, None),
        P(ALL),
        P(ALL, None),
        P(ALL, None),
        P(ALL, None, None),
        P(ALL, None, None),
        P(),
        P(),
        P(),
        P(),
        P(),
        P(),
        P(ALL, None, None),
    )
    return jax.shard_map(
        body,
        mesh=Mesh(mesh.devices.reshape(mesh.shape["tx"], -1, 2), ALL),
        in_specs=placed,
        out_specs=(
            P(ALL, None, None),
            P(ALL, None, None),
            P(),
            P(),
            P(),
            P(),
            P(),
            P(),
        ),
        check_vma=False,
    )
```

```python
import math

import jax
import jax.numpy as jnp
from jax import lax
from jax.experimental import pallas as pl
from jax.experimental.pallas import tpu as pltpu
from jax.sharding import Mesh, PartitionSpec as P

PATCH = 1024
LINES = ("tyc", "core")
ALL = ("tx",) + LINES


eps_norm = 1e-06
gelu_coef = 0.7978845608028654
cubic_coef = 0.044715


def shifted(value, axis, steps):
    count = lax.axis_size(axis)
    initial, last = (max(0, -steps), min(count, count - steps))
    return lax.ppermute(value, axis, [(source, source + steps) for source in range(initial, last)])


def gelu_tanh(value):
    inner = gelu_coef * (value + cubic_coef * value * value * value)
    return 0.5 * value * (1.0 + jnp.tanh(inner))


def gelu_slope(value):
    inner = gelu_coef * (value + cubic_coef * value * value * value)
    tangent = jnp.tanh(inner)
    return 0.5 * (1.0 + tangent) + 0.5 * value * (1.0 - tangent * tangent) * gelu_coef * (
        1.0 + 3.0 * cubic_coef * value * value
    )


def inverse_rms(value):
    return lax.rsqrt(jnp.mean(value * value, axis=-1, keepdims=True) + eps_norm)


def near_counts(near_tile, ext_count):
    rows = lax.broadcasted_iota(jnp.int32, (ext_count, near_tile.shape[1]), 0)
    total = jnp.zeros((ext_count, near_tile.shape[1]), jnp.float32)
    for index in range(near_tile.shape[0]):
        total = total + (near_tile[index][None, :] == rows).astype(jnp.float32)
    return total.astype(jnp.bfloat16)


def tile_forward(points_tile, halo_rows, counts_t, w_near, count_near):
    extended = jnp.concatenate([points_tile, halo_rows], axis=0)
    total = lax.dot_general(
        counts_t, extended, (((0,), (0,)), ((), ())), preferred_element_type=jnp.float32
    )
    average = (total * (1.0 / count_near)).astype(jnp.bfloat16)
    linear_part = jnp.dot(average, w_near, preferred_element_type=jnp.float32)
    lifted = (points_tile.astype(jnp.float32) + gelu_tanh(linear_part)).astype(jnp.bfloat16)
    return (average, linear_part, lifted)


def tile_backward(lifted_grad, average, linear_part, counts_t, w_near, count_near):
    tile_rows = lifted_grad.shape[0]
    act_grad = (lifted_grad.astype(jnp.float32) * gelu_slope(linear_part)).astype(jnp.bfloat16)
    near_grad = lax.dot_general(
        average, act_grad, (((0,), (0,)), ((), ())), preferred_element_type=jnp.float32
    )
    spread = lax.dot_general(
        act_grad, w_near, (((1,), (1,)), ((), ())), preferred_element_type=jnp.float32
    ) * (1.0 / count_near)
    spread_hi = spread.astype(jnp.bfloat16)
    spread_lo = (spread - spread_hi.astype(jnp.float32)).astype(jnp.bfloat16)
    ext_grad = jnp.dot(counts_t, spread_hi, preferred_element_type=jnp.float32) + jnp.dot(
        counts_t, spread_lo, preferred_element_type=jnp.float32
    )
    row_grad = lifted_grad.astype(jnp.float32) + ext_grad[:tile_rows]
    halo_grad = ext_grad[tile_rows:].astype(jnp.bfloat16)
    return (near_grad, row_grad, halo_grad)


def route_ranks(owner_tile, count, tiles):
    tile_rows = owner_tile.shape[0]
    index = jnp.arange(tile_rows, dtype=jnp.int32)
    live = index < count
    score = jnp.where(live, owner_tile * tile_rows + index, tiles * tile_rows + index)
    order = jnp.argsort(score, stable=True)
    members = (owner_tile[:, None] == jnp.arange(tiles, dtype=jnp.int32)[None, :]) & live[:, None]
    per_owner = jnp.sum(members.astype(jnp.int32), axis=0)
    starts = jnp.cumsum(per_owner) - per_owner
    sorted_owner = jnp.take(owner_tile, order)
    ranked = index - jnp.take(starts, sorted_owner)
    rank = jnp.zeros((tile_rows,), jnp.int32).at[order].set(ranked)
    return (rank, live)


def route_slots(owner_tile, count, tiles, capacity):
    tile_rows = owner_tile.shape[0]
    live = jnp.arange(tile_rows, dtype=jnp.int32) < count
    owner_ids = lax.broadcasted_iota(jnp.int32, (tile_rows, tiles), 1)
    members = ((owner_tile[:, None] == owner_ids) & live[:, None]).astype(jnp.bfloat16)
    before = (
        lax.broadcasted_iota(jnp.int32, (tile_rows, tile_rows), 1)
        < lax.broadcasted_iota(jnp.int32, (tile_rows, tile_rows), 0)
    ).astype(jnp.bfloat16)
    prefix = jnp.dot(before, members, preferred_element_type=jnp.float32)
    rank = jnp.sum(prefix * members.astype(jnp.float32), axis=1).astype(jnp.int32)
    return jnp.where(live, owner_tile * capacity + rank, tiles * capacity)


def one_hot_rows(ids, size):
    return (lax.broadcasted_iota(jnp.int32, (size, ids.shape[0]), 0) == ids[None, :]).astype(
        jnp.bfloat16
    )


def move_rows(picks, rows, transpose):
    dims = (((0,), (0,)), ((), ())) if transpose else (((1,), (0,)), ((), ()))
    return lax.dot_general(picks, rows, dims, preferred_element_type=jnp.float32).astype(rows.dtype)


def shift_down(rows):
    patches = rows.reshape(-1, PATCH, rows.shape[-1])
    moved = jnp.concatenate([jnp.zeros_like(patches[:, :1]), patches[:, :-1]], axis=1)
    return moved.reshape(rows.shape)


def shift_up(rows):
    patches = rows.reshape(-1, PATCH, rows.shape[-1])
    moved = jnp.concatenate([patches[:, 1:], jnp.zeros_like(patches[:, :1])], axis=1)
    return moved.reshape(rows.shape)


def block_taps(conv_w):
    groups, inner = (conv_w.shape[1], conv_w.shape[2])
    identity_blocks = jnp.eye(groups, dtype=conv_w.dtype)
    full = jnp.einsum("gh,ogab->ogahb", identity_blocks, conv_w)
    return full.reshape(conv_w.shape[0], groups * inner, groups * inner)


def grouped_weight(inputs, outputs, groups, inner):
    length = inputs.shape[0]
    left = inputs.reshape(length, groups, inner)
    right = outputs.reshape(length, groups, inner)
    return jnp.einsum("pga,pgb->gab", left, right, preferred_element_type=jnp.float32)


def tap_back(rows, tap):
    return lax.dot_general(rows, tap, (((1,), (1,)), ((), ())), preferred_element_type=jnp.float32)


def mlp_kernel(
    second_ref, grad_ref, state_ref, up_ref, down_ref, result_ref, sgrad_ref, upg_ref, downg_ref
):
    @pl.when(pl.program_id(0) == 0)
    def _():
        upg_ref[...] = jnp.zeros_like(upg_ref)
        downg_ref[...] = jnp.zeros_like(downg_ref)

    second = second_ref[...]
    out_grad = grad_ref[...]
    hidden_pre = jnp.dot(second, up_ref[...], preferred_element_type=jnp.float32)
    inner = gelu_coef * (hidden_pre + cubic_coef * hidden_pre * hidden_pre * hidden_pre)
    tangent = jnp.tanh(inner)
    hidden = (0.5 * hidden_pre * (1.0 + tangent)).astype(jnp.bfloat16)
    result_ref[...] = (
        state_ref[...] + jnp.dot(hidden, down_ref[...], preferred_element_type=jnp.float32)
    ).astype(jnp.bfloat16)
    downg_ref[...] += lax.dot_general(
        hidden, out_grad, (((0,), (0,)), ((), ())), preferred_element_type=jnp.float32
    )
    hidden_grad = lax.dot_general(
        out_grad, down_ref[...], (((1,), (1,)), ((), ())), preferred_element_type=jnp.float32
    ).astype(jnp.bfloat16)
    slope = 0.5 * (1.0 + tangent) + 0.5 * hidden_pre * (1.0 - tangent * tangent) * gelu_coef * (
        1.0 + 3.0 * cubic_coef * hidden_pre * hidden_pre
    )
    pre_grad = (hidden_grad.astype(jnp.float32) * slope).astype(jnp.bfloat16)
    upg_ref[...] += lax.dot_general(
        second, pre_grad, (((0,), (0,)), ((), ())), preferred_element_type=jnp.float32
    )
    sgrad_ref[...] = lax.dot_general(
        pre_grad, up_ref[...], (((1,), (1,)), ((), ())), preferred_element_type=jnp.float32
    ).astype(jnp.bfloat16)


def mlp_pass(second, out_grad, state, w_up, w_down, block_rows=512):
    rows, width = second.shape
    ffn = w_up.shape[1]
    row_block = pl.BlockSpec((block_rows, width), lambda step: (step, 0))
    whole = lambda shape: pl.BlockSpec(shape, lambda step: (0, 0))
    flops = 2 * rows * width * ffn * 6
    return pl.pallas_call(
        mlp_kernel,
        grid=(rows // block_rows,),
        in_specs=[row_block, row_block, row_block, whole((width, ffn)), whole((ffn, width))],
        out_specs=[row_block, row_block, whole((width, ffn)), whole((ffn, width))],
        out_shape=[
            jax.ShapeDtypeStruct((rows, width), jnp.bfloat16),
            jax.ShapeDtypeStruct((rows, width), jnp.bfloat16),
            jax.ShapeDtypeStruct((width, ffn), jnp.float32),
            jax.ShapeDtypeStruct((ffn, width), jnp.float32),
        ],
        compiler_params=pltpu.CompilerParams(dimension_semantics=("arbitrary",)),
        cost_estimate=pl.CostEstimate(
            flops=flops, transcendentals=rows * ffn, bytes_accessed=rows * width * 10 + 4 * width * ffn * 3
        ),
    )(second, out_grad, state, w_up, w_down)


def patch_pass(serial, out_grad, gain_one, conv_w, taps_full, gain_two, w_up, w_down):
    groups, inner = (conv_w.shape[1], conv_w.shape[2])
    serial_f = serial.astype(jnp.float32)
    scale_one = inverse_rms(serial_f)
    normed = (serial_f * scale_one * gain_one).astype(jnp.bfloat16)
    taps = (shift_down(normed), normed, shift_up(normed))
    mixed = (
        jnp.dot(taps[0], taps_full[0], preferred_element_type=jnp.float32)
        + jnp.dot(taps[1], taps_full[1], preferred_element_type=jnp.float32)
        + jnp.dot(taps[2], taps_full[2], preferred_element_type=jnp.float32)
    )
    state = serial_f + mixed
    scale_two = inverse_rms(state)
    second = (state * scale_two * gain_two).astype(jnp.bfloat16)
    result, second_grad, up_grad, down_grad = mlp_pass(second, out_grad, state, w_up, w_down)
    unit_two = state * scale_two
    weighted_two = second_grad.astype(jnp.float32) * gain_two
    gain_two_grad = jnp.sum(second_grad.astype(jnp.float32) * unit_two, axis=0)
    state_grad = out_grad.astype(jnp.float32) + scale_two * (
        weighted_two - unit_two * jnp.mean(weighted_two * unit_two, axis=-1, keepdims=True)
    )
    mixed_grad = state_grad.astype(jnp.bfloat16)
    conv_grad = jnp.stack(
        [
            grouped_weight(taps[0], mixed_grad, groups, inner),
            grouped_weight(taps[1], mixed_grad, groups, inner),
            grouped_weight(taps[2], mixed_grad, groups, inner),
        ],
        axis=0,
    )
    normed_grad = (
        shift_up(tap_back(mixed_grad, taps_full[0]))
        + tap_back(mixed_grad, taps_full[1])
        + shift_down(tap_back(mixed_grad, taps_full[2]))
    ).astype(jnp.bfloat16)
    unit_one = serial_f * scale_one
    weighted_one = normed_grad.astype(jnp.float32) * gain_one
    gain_one_grad = jnp.sum(normed_grad.astype(jnp.float32) * unit_one, axis=0)
    serial_grad = (
        state_grad
        + scale_one
        * (weighted_one - unit_one * jnp.mean(weighted_one * unit_one, axis=-1, keepdims=True))
    ).astype(jnp.bfloat16)
    return (result, serial_grad, (gain_one_grad, conv_grad, gain_two_grad, up_grad, down_grad))


def all_sum(flat, axes):
    devices = lax.axis_size(axes)
    chunk = -(-flat.shape[0] // (devices * 1024)) * 1024
    padded = jnp.pad(flat, (0, devices * chunk - flat.shape[0])).reshape(devices, chunk // 128, 128)
    pieces = lax.all_to_all(padded, axes, split_axis=0, concat_axis=0, tiled=True)
    part = jnp.sum(pieces, axis=0)
    spread = jnp.broadcast_to(part[None], (devices,) + part.shape)
    whole = lax.all_to_all(spread, axes, split_axis=0, concat_axis=0, tiled=True)
    return whole.reshape(-1)[: flat.shape[0]]


def pair_sum(flat, group):
    devices = lax.axis_size(group)
    chunk = -(-flat.shape[0] // (2 * devices * 1024)) * 1024
    halves = jnp.pad(flat, (0, 2 * devices * chunk - flat.shape[0])).reshape(2, devices * chunk)
    core = lax.axis_index("core")
    swap = [(0, 1), (1, 0)]
    mine = jnp.where(core == 0, halves[0], halves[1])
    theirs = jnp.where(core == 0, halves[1], halves[0])
    half_sum = mine + lax.ppermute(theirs, "core", swap)
    total = all_sum(half_sum, group)
    other = lax.ppermute(total, "core", swap)
    first = jnp.where(core == 0, total, other)
    second = jnp.where(core == 0, other, total)
    return jnp.concatenate([first, second])[: flat.shape[0]]


def pass_columns(rows, shift_by):
    return shifted(rows, "tx", shift_by)


def pass_lines(rows, shift_by):
    return shifted(rows, LINES, shift_by)


def body(
    points,
    counts,
    owner,
    zorder,
    border,
    near,
    w_near,
    gain_one,
    conv_w,
    gain_two,
    w_up,
    w_down,
    grad_out,
):
    points_tile = points[0]
    tile_rows, width = points_tile.shape
    lists = border[0]
    border_rows = lists.shape[1]
    cols_count = lax.axis_size("tx")
    lines_count = lax.axis_size(LINES)
    tiles = cols_count * lines_count
    recv_rows = zorder.shape[1]
    capacity = recv_rows // tiles
    near_tile = near[0]
    owner_tile = owner[0]
    sent = jnp.take(points_tile, lists.reshape(-1), axis=0).reshape(4, border_rows, width)
    halo = jnp.concatenate(
        [
            pass_columns(sent[0], -1),
            pass_columns(sent[1], 1),
            pass_lines(sent[2], -1),
            pass_lines(sent[3], 1),
        ],
        axis=0,
    )
    count_near = near_tile.shape[0]
    counts_t = near_counts(near_tile, tile_rows + 4 * border_rows)
    average, linear_part, lifted = tile_forward(points_tile, halo, counts_t, w_near, count_near)
    slots = route_slots(owner_tile, counts[0], tiles, capacity)
    slot_picks = one_hot_rows(slots, tiles * capacity)
    order_picks = one_hot_rows(zorder[0], recv_rows).T
    payload = jnp.concatenate([lifted, grad_out[0]], axis=1)
    outgoing = move_rows(slot_picks, payload, False)
    incoming = lax.all_to_all(outgoing, ALL, split_axis=0, concat_axis=0, tiled=True)
    serial_both = move_rows(order_picks, incoming, False)
    taps_full = block_taps(conv_w)

    results, serial_grads, sums = patch_pass(
        serial_both[:, :width], serial_both[:, width:], gain_one, conv_w, taps_full, gain_two, w_up, w_down
    )
    back = jnp.concatenate(
        [results.reshape(recv_rows, width), serial_grads.reshape(recv_rows, width)], axis=1
    )
    back_slots = move_rows(order_picks, back, True)
    returned = lax.all_to_all(back_slots, ALL, split_axis=0, concat_axis=0, tiled=True)
    back_rows = move_rows(slot_picks, returned, True)
    out_rows = back_rows[:, :width]
    lifted_grad = back_rows[:, width:]
    patch_flat = jnp.concatenate(
        [sums[0], sums[2], sums[1].reshape(-1), sums[3].reshape(-1), sums[4].reshape(-1)]
    )
    near_grad, row_grad, halo_grad = tile_backward(
        lifted_grad, average, linear_part, counts_t, w_near, count_near
    )
    came_back = (
        pass_columns(halo_grad[0:border_rows], 1),
        pass_columns(halo_grad[border_rows : 2 * border_rows], -1),
        pass_lines(halo_grad[2 * border_rows : 3 * border_rows], 1),
        pass_lines(halo_grad[3 * border_rows : 4 * border_rows], -1),
    )
    for direction in range(4):
        row_grad = row_grad.at[lists[direction]].add(came_back[direction].astype(jnp.float32))
    grads_total = pair_sum(jnp.concatenate([near_grad.reshape(-1), patch_flat]), ("tx", "tyc"))
    near_sum = grads_total[: near_grad.size].reshape(near_grad.shape)
    patch_total = grads_total[near_grad.size :]
    sizes = [width, width, conv_w.size, w_up.size, w_down.size]
    shapes = [(width,), (width,), conv_w.shape, w_up.shape, w_down.shape]
    offsets = [sum(sizes[:index]) for index in range(len(sizes))]
    gain_one_sum, gain_two_sum, conv_sum, up_sum, down_sum = [
        patch_total[start : start + size].reshape(shape)
        for start, size, shape in zip(offsets, sizes, shapes)
    ]
    totals = (gain_one_sum, conv_sum, gain_two_sum, up_sum, down_sum)
    scale = 1.0 / math.sqrt(tiles * tile_rows)
    return (
        out_rows[None],
        row_grad.astype(jnp.bfloat16)[None],
        near_sum * scale,
        totals[0] * scale,
        totals[1] * scale,
        totals[2] * scale,
        totals[3] * scale,
        totals[4] * scale,
    )


def solution(mesh):
    placed = (
        P(ALL, None, None),
        P(ALL),
        P(ALL, None),
        P(ALL, None),
        P(ALL, None, None),
        P(ALL, None, None),
        P(),
        P(),
        P(),
        P(),
        P(),
        P(),
        P(ALL, None, None),
    )
    return jax.shard_map(
        body,
        mesh=Mesh(mesh.devices.reshape(mesh.shape["tx"], -1, 2), ALL),
        in_specs=placed,
        out_specs=(
            P(ALL, None, None),
            P(ALL, None, None),
            P(),
            P(),
            P(),
            P(),
            P(),
            P(),
        ),
        check_vma=False,
    )
```

```python
import math

import jax
import jax.numpy as jnp
from jax import lax
from jax.experimental import pallas as pl
from jax.experimental.pallas import tpu as pltpu
from jax.sharding import Mesh, PartitionSpec as P

PATCH = 1024
LINES = ("tyc", "core")
ALL = ("tx",) + LINES


eps_norm = 1e-06
gelu_coef = 0.7978845608028654
cubic_coef = 0.044715


def shifted(value, axis, steps):
    count = lax.axis_size(axis)
    initial, last = (max(0, -steps), min(count, count - steps))
    return lax.ppermute(value, axis, [(source, source + steps) for source in range(initial, last)])


def gelu_tanh(value):
    inner = gelu_coef * (value + cubic_coef * value * value * value)
    return 0.5 * value * (1.0 + jnp.tanh(inner))


def gelu_slope(value):
    inner = gelu_coef * (value + cubic_coef * value * value * value)
    tangent = jnp.tanh(inner)
    return 0.5 * (1.0 + tangent) + 0.5 * value * (1.0 - tangent * tangent) * gelu_coef * (
        1.0 + 3.0 * cubic_coef * value * value
    )


def inverse_rms(value):
    return lax.rsqrt(jnp.mean(value * value, axis=-1, keepdims=True) + eps_norm)


def near_counts(near_tile, ext_count):
    rows = lax.broadcasted_iota(jnp.int32, (ext_count, near_tile.shape[1]), 0)
    total = jnp.zeros((ext_count, near_tile.shape[1]), jnp.bfloat16)
    for index in range(near_tile.shape[0]):
        total = total + (near_tile[index][None, :] == rows).astype(jnp.bfloat16)
    return total


def tile_forward(points_tile, halo_rows, counts_t, w_near, count_near):
    extended = jnp.concatenate([points_tile, halo_rows], axis=0)
    total = lax.dot_general(
        counts_t, extended, (((0,), (0,)), ((), ())), preferred_element_type=jnp.float32
    )
    average = (total * (1.0 / count_near)).astype(jnp.bfloat16)
    linear_part = jnp.dot(average, w_near, preferred_element_type=jnp.float32)
    lifted = (points_tile.astype(jnp.float32) + gelu_tanh(linear_part)).astype(jnp.bfloat16)
    return (average, linear_part, lifted)


def tile_backward(lifted_grad, average, linear_part, counts_t, w_near, count_near):
    tile_rows = lifted_grad.shape[0]
    act_grad = (lifted_grad.astype(jnp.float32) * gelu_slope(linear_part)).astype(jnp.bfloat16)
    near_grad = lax.dot_general(
        average, act_grad, (((0,), (0,)), ((), ())), preferred_element_type=jnp.float32
    )
    spread = lax.dot_general(
        act_grad, w_near, (((1,), (1,)), ((), ())), preferred_element_type=jnp.float32
    ) * (1.0 / count_near)
    spread_hi = spread.astype(jnp.bfloat16)
    spread_lo = (spread - spread_hi.astype(jnp.float32)).astype(jnp.bfloat16)
    ext_grad = jnp.dot(counts_t, spread_hi, preferred_element_type=jnp.float32) + jnp.dot(
        counts_t, spread_lo, preferred_element_type=jnp.float32
    )
    row_grad = lifted_grad.astype(jnp.float32) + ext_grad[:tile_rows]
    halo_grad = ext_grad[tile_rows:].astype(jnp.bfloat16)
    return (near_grad, row_grad, halo_grad)


def route_ranks(owner_tile, count, tiles):
    tile_rows = owner_tile.shape[0]
    index = jnp.arange(tile_rows, dtype=jnp.int32)
    live = index < count
    score = jnp.where(live, owner_tile * tile_rows + index, tiles * tile_rows + index)
    order = jnp.argsort(score, stable=True)
    members = (owner_tile[:, None] == jnp.arange(tiles, dtype=jnp.int32)[None, :]) & live[:, None]
    per_owner = jnp.sum(members.astype(jnp.int32), axis=0)
    starts = jnp.cumsum(per_owner) - per_owner
    sorted_owner = jnp.take(owner_tile, order)
    ranked = index - jnp.take(starts, sorted_owner)
    rank = jnp.zeros((tile_rows,), jnp.int32).at[order].set(ranked)
    return (rank, live)


def route_slots(owner_tile, count, tiles, capacity):
    tile_rows = owner_tile.shape[0]
    live = jnp.arange(tile_rows, dtype=jnp.int32) < count
    owner_ids = lax.broadcasted_iota(jnp.int32, (tile_rows, tiles), 1)
    members = ((owner_tile[:, None] == owner_ids) & live[:, None]).astype(jnp.bfloat16)
    before = (
        lax.broadcasted_iota(jnp.int32, (tile_rows, tile_rows), 1)
        < lax.broadcasted_iota(jnp.int32, (tile_rows, tile_rows), 0)
    ).astype(jnp.bfloat16)
    prefix = jnp.dot(before, members, preferred_element_type=jnp.float32)
    rank = jnp.sum(prefix * members.astype(jnp.float32), axis=1).astype(jnp.int32)
    return jnp.where(live, owner_tile * capacity + rank, tiles * capacity)


def one_hot_rows(ids, size):
    return (lax.broadcasted_iota(jnp.int32, (size, ids.shape[0]), 0) == ids[None, :]).astype(
        jnp.bfloat16
    )


def move_rows(picks, rows, transpose):
    dims = (((0,), (0,)), ((), ())) if transpose else (((1,), (0,)), ((), ()))
    return lax.dot_general(picks, rows, dims, preferred_element_type=jnp.float32).astype(rows.dtype)


def shift_down(rows):
    patches = rows.reshape(-1, PATCH, rows.shape[-1])
    moved = jnp.concatenate([jnp.zeros_like(patches[:, :1]), patches[:, :-1]], axis=1)
    return moved.reshape(rows.shape)


def shift_up(rows):
    patches = rows.reshape(-1, PATCH, rows.shape[-1])
    moved = jnp.concatenate([patches[:, 1:], jnp.zeros_like(patches[:, :1])], axis=1)
    return moved.reshape(rows.shape)


def block_taps(conv_w):
    groups, inner = (conv_w.shape[1], conv_w.shape[2])
    identity_blocks = jnp.eye(groups, dtype=conv_w.dtype)
    full = jnp.einsum("gh,ogab->ogahb", identity_blocks, conv_w)
    return full.reshape(conv_w.shape[0], groups * inner, groups * inner)


def grouped_weight(inputs, outputs, groups, inner):
    length = inputs.shape[0]
    left = inputs.reshape(length, groups, inner)
    right = outputs.reshape(length, groups, inner)
    return jnp.einsum("pga,pgb->gab", left, right, preferred_element_type=jnp.float32)


def tap_back(rows, tap):
    return lax.dot_general(rows, tap, (((1,), (1,)), ((), ())), preferred_element_type=jnp.float32)


def mlp_kernel(
    second_ref, grad_ref, state_ref, up_ref, down_ref, result_ref, sgrad_ref, upg_ref, downg_ref
):
    @pl.when(pl.program_id(0) == 0)
    def _():
        upg_ref[...] = jnp.zeros_like(upg_ref)
        downg_ref[...] = jnp.zeros_like(downg_ref)

    second = second_ref[...]
    out_grad = grad_ref[...]
    hidden_pre = jnp.dot(second, up_ref[...], preferred_element_type=jnp.float32)
    inner = gelu_coef * (hidden_pre + cubic_coef * hidden_pre * hidden_pre * hidden_pre)
    tangent = jnp.tanh(inner)
    hidden = (0.5 * hidden_pre * (1.0 + tangent)).astype(jnp.bfloat16)
    result_ref[...] = (
        state_ref[...] + jnp.dot(hidden, down_ref[...], preferred_element_type=jnp.float32)
    ).astype(jnp.bfloat16)
    downg_ref[...] += lax.dot_general(
        hidden, out_grad, (((0,), (0,)), ((), ())), preferred_element_type=jnp.float32
    )
    hidden_grad = lax.dot_general(
        out_grad, down_ref[...], (((1,), (1,)), ((), ())), preferred_element_type=jnp.float32
    ).astype(jnp.bfloat16)
    slope = 0.5 * (1.0 + tangent) + 0.5 * hidden_pre * (1.0 - tangent * tangent) * gelu_coef * (
        1.0 + 3.0 * cubic_coef * hidden_pre * hidden_pre
    )
    pre_grad = (hidden_grad.astype(jnp.float32) * slope).astype(jnp.bfloat16)
    upg_ref[...] += lax.dot_general(
        second, pre_grad, (((0,), (0,)), ((), ())), preferred_element_type=jnp.float32
    )
    sgrad_ref[...] = lax.dot_general(
        pre_grad, up_ref[...], (((1,), (1,)), ((), ())), preferred_element_type=jnp.float32
    ).astype(jnp.bfloat16)


def mlp_pass(second, out_grad, state, w_up, w_down, block_rows=512):
    rows, width = second.shape
    ffn = w_up.shape[1]
    row_block = pl.BlockSpec((block_rows, width), lambda step: (step, 0))
    whole = lambda shape: pl.BlockSpec(shape, lambda step: (0, 0))
    flops = 2 * rows * width * ffn * 6
    return pl.pallas_call(
        mlp_kernel,
        grid=(rows // block_rows,),
        in_specs=[row_block, row_block, row_block, whole((width, ffn)), whole((ffn, width))],
        out_specs=[row_block, row_block, whole((width, ffn)), whole((ffn, width))],
        out_shape=[
            jax.ShapeDtypeStruct((rows, width), jnp.bfloat16),
            jax.ShapeDtypeStruct((rows, width), jnp.bfloat16),
            jax.ShapeDtypeStruct((width, ffn), jnp.float32),
            jax.ShapeDtypeStruct((ffn, width), jnp.float32),
        ],
        compiler_params=pltpu.CompilerParams(dimension_semantics=("arbitrary",)),
        cost_estimate=pl.CostEstimate(
            flops=flops, transcendentals=rows * ffn, bytes_accessed=rows * width * 10 + 4 * width * ffn * 3
        ),
    )(second, out_grad, state, w_up, w_down)


def patch_pass(serial, out_grad, gain_one, conv_w, taps_full, gain_two, w_up, w_down):
    groups, inner = (conv_w.shape[1], conv_w.shape[2])
    serial_f = serial.astype(jnp.float32)
    scale_one = inverse_rms(serial_f)
    normed = (serial_f * scale_one * gain_one).astype(jnp.bfloat16)
    taps = (shift_down(normed), normed, shift_up(normed))
    mixed = (
        jnp.dot(taps[0], taps_full[0], preferred_element_type=jnp.float32)
        + jnp.dot(taps[1], taps_full[1], preferred_element_type=jnp.float32)
        + jnp.dot(taps[2], taps_full[2], preferred_element_type=jnp.float32)
    )
    state = serial_f + mixed
    scale_two = inverse_rms(state)
    second = (state * scale_two * gain_two).astype(jnp.bfloat16)
    result, second_grad, up_grad, down_grad = mlp_pass(second, out_grad, state, w_up, w_down)
    unit_two = state * scale_two
    weighted_two = second_grad.astype(jnp.float32) * gain_two
    gain_two_grad = jnp.sum(second_grad.astype(jnp.float32) * unit_two, axis=0)
    state_grad = out_grad.astype(jnp.float32) + scale_two * (
        weighted_two - unit_two * jnp.mean(weighted_two * unit_two, axis=-1, keepdims=True)
    )
    mixed_grad = state_grad.astype(jnp.bfloat16)
    conv_grad = jnp.stack(
        [
            grouped_weight(taps[0], mixed_grad, groups, inner),
            grouped_weight(taps[1], mixed_grad, groups, inner),
            grouped_weight(taps[2], mixed_grad, groups, inner),
        ],
        axis=0,
    )
    normed_grad = (
        shift_up(tap_back(mixed_grad, taps_full[0]))
        + tap_back(mixed_grad, taps_full[1])
        + shift_down(tap_back(mixed_grad, taps_full[2]))
    ).astype(jnp.bfloat16)
    unit_one = serial_f * scale_one
    weighted_one = normed_grad.astype(jnp.float32) * gain_one
    gain_one_grad = jnp.sum(normed_grad.astype(jnp.float32) * unit_one, axis=0)
    serial_grad = (
        state_grad
        + scale_one
        * (weighted_one - unit_one * jnp.mean(weighted_one * unit_one, axis=-1, keepdims=True))
    ).astype(jnp.bfloat16)
    return (result, serial_grad, (gain_one_grad, conv_grad, gain_two_grad, up_grad, down_grad))


def all_sum(flat, axes):
    devices = lax.axis_size(axes)
    chunk = -(-flat.shape[0] // (devices * 1024)) * 1024
    padded = jnp.pad(flat, (0, devices * chunk - flat.shape[0])).reshape(devices, chunk // 128, 128)
    pieces = lax.all_to_all(padded, axes, split_axis=0, concat_axis=0, tiled=True)
    part = jnp.sum(pieces, axis=0)
    spread = jnp.broadcast_to(part[None], (devices,) + part.shape)
    whole = lax.all_to_all(spread, axes, split_axis=0, concat_axis=0, tiled=True)
    return whole.reshape(-1)[: flat.shape[0]]


def pair_sum(flat, group):
    devices = lax.axis_size(group)
    chunk = -(-flat.shape[0] // (2 * devices * 1024)) * 1024
    halves = jnp.pad(flat, (0, 2 * devices * chunk - flat.shape[0])).reshape(2, devices * chunk)
    core = lax.axis_index("core")
    swap = [(0, 1), (1, 0)]
    mine = jnp.where(core == 0, halves[0], halves[1])
    theirs = jnp.where(core == 0, halves[1], halves[0])
    half_sum = mine + lax.ppermute(theirs, "core", swap)
    total = all_sum(half_sum, group)
    other = lax.ppermute(total, "core", swap)
    whole = jnp.where(core == 0, jnp.concatenate([total, other]), jnp.concatenate([other, total]))
    return whole[: flat.shape[0]]


def pass_columns(rows, shift_by):
    return shifted(rows, "tx", shift_by)


def pass_lines(rows, shift_by):
    return shifted(rows, LINES, shift_by)


def body(
    points,
    counts,
    owner,
    zorder,
    border,
    near,
    w_near,
    gain_one,
    conv_w,
    gain_two,
    w_up,
    w_down,
    grad_out,
):
    points_tile = points[0]
    tile_rows, width = points_tile.shape
    lists = border[0]
    border_rows = lists.shape[1]
    cols_count = lax.axis_size("tx")
    lines_count = lax.axis_size(LINES)
    tiles = cols_count * lines_count
    recv_rows = zorder.shape[1]
    capacity = recv_rows // tiles
    near_tile = near[0]
    owner_tile = owner[0]
    sent = jnp.take(points_tile, lists.reshape(-1), axis=0).reshape(4, border_rows, width)
    halo = jnp.concatenate(
        [
            pass_columns(sent[0], -1),
            pass_columns(sent[1], 1),
            pass_lines(sent[2], -1),
            pass_lines(sent[3], 1),
        ],
        axis=0,
    )
    count_near = near_tile.shape[0]
    counts_t = near_counts(near_tile, tile_rows + 4 * border_rows)
    average, linear_part, lifted = tile_forward(points_tile, halo, counts_t, w_near, count_near)
    slots = route_slots(owner_tile, counts[0], tiles, capacity)
    slot_picks = one_hot_rows(slots, tiles * capacity)
    order_picks = one_hot_rows(zorder[0], recv_rows).T
    payload = jnp.concatenate([lifted, grad_out[0]], axis=1)
    outgoing = move_rows(slot_picks, payload, False)
    incoming = lax.all_to_all(outgoing, ALL, split_axis=0, concat_axis=0, tiled=True)
    serial_both = move_rows(order_picks, incoming, False)
    taps_full = block_taps(conv_w)

    results, serial_grads, sums = patch_pass(
        serial_both[:, :width], serial_both[:, width:], gain_one, conv_w, taps_full, gain_two, w_up, w_down
    )
    back = jnp.concatenate(
        [results.reshape(recv_rows, width), serial_grads.reshape(recv_rows, width)], axis=1
    )
    back_slots = move_rows(order_picks, back, True)
    returned = lax.all_to_all(back_slots, ALL, split_axis=0, concat_axis=0, tiled=True)
    back_rows = move_rows(slot_picks, returned, True)
    out_rows = back_rows[:, :width]
    lifted_grad = back_rows[:, width:]
    patch_flat = jnp.concatenate(
        [sums[0], sums[2], sums[1].reshape(-1), sums[3].reshape(-1), sums[4].reshape(-1)]
    )
    near_grad, row_grad, halo_grad = tile_backward(
        lifted_grad, average, linear_part, counts_t, w_near, count_near
    )
    came_back = (
        pass_columns(halo_grad[0:border_rows], 1),
        pass_columns(halo_grad[border_rows : 2 * border_rows], -1),
        pass_lines(halo_grad[2 * border_rows : 3 * border_rows], 1),
        pass_lines(halo_grad[3 * border_rows : 4 * border_rows], -1),
    )
    for direction in range(4):
        row_grad = row_grad.at[lists[direction]].add(came_back[direction].astype(jnp.float32))
    grads_total = pair_sum(jnp.concatenate([near_grad.reshape(-1), patch_flat]), ("tx", "tyc"))
    near_sum = grads_total[: near_grad.size].reshape(near_grad.shape)
    patch_total = grads_total[near_grad.size :]
    sizes = [width, width, conv_w.size, w_up.size, w_down.size]
    shapes = [(width,), (width,), conv_w.shape, w_up.shape, w_down.shape]
    offsets = [sum(sizes[:index]) for index in range(len(sizes))]
    gain_one_sum, gain_two_sum, conv_sum, up_sum, down_sum = [
        patch_total[start : start + size].reshape(shape)
        for start, size, shape in zip(offsets, sizes, shapes)
    ]
    totals = (gain_one_sum, conv_sum, gain_two_sum, up_sum, down_sum)
    scale = 1.0 / math.sqrt(tiles * tile_rows)
    return (
        out_rows[None],
        row_grad.astype(jnp.bfloat16)[None],
        near_sum * scale,
        totals[0] * scale,
        totals[1] * scale,
        totals[2] * scale,
        totals[3] * scale,
        totals[4] * scale,
    )


def solution(mesh):
    placed = (
        P(ALL, None, None),
        P(ALL),
        P(ALL, None),
        P(ALL, None),
        P(ALL, None, None),
        P(ALL, None, None),
        P(),
        P(),
        P(),
        P(),
        P(),
        P(),
        P(ALL, None, None),
    )
    return jax.shard_map(
        body,
        mesh=Mesh(mesh.devices.reshape(mesh.shape["tx"], -1, 2), ALL),
        in_specs=placed,
        out_specs=(
            P(ALL, None, None),
            P(ALL, None, None),
            P(),
            P(),
            P(),
            P(),
            P(),
            P(),
        ),
        check_vma=False,
    )
```

```python
import math

import jax
import jax.numpy as jnp
from jax import lax
from jax.experimental import pallas as pl
from jax.experimental.pallas import tpu as pltpu
from jax.sharding import Mesh, PartitionSpec as P

PATCH = 1024
LINES = ("tyc", "core")
ALL = ("tx",) + LINES


eps_norm = 1e-06
gelu_coef = 0.7978845608028654
cubic_coef = 0.044715


def shifted(value, axis, steps):
    count = lax.axis_size(axis)
    initial, last = (max(0, -steps), min(count, count - steps))
    return lax.ppermute(value, axis, [(source, source + steps) for source in range(initial, last)])


def gelu_tanh(value):
    inner = gelu_coef * (value + cubic_coef * value * value * value)
    return 0.5 * value * (1.0 + jnp.tanh(inner))


def gelu_slope(value):
    inner = gelu_coef * (value + cubic_coef * value * value * value)
    tangent = jnp.tanh(inner)
    return 0.5 * (1.0 + tangent) + 0.5 * value * (1.0 - tangent * tangent) * gelu_coef * (
        1.0 + 3.0 * cubic_coef * value * value
    )


def inverse_rms(value):
    return lax.rsqrt(jnp.mean(value * value, axis=-1, keepdims=True) + eps_norm)


def near_counts(near_tile, ext_count):
    rows = lax.broadcasted_iota(jnp.int32, (ext_count, near_tile.shape[1]), 0)
    total = jnp.zeros((ext_count, near_tile.shape[1]), jnp.float32)
    for index in range(near_tile.shape[0]):
        total = total + (near_tile[index][None, :] == rows).astype(jnp.float32)
    return total.astype(jnp.bfloat16)


def tile_forward(points_tile, halo_rows, counts_t, w_near, count_near):
    extended = jnp.concatenate([points_tile, halo_rows], axis=0)
    total = lax.dot_general(
        counts_t, extended, (((0,), (0,)), ((), ())), preferred_element_type=jnp.float32
    )
    average = (total * (1.0 / count_near)).astype(jnp.bfloat16)
    linear_part = jnp.dot(average, w_near, preferred_element_type=jnp.float32)
    lifted = (points_tile.astype(jnp.float32) + gelu_tanh(linear_part)).astype(jnp.bfloat16)
    return (average, linear_part, lifted)


def tile_backward(lifted_grad, average, linear_part, counts_t, w_near, count_near):
    tile_rows = lifted_grad.shape[0]
    act_grad = (lifted_grad.astype(jnp.float32) * gelu_slope(linear_part)).astype(jnp.bfloat16)
    near_grad = lax.dot_general(
        average, act_grad, (((0,), (0,)), ((), ())), preferred_element_type=jnp.float32
    )
    spread = lax.dot_general(
        act_grad, w_near, (((1,), (1,)), ((), ())), preferred_element_type=jnp.float32
    ) * (1.0 / count_near)
    spread_hi = spread.astype(jnp.bfloat16)
    spread_lo = (spread - spread_hi.astype(jnp.float32)).astype(jnp.bfloat16)
    ext_grad = jnp.dot(counts_t, spread_hi, preferred_element_type=jnp.float32) + jnp.dot(
        counts_t, spread_lo, preferred_element_type=jnp.float32
    )
    row_grad = lifted_grad.astype(jnp.float32) + ext_grad[:tile_rows]
    halo_grad = ext_grad[tile_rows:].astype(jnp.bfloat16)
    return (near_grad, row_grad, halo_grad)


def route_ranks(owner_tile, count, tiles):
    tile_rows = owner_tile.shape[0]
    index = jnp.arange(tile_rows, dtype=jnp.int32)
    live = index < count
    score = jnp.where(live, owner_tile * tile_rows + index, tiles * tile_rows + index)
    order = jnp.argsort(score, stable=True)
    members = (owner_tile[:, None] == jnp.arange(tiles, dtype=jnp.int32)[None, :]) & live[:, None]
    per_owner = jnp.sum(members.astype(jnp.int32), axis=0)
    starts = jnp.cumsum(per_owner) - per_owner
    sorted_owner = jnp.take(owner_tile, order)
    ranked = index - jnp.take(starts, sorted_owner)
    rank = jnp.zeros((tile_rows,), jnp.int32).at[order].set(ranked)
    return (rank, live)


def route_slots(owner_tile, count, tiles, capacity):
    tile_rows = owner_tile.shape[0]
    live = jnp.arange(tile_rows, dtype=jnp.int32) < count
    owner_ids = lax.broadcasted_iota(jnp.int32, (tile_rows, tiles), 1)
    members = ((owner_tile[:, None] == owner_ids) & live[:, None]).astype(jnp.bfloat16)
    before = (
        lax.broadcasted_iota(jnp.int32, (tile_rows, tile_rows), 1)
        < lax.broadcasted_iota(jnp.int32, (tile_rows, tile_rows), 0)
    ).astype(jnp.bfloat16)
    prefix = jnp.dot(before, members, preferred_element_type=jnp.float32)
    rank = jnp.sum(prefix * members.astype(jnp.float32), axis=1).astype(jnp.int32)
    return jnp.where(live, owner_tile * capacity + rank, tiles * capacity)


def one_hot_rows(ids, size):
    return (lax.broadcasted_iota(jnp.int32, (size, ids.shape[0]), 0) == ids[None, :]).astype(
        jnp.bfloat16
    )


def move_rows(picks, rows, transpose):
    dims = (((0,), (0,)), ((), ())) if transpose else (((1,), (0,)), ((), ()))
    return lax.dot_general(picks, rows, dims, preferred_element_type=jnp.float32).astype(rows.dtype)


def shift_down(rows):
    patches = rows.reshape(-1, PATCH, rows.shape[-1])
    moved = jnp.concatenate([jnp.zeros_like(patches[:, :1]), patches[:, :-1]], axis=1)
    return moved.reshape(rows.shape)


def shift_up(rows):
    patches = rows.reshape(-1, PATCH, rows.shape[-1])
    moved = jnp.concatenate([patches[:, 1:], jnp.zeros_like(patches[:, :1])], axis=1)
    return moved.reshape(rows.shape)


def block_taps(conv_w):
    groups, inner = (conv_w.shape[1], conv_w.shape[2])
    identity_blocks = jnp.eye(groups, dtype=conv_w.dtype)
    full = jnp.einsum("gh,ogab->ogahb", identity_blocks, conv_w)
    return full.reshape(conv_w.shape[0], groups * inner, groups * inner)


def grouped_weight(inputs, outputs, groups, inner):
    length = inputs.shape[0]
    left = inputs.reshape(length, groups, inner)
    right = outputs.reshape(length, groups, inner)
    return jnp.einsum("pga,pgb->gab", left, right, preferred_element_type=jnp.float32)


def tap_back(rows, tap):
    return lax.dot_general(rows, tap, (((1,), (1,)), ((), ())), preferred_element_type=jnp.float32)


def mlp_kernel(
    state_ref, scale_ref, gain_ref, grad_ref, up_ref, down_ref, result_ref, sgrad_ref, upg_ref, downg_ref
):
    @pl.when(pl.program_id(0) == 0)
    def _():
        upg_ref[...] = jnp.zeros_like(upg_ref)
        downg_ref[...] = jnp.zeros_like(downg_ref)

    second = (state_ref[...] * scale_ref[...] * gain_ref[...]).astype(jnp.bfloat16)
    out_grad = grad_ref[...]
    hidden_pre = jnp.dot(second, up_ref[...], preferred_element_type=jnp.float32)
    inner = gelu_coef * (hidden_pre + cubic_coef * hidden_pre * hidden_pre * hidden_pre)
    tangent = jnp.tanh(inner)
    hidden = (0.5 * hidden_pre * (1.0 + tangent)).astype(jnp.bfloat16)
    result_ref[...] = (
        state_ref[...] + jnp.dot(hidden, down_ref[...], preferred_element_type=jnp.float32)
    ).astype(jnp.bfloat16)
    downg_ref[...] += lax.dot_general(
        hidden, out_grad, (((0,), (0,)), ((), ())), preferred_element_type=jnp.float32
    )
    hidden_grad = lax.dot_general(
        out_grad, down_ref[...], (((1,), (1,)), ((), ())), preferred_element_type=jnp.float32
    ).astype(jnp.bfloat16)
    slope = 0.5 * (1.0 + tangent) + 0.5 * hidden_pre * (1.0 - tangent * tangent) * gelu_coef * (
        1.0 + 3.0 * cubic_coef * hidden_pre * hidden_pre
    )
    pre_grad = (hidden_grad.astype(jnp.float32) * slope).astype(jnp.bfloat16)
    upg_ref[...] += lax.dot_general(
        second, pre_grad, (((0,), (0,)), ((), ())), preferred_element_type=jnp.float32
    )
    sgrad_ref[...] = lax.dot_general(
        pre_grad, up_ref[...], (((1,), (1,)), ((), ())), preferred_element_type=jnp.float32
    ).astype(jnp.bfloat16)


def mlp_pass(state, scale_two, gain_two, out_grad, w_up, w_down, block_rows=512):
    rows, width = state.shape
    ffn = w_up.shape[1]
    row_block = pl.BlockSpec((block_rows, width), lambda step: (step, 0))
    whole = lambda shape: pl.BlockSpec(shape, lambda step: (0, 0))
    flops = 2 * rows * width * ffn * 6
    return pl.pallas_call(
        mlp_kernel,
        grid=(rows // block_rows,),
        in_specs=[
            row_block,
            pl.BlockSpec((block_rows, 1), lambda step: (step, 0)),
            whole((1, width)),
            row_block,
            whole((width, ffn)),
            whole((ffn, width)),
        ],
        out_specs=[row_block, row_block, whole((width, ffn)), whole((ffn, width))],
        out_shape=[
            jax.ShapeDtypeStruct((rows, width), jnp.bfloat16),
            jax.ShapeDtypeStruct((rows, width), jnp.bfloat16),
            jax.ShapeDtypeStruct((width, ffn), jnp.float32),
            jax.ShapeDtypeStruct((ffn, width), jnp.float32),
        ],
        compiler_params=pltpu.CompilerParams(dimension_semantics=("arbitrary",)),
        cost_estimate=pl.CostEstimate(
            flops=flops, transcendentals=rows * ffn, bytes_accessed=rows * width * 10 + 4 * width * ffn * 3
        ),
    )(state, scale_two, gain_two.reshape(1, width), out_grad, w_up, w_down)


def patch_pass(serial, out_grad, gain_one, conv_w, taps_full, gain_two, w_up, w_down):
    groups, inner = (conv_w.shape[1], conv_w.shape[2])
    serial_f = serial.astype(jnp.float32)
    scale_one = inverse_rms(serial_f)
    normed = (serial_f * scale_one * gain_one).astype(jnp.bfloat16)
    taps = (shift_down(normed), normed, shift_up(normed))
    mixed = (
        jnp.dot(taps[0], taps_full[0], preferred_element_type=jnp.float32)
        + jnp.dot(taps[1], taps_full[1], preferred_element_type=jnp.float32)
        + jnp.dot(taps[2], taps_full[2], preferred_element_type=jnp.float32)
    )
    state = serial_f + mixed
    scale_two = inverse_rms(state)
    result, second_grad, up_grad, down_grad = mlp_pass(state, scale_two, gain_two, out_grad, w_up, w_down)
    unit_two = state * scale_two
    weighted_two = second_grad.astype(jnp.float32) * gain_two
    gain_two_grad = jnp.sum(second_grad.astype(jnp.float32) * unit_two, axis=0)
    state_grad = out_grad.astype(jnp.float32) + scale_two * (
        weighted_two - unit_two * jnp.mean(weighted_two * unit_two, axis=-1, keepdims=True)
    )
    mixed_grad = state_grad.astype(jnp.bfloat16)
    conv_grad = jnp.stack(
        [
            grouped_weight(taps[0], mixed_grad, groups, inner),
            grouped_weight(taps[1], mixed_grad, groups, inner),
            grouped_weight(taps[2], mixed_grad, groups, inner),
        ],
        axis=0,
    )
    normed_grad = (
        shift_up(tap_back(mixed_grad, taps_full[0]))
        + tap_back(mixed_grad, taps_full[1])
        + shift_down(tap_back(mixed_grad, taps_full[2]))
    ).astype(jnp.bfloat16)
    unit_one = serial_f * scale_one
    weighted_one = normed_grad.astype(jnp.float32) * gain_one
    gain_one_grad = jnp.sum(normed_grad.astype(jnp.float32) * unit_one, axis=0)
    serial_grad = (
        state_grad
        + scale_one
        * (weighted_one - unit_one * jnp.mean(weighted_one * unit_one, axis=-1, keepdims=True))
    ).astype(jnp.bfloat16)
    return (result, serial_grad, (gain_one_grad, conv_grad, gain_two_grad, up_grad, down_grad))


def all_sum(flat, axes):
    devices = lax.axis_size(axes)
    chunk = -(-flat.shape[0] // (devices * 1024)) * 1024
    padded = jnp.pad(flat, (0, devices * chunk - flat.shape[0])).reshape(devices, chunk // 128, 128)
    pieces = lax.all_to_all(padded, axes, split_axis=0, concat_axis=0, tiled=True)
    part = jnp.sum(pieces, axis=0)
    spread = jnp.broadcast_to(part[None], (devices,) + part.shape)
    whole = lax.all_to_all(spread, axes, split_axis=0, concat_axis=0, tiled=True)
    return whole.reshape(-1)[: flat.shape[0]]


def pair_sum(flat, group):
    devices = lax.axis_size(group)
    chunk = -(-flat.shape[0] // (2 * devices * 1024)) * 1024
    halves = jnp.pad(flat, (0, 2 * devices * chunk - flat.shape[0])).reshape(2, devices * chunk)
    core = lax.axis_index("core")
    swap = [(0, 1), (1, 0)]
    mine = jnp.where(core == 0, halves[0], halves[1])
    theirs = jnp.where(core == 0, halves[1], halves[0])
    half_sum = mine + lax.ppermute(theirs, "core", swap)
    total = all_sum(half_sum, group)
    other = lax.ppermute(total, "core", swap)
    whole = jnp.where(core == 0, jnp.concatenate([total, other]), jnp.concatenate([other, total]))
    return whole[: flat.shape[0]]


def pass_columns(rows, shift_by):
    return shifted(rows, "tx", shift_by)


def pass_lines(rows, shift_by):
    return shifted(rows, LINES, shift_by)


def body(
    points,
    counts,
    owner,
    zorder,
    border,
    near,
    w_near,
    gain_one,
    conv_w,
    gain_two,
    w_up,
    w_down,
    grad_out,
):
    points_tile = points[0]
    tile_rows, width = points_tile.shape
    lists = border[0]
    border_rows = lists.shape[1]
    cols_count = lax.axis_size("tx")
    lines_count = lax.axis_size(LINES)
    tiles = cols_count * lines_count
    recv_rows = zorder.shape[1]
    capacity = recv_rows // tiles
    near_tile = near[0]
    owner_tile = owner[0]
    sent = jnp.take(points_tile, lists.reshape(-1), axis=0).reshape(4, border_rows, width)
    halo = jnp.concatenate(
        [
            pass_columns(sent[0], -1),
            pass_columns(sent[1], 1),
            pass_lines(sent[2], -1),
            pass_lines(sent[3], 1),
        ],
        axis=0,
    )
    count_near = near_tile.shape[0]
    counts_t = near_counts(near_tile, tile_rows + 4 * border_rows)
    average, linear_part, lifted = tile_forward(points_tile, halo, counts_t, w_near, count_near)
    slots = route_slots(owner_tile, counts[0], tiles, capacity)
    slot_picks = one_hot_rows(slots, tiles * capacity)
    order_picks = one_hot_rows(zorder[0], recv_rows).T
    payload = jnp.concatenate([lifted, grad_out[0]], axis=1)
    outgoing = move_rows(slot_picks, payload, False)
    incoming = lax.all_to_all(outgoing, ALL, split_axis=0, concat_axis=0, tiled=True)
    serial_both = move_rows(order_picks, incoming, False)
    taps_full = block_taps(conv_w)

    results, serial_grads, sums = patch_pass(
        serial_both[:, :width], serial_both[:, width:], gain_one, conv_w, taps_full, gain_two, w_up, w_down
    )
    back = jnp.concatenate(
        [results.reshape(recv_rows, width), serial_grads.reshape(recv_rows, width)], axis=1
    )
    back_slots = move_rows(order_picks, back, True)
    returned = lax.all_to_all(back_slots, ALL, split_axis=0, concat_axis=0, tiled=True)
    back_rows = move_rows(slot_picks, returned, True)
    out_rows = back_rows[:, :width]
    lifted_grad = back_rows[:, width:]
    patch_flat = jnp.concatenate(
        [sums[0], sums[2], sums[1].reshape(-1), sums[3].reshape(-1), sums[4].reshape(-1)]
    )
    near_grad, row_grad, halo_grad = tile_backward(
        lifted_grad, average, linear_part, counts_t, w_near, count_near
    )
    came_back = (
        pass_columns(halo_grad[0:border_rows], 1),
        pass_columns(halo_grad[border_rows : 2 * border_rows], -1),
        pass_lines(halo_grad[2 * border_rows : 3 * border_rows], 1),
        pass_lines(halo_grad[3 * border_rows : 4 * border_rows], -1),
    )
    for direction in range(4):
        row_grad = row_grad.at[lists[direction]].add(came_back[direction].astype(jnp.float32))
    grads_total = pair_sum(jnp.concatenate([near_grad.reshape(-1), patch_flat]), ("tx", "tyc"))
    near_sum = grads_total[: near_grad.size].reshape(near_grad.shape)
    patch_total = grads_total[near_grad.size :]
    sizes = [width, width, conv_w.size, w_up.size, w_down.size]
    shapes = [(width,), (width,), conv_w.shape, w_up.shape, w_down.shape]
    offsets = [sum(sizes[:index]) for index in range(len(sizes))]
    gain_one_sum, gain_two_sum, conv_sum, up_sum, down_sum = [
        patch_total[start : start + size].reshape(shape)
        for start, size, shape in zip(offsets, sizes, shapes)
    ]
    totals = (gain_one_sum, conv_sum, gain_two_sum, up_sum, down_sum)
    scale = 1.0 / math.sqrt(tiles * tile_rows)
    return (
        out_rows[None],
        row_grad.astype(jnp.bfloat16)[None],
        near_sum * scale,
        totals[0] * scale,
        totals[1] * scale,
        totals[2] * scale,
        totals[3] * scale,
        totals[4] * scale,
    )


def solution(mesh):
    placed = (
        P(ALL, None, None),
        P(ALL),
        P(ALL, None),
        P(ALL, None),
        P(ALL, None, None),
        P(ALL, None, None),
        P(),
        P(),
        P(),
        P(),
        P(),
        P(),
        P(ALL, None, None),
    )
    return jax.shard_map(
        body,
        mesh=Mesh(mesh.devices.reshape(mesh.shape["tx"], -1, 2), ALL),
        in_specs=placed,
        out_specs=(
            P(ALL, None, None),
            P(ALL, None, None),
            P(),
            P(),
            P(),
            P(),
            P(),
            P(),
        ),
        check_vma=False,
    )
```

```python
import math

import jax
import jax.numpy as jnp
from jax import lax
from jax.experimental import pallas as pl
from jax.experimental.pallas import tpu as pltpu
from jax.sharding import Mesh, PartitionSpec as P

PATCH = 1024
LINES = ("tyc", "core")
ALL = ("tx",) + LINES


eps_norm = 1e-06
gelu_coef = 0.7978845608028654
cubic_coef = 0.044715


def shifted(value, axis, steps):
    count = lax.axis_size(axis)
    initial, last = (max(0, -steps), min(count, count - steps))
    return lax.ppermute(value, axis, [(source, source + steps) for source in range(initial, last)])


def gelu_tanh(value):
    inner = gelu_coef * (value + cubic_coef * value * value * value)
    return 0.5 * value * (1.0 + jnp.tanh(inner))


def gelu_slope(value):
    inner = gelu_coef * (value + cubic_coef * value * value * value)
    tangent = jnp.tanh(inner)
    return 0.5 * (1.0 + tangent) + 0.5 * value * (1.0 - tangent * tangent) * gelu_coef * (
        1.0 + 3.0 * cubic_coef * value * value
    )


def inverse_rms(value):
    return lax.rsqrt(jnp.mean(value * value, axis=-1, keepdims=True) + eps_norm)


def near_counts(near_tile, ext_count):
    rows = lax.broadcasted_iota(jnp.int32, (ext_count, near_tile.shape[1]), 0)
    total = jnp.zeros((ext_count, near_tile.shape[1]), jnp.float32)
    for index in range(near_tile.shape[0]):
        total = total + (near_tile[index][None, :] == rows).astype(jnp.float32)
    return total.astype(jnp.bfloat16)


def tile_forward(points_tile, halo_rows, counts_t, w_near, count_near):
    extended = jnp.concatenate([points_tile, halo_rows], axis=0)
    total = lax.dot_general(
        counts_t, extended, (((0,), (0,)), ((), ())), preferred_element_type=jnp.float32
    )
    average = (total * (1.0 / count_near)).astype(jnp.bfloat16)
    linear_part = jnp.dot(average, w_near, preferred_element_type=jnp.float32)
    lifted = (points_tile.astype(jnp.float32) + gelu_tanh(linear_part)).astype(jnp.bfloat16)
    return (average, linear_part, lifted)


def tile_backward(lifted_grad, average, linear_part, counts_t, w_near, count_near):
    tile_rows = lifted_grad.shape[0]
    act_grad = (lifted_grad.astype(jnp.float32) * gelu_slope(linear_part)).astype(jnp.bfloat16)
    near_grad = lax.dot_general(
        average, act_grad, (((0,), (0,)), ((), ())), preferred_element_type=jnp.float32
    )
    spread = lax.dot_general(
        act_grad, w_near, (((1,), (1,)), ((), ())), preferred_element_type=jnp.float32
    ) * (1.0 / count_near)
    spread_hi = spread.astype(jnp.bfloat16)
    spread_lo = (spread - spread_hi.astype(jnp.float32)).astype(jnp.bfloat16)
    ext_grad = jnp.dot(counts_t, spread_hi, preferred_element_type=jnp.float32) + jnp.dot(
        counts_t, spread_lo, preferred_element_type=jnp.float32
    )
    row_grad = lifted_grad.astype(jnp.float32) + ext_grad[:tile_rows]
    halo_grad = ext_grad[tile_rows:].astype(jnp.bfloat16)
    return (near_grad, row_grad, halo_grad)


def route_ranks(owner_tile, count, tiles):
    tile_rows = owner_tile.shape[0]
    index = jnp.arange(tile_rows, dtype=jnp.int32)
    live = index < count
    score = jnp.where(live, owner_tile * tile_rows + index, tiles * tile_rows + index)
    order = jnp.argsort(score, stable=True)
    members = (owner_tile[:, None] == jnp.arange(tiles, dtype=jnp.int32)[None, :]) & live[:, None]
    per_owner = jnp.sum(members.astype(jnp.int32), axis=0)
    starts = jnp.cumsum(per_owner) - per_owner
    sorted_owner = jnp.take(owner_tile, order)
    ranked = index - jnp.take(starts, sorted_owner)
    rank = jnp.zeros((tile_rows,), jnp.int32).at[order].set(ranked)
    return (rank, live)


def route_slots(owner_tile, count, tiles, capacity):
    tile_rows = owner_tile.shape[0]
    live = jnp.arange(tile_rows, dtype=jnp.int32) < count
    owner_ids = lax.broadcasted_iota(jnp.int32, (tile_rows, tiles), 1)
    members = ((owner_tile[:, None] == owner_ids) & live[:, None]).astype(jnp.bfloat16)
    before = (
        lax.broadcasted_iota(jnp.int32, (tile_rows, tile_rows), 1)
        < lax.broadcasted_iota(jnp.int32, (tile_rows, tile_rows), 0)
    ).astype(jnp.bfloat16)
    prefix = jnp.dot(before, members, preferred_element_type=jnp.float32)
    rank = jnp.sum(prefix * members.astype(jnp.float32), axis=1).astype(jnp.int32)
    return jnp.where(live, owner_tile * capacity + rank, tiles * capacity)


def one_hot_rows(ids, size):
    return (lax.broadcasted_iota(jnp.int32, (size, ids.shape[0]), 0) == ids[None, :]).astype(
        jnp.bfloat16
    )


def move_rows(picks, rows, transpose):
    dims = (((0,), (0,)), ((), ())) if transpose else (((1,), (0,)), ((), ()))
    return lax.dot_general(picks, rows, dims, preferred_element_type=jnp.float32).astype(rows.dtype)


def shift_down(rows):
    patches = rows.reshape(-1, PATCH, rows.shape[-1])
    moved = jnp.concatenate([jnp.zeros_like(patches[:, :1]), patches[:, :-1]], axis=1)
    return moved.reshape(rows.shape)


def shift_up(rows):
    patches = rows.reshape(-1, PATCH, rows.shape[-1])
    moved = jnp.concatenate([patches[:, 1:], jnp.zeros_like(patches[:, :1])], axis=1)
    return moved.reshape(rows.shape)


def block_taps(conv_w):
    groups, inner = (conv_w.shape[1], conv_w.shape[2])
    identity_blocks = jnp.eye(groups, dtype=conv_w.dtype)
    full = jnp.einsum("gh,ogab->ogahb", identity_blocks, conv_w)
    return full.reshape(conv_w.shape[0], groups * inner, groups * inner)


def grouped_weight(inputs, outputs, groups, inner):
    length = inputs.shape[0]
    left = inputs.reshape(length, groups, inner)
    right = outputs.reshape(length, groups, inner)
    return jnp.einsum("pga,pgb->gab", left, right, preferred_element_type=jnp.float32)


def tap_back(rows, tap):
    return lax.dot_general(rows, tap, (((1,), (1,)), ((), ())), preferred_element_type=jnp.float32)


def mlp_kernel(
    second_ref, grad_ref, state_ref, up_ref, down_ref, result_ref, sgrad_ref, upg_ref, downg_ref
):
    @pl.when(pl.program_id(0) == 0)
    def _():
        upg_ref[...] = jnp.zeros_like(upg_ref)
        downg_ref[...] = jnp.zeros_like(downg_ref)

    second = second_ref[...]
    out_grad = grad_ref[...]
    hidden_pre = jnp.dot(second, up_ref[...], preferred_element_type=jnp.float32)
    inner = gelu_coef * (hidden_pre + cubic_coef * hidden_pre * hidden_pre * hidden_pre)
    tangent = jnp.tanh(inner)
    hidden = (0.5 * hidden_pre * (1.0 + tangent)).astype(jnp.bfloat16)
    result_ref[...] = (
        state_ref[...] + jnp.dot(hidden, down_ref[...], preferred_element_type=jnp.float32)
    ).astype(jnp.bfloat16)
    downg_ref[...] += lax.dot_general(
        hidden, out_grad, (((0,), (0,)), ((), ())), preferred_element_type=jnp.float32
    )
    hidden_grad = lax.dot_general(
        out_grad, down_ref[...], (((1,), (1,)), ((), ())), preferred_element_type=jnp.float32
    ).astype(jnp.bfloat16)
    slope = 0.5 * (1.0 + tangent) + 0.5 * hidden_pre * (1.0 - tangent * tangent) * gelu_coef * (
        1.0 + 3.0 * cubic_coef * hidden_pre * hidden_pre
    )
    pre_grad = (hidden_grad.astype(jnp.float32) * slope).astype(jnp.bfloat16)
    upg_ref[...] += lax.dot_general(
        second, pre_grad, (((0,), (0,)), ((), ())), preferred_element_type=jnp.float32
    )
    sgrad_ref[...] = lax.dot_general(
        pre_grad, up_ref[...], (((1,), (1,)), ((), ())), preferred_element_type=jnp.float32
    ).astype(jnp.bfloat16)


def mlp_pass(second, out_grad, state, w_up, w_down, block_rows=1024):
    rows, width = second.shape
    ffn = w_up.shape[1]
    row_block = pl.BlockSpec((block_rows, width), lambda step: (step, 0))
    whole = lambda shape: pl.BlockSpec(shape, lambda step: (0, 0))
    flops = 2 * rows * width * ffn * 6
    return pl.pallas_call(
        mlp_kernel,
        grid=(rows // block_rows,),
        in_specs=[row_block, row_block, row_block, whole((width, ffn)), whole((ffn, width))],
        out_specs=[row_block, row_block, whole((width, ffn)), whole((ffn, width))],
        out_shape=[
            jax.ShapeDtypeStruct((rows, width), jnp.bfloat16),
            jax.ShapeDtypeStruct((rows, width), jnp.bfloat16),
            jax.ShapeDtypeStruct((width, ffn), jnp.float32),
            jax.ShapeDtypeStruct((ffn, width), jnp.float32),
        ],
        compiler_params=pltpu.CompilerParams(dimension_semantics=("arbitrary",)),
        cost_estimate=pl.CostEstimate(
            flops=flops, transcendentals=rows * ffn, bytes_accessed=rows * width * 10 + 4 * width * ffn * 3
        ),
    )(second, out_grad, state, w_up, w_down)


def patch_pass(serial, out_grad, gain_one, conv_w, taps_full, gain_two, w_up, w_down):
    groups, inner = (conv_w.shape[1], conv_w.shape[2])
    serial_f = serial.astype(jnp.float32)
    scale_one = inverse_rms(serial_f)
    normed = (serial_f * scale_one * gain_one).astype(jnp.bfloat16)
    taps = (shift_down(normed), normed, shift_up(normed))
    mixed = (
        jnp.dot(taps[0], taps_full[0], preferred_element_type=jnp.float32)
        + jnp.dot(taps[1], taps_full[1], preferred_element_type=jnp.float32)
        + jnp.dot(taps[2], taps_full[2], preferred_element_type=jnp.float32)
    )
    state = serial_f + mixed
    scale_two = inverse_rms(state)
    second = (state * scale_two * gain_two).astype(jnp.bfloat16)
    result, second_grad, up_grad, down_grad = mlp_pass(second, out_grad, state, w_up, w_down)
    unit_two = state * scale_two
    weighted_two = second_grad.astype(jnp.float32) * gain_two
    gain_two_grad = jnp.sum(second_grad.astype(jnp.float32) * unit_two, axis=0)
    state_grad = out_grad.astype(jnp.float32) + scale_two * (
        weighted_two - unit_two * jnp.mean(weighted_two * unit_two, axis=-1, keepdims=True)
    )
    mixed_grad = state_grad.astype(jnp.bfloat16)
    conv_grad = jnp.stack(
        [
            grouped_weight(taps[0], mixed_grad, groups, inner),
            grouped_weight(taps[1], mixed_grad, groups, inner),
            grouped_weight(taps[2], mixed_grad, groups, inner),
        ],
        axis=0,
    )
    normed_grad = (
        shift_up(tap_back(mixed_grad, taps_full[0]))
        + tap_back(mixed_grad, taps_full[1])
        + shift_down(tap_back(mixed_grad, taps_full[2]))
    ).astype(jnp.bfloat16)
    unit_one = serial_f * scale_one
    weighted_one = normed_grad.astype(jnp.float32) * gain_one
    gain_one_grad = jnp.sum(normed_grad.astype(jnp.float32) * unit_one, axis=0)
    serial_grad = (
        state_grad
        + scale_one
        * (weighted_one - unit_one * jnp.mean(weighted_one * unit_one, axis=-1, keepdims=True))
    ).astype(jnp.bfloat16)
    return (result, serial_grad, (gain_one_grad, conv_grad, gain_two_grad, up_grad, down_grad))


def all_sum(flat, axes):
    devices = lax.axis_size(axes)
    chunk = -(-flat.shape[0] // (devices * 1024)) * 1024
    padded = jnp.pad(flat, (0, devices * chunk - flat.shape[0])).reshape(devices, chunk // 128, 128)
    pieces = lax.all_to_all(padded, axes, split_axis=0, concat_axis=0, tiled=True)
    part = jnp.sum(pieces, axis=0)
    spread = jnp.broadcast_to(part[None], (devices,) + part.shape)
    whole = lax.all_to_all(spread, axes, split_axis=0, concat_axis=0, tiled=True)
    return whole.reshape(-1)[: flat.shape[0]]


def pair_sum(flat, group):
    devices = lax.axis_size(group)
    chunk = -(-flat.shape[0] // (2 * devices * 1024)) * 1024
    halves = jnp.pad(flat, (0, 2 * devices * chunk - flat.shape[0])).reshape(2, devices * chunk)
    core = lax.axis_index("core")
    swap = [(0, 1), (1, 0)]
    mine = jnp.where(core == 0, halves[0], halves[1])
    theirs = jnp.where(core == 0, halves[1], halves[0])
    half_sum = mine + lax.ppermute(theirs, "core", swap)
    total = all_sum(half_sum, group)
    other = lax.ppermute(total, "core", swap)
    whole = jnp.where(core == 0, jnp.concatenate([total, other]), jnp.concatenate([other, total]))
    return whole[: flat.shape[0]]


def pass_columns(rows, shift_by):
    return shifted(rows, "tx", shift_by)


def pass_lines(rows, shift_by):
    return shifted(rows, LINES, shift_by)


def body(
    points,
    counts,
    owner,
    zorder,
    border,
    near,
    w_near,
    gain_one,
    conv_w,
    gain_two,
    w_up,
    w_down,
    grad_out,
):
    points_tile = points[0]
    tile_rows, width = points_tile.shape
    lists = border[0]
    border_rows = lists.shape[1]
    cols_count = lax.axis_size("tx")
    lines_count = lax.axis_size(LINES)
    tiles = cols_count * lines_count
    recv_rows = zorder.shape[1]
    capacity = recv_rows // tiles
    near_tile = near[0]
    owner_tile = owner[0]
    sent = jnp.take(points_tile, lists.reshape(-1), axis=0).reshape(4, border_rows, width)
    halo = jnp.concatenate(
        [
            pass_columns(sent[0], -1),
            pass_columns(sent[1], 1),
            pass_lines(sent[2], -1),
            pass_lines(sent[3], 1),
        ],
        axis=0,
    )
    count_near = near_tile.shape[0]
    counts_t = near_counts(near_tile, tile_rows + 4 * border_rows)
    average, linear_part, lifted = tile_forward(points_tile, halo, counts_t, w_near, count_near)
    slots = route_slots(owner_tile, counts[0], tiles, capacity)
    slot_picks = one_hot_rows(slots, tiles * capacity)
    order_picks = one_hot_rows(zorder[0], recv_rows).T
    payload = jnp.concatenate([lifted, grad_out[0]], axis=1)
    outgoing = move_rows(slot_picks, payload, False)
    incoming = lax.all_to_all(outgoing, ALL, split_axis=0, concat_axis=0, tiled=True)
    serial_both = move_rows(order_picks, incoming, False)
    taps_full = block_taps(conv_w)

    results, serial_grads, sums = patch_pass(
        serial_both[:, :width], serial_both[:, width:], gain_one, conv_w, taps_full, gain_two, w_up, w_down
    )
    back = jnp.concatenate(
        [results.reshape(recv_rows, width), serial_grads.reshape(recv_rows, width)], axis=1
    )
    back_slots = move_rows(order_picks, back, True)
    returned = lax.all_to_all(back_slots, ALL, split_axis=0, concat_axis=0, tiled=True)
    back_rows = move_rows(slot_picks, returned, True)
    out_rows = back_rows[:, :width]
    lifted_grad = back_rows[:, width:]
    patch_flat = jnp.concatenate(
        [sums[0], sums[2], sums[1].reshape(-1), sums[3].reshape(-1), sums[4].reshape(-1)]
    )
    near_grad, row_grad, halo_grad = tile_backward(
        lifted_grad, average, linear_part, counts_t, w_near, count_near
    )
    came_back = (
        pass_columns(halo_grad[0:border_rows], 1),
        pass_columns(halo_grad[border_rows : 2 * border_rows], -1),
        pass_lines(halo_grad[2 * border_rows : 3 * border_rows], 1),
        pass_lines(halo_grad[3 * border_rows : 4 * border_rows], -1),
    )
    for direction in range(4):
        row_grad = row_grad.at[lists[direction]].add(came_back[direction].astype(jnp.float32))
    grads_total = pair_sum(jnp.concatenate([near_grad.reshape(-1), patch_flat]), ("tx", "tyc"))
    near_sum = grads_total[: near_grad.size].reshape(near_grad.shape)
    patch_total = grads_total[near_grad.size :]
    sizes = [width, width, conv_w.size, w_up.size, w_down.size]
    shapes = [(width,), (width,), conv_w.shape, w_up.shape, w_down.shape]
    offsets = [sum(sizes[:index]) for index in range(len(sizes))]
    gain_one_sum, gain_two_sum, conv_sum, up_sum, down_sum = [
        patch_total[start : start + size].reshape(shape)
        for start, size, shape in zip(offsets, sizes, shapes)
    ]
    totals = (gain_one_sum, conv_sum, gain_two_sum, up_sum, down_sum)
    scale = 1.0 / math.sqrt(tiles * tile_rows)
    return (
        out_rows[None],
        row_grad.astype(jnp.bfloat16)[None],
        near_sum * scale,
        totals[0] * scale,
        totals[1] * scale,
        totals[2] * scale,
        totals[3] * scale,
        totals[4] * scale,
    )


def solution(mesh):
    placed = (
        P(ALL, None, None),
        P(ALL),
        P(ALL, None),
        P(ALL, None),
        P(ALL, None, None),
        P(ALL, None, None),
        P(),
        P(),
        P(),
        P(),
        P(),
        P(),
        P(ALL, None, None),
    )
    return jax.shard_map(
        body,
        mesh=Mesh(mesh.devices.reshape(mesh.shape["tx"], -1, 2), ALL),
        in_specs=placed,
        out_specs=(
            P(ALL, None, None),
            P(ALL, None, None),
            P(),
            P(),
            P(),
            P(),
            P(),
            P(),
        ),
        check_vma=False,
    )
```

```python
import math

import jax
import jax.numpy as jnp
from jax import lax
from jax.experimental import pallas as pl
from jax.experimental.pallas import tpu as pltpu
from jax.sharding import Mesh, PartitionSpec as P

PATCH = 1024
LINES = ("tyc", "core")
ALL = ("tx",) + LINES


eps_norm = 1e-06
gelu_coef = 0.7978845608028654
cubic_coef = 0.044715


def shifted(value, axis, steps):
    count = lax.axis_size(axis)
    initial, last = (max(0, -steps), min(count, count - steps))
    return lax.ppermute(value, axis, [(source, source + steps) for source in range(initial, last)])


def gelu_tanh(value):
    inner = gelu_coef * (value + cubic_coef * value * value * value)
    return 0.5 * value * (1.0 + jnp.tanh(inner))


def gelu_slope(value):
    inner = gelu_coef * (value + cubic_coef * value * value * value)
    tangent = jnp.tanh(inner)
    return 0.5 * (1.0 + tangent) + 0.5 * value * (1.0 - tangent * tangent) * gelu_coef * (
        1.0 + 3.0 * cubic_coef * value * value
    )


def inverse_rms(value):
    return lax.rsqrt(jnp.mean(value * value, axis=-1, keepdims=True) + eps_norm)


def near_counts(near_tile, ext_count):
    rows = lax.broadcasted_iota(jnp.int32, (ext_count, near_tile.shape[1]), 0)
    total = jnp.zeros((ext_count, near_tile.shape[1]), jnp.float32)
    for index in range(near_tile.shape[0]):
        total = total + (near_tile[index][None, :] == rows).astype(jnp.float32)
    return total.astype(jnp.bfloat16)


def tile_forward(points_tile, halo_rows, counts_t, w_near, count_near):
    extended = jnp.concatenate([points_tile, halo_rows], axis=0)
    total = lax.dot_general(
        counts_t, extended, (((0,), (0,)), ((), ())), preferred_element_type=jnp.float32
    )
    average = (total * (1.0 / count_near)).astype(jnp.bfloat16)
    linear_part = jnp.dot(average, w_near, preferred_element_type=jnp.float32)
    lifted = (points_tile.astype(jnp.float32) + gelu_tanh(linear_part)).astype(jnp.bfloat16)
    return (average, linear_part, lifted)


def tile_backward(lifted_grad, average, linear_part, counts_t, w_near, count_near):
    tile_rows = lifted_grad.shape[0]
    act_grad = (lifted_grad.astype(jnp.float32) * gelu_slope(linear_part)).astype(jnp.bfloat16)
    near_grad = lax.dot_general(
        average, act_grad, (((0,), (0,)), ((), ())), preferred_element_type=jnp.float32
    )
    spread = lax.dot_general(
        act_grad, w_near, (((1,), (1,)), ((), ())), preferred_element_type=jnp.float32
    ) * (1.0 / count_near)
    spread_hi = spread.astype(jnp.bfloat16)
    spread_lo = (spread - spread_hi.astype(jnp.float32)).astype(jnp.bfloat16)
    ext_grad = jnp.dot(counts_t, spread_hi, preferred_element_type=jnp.float32) + jnp.dot(
        counts_t, spread_lo, preferred_element_type=jnp.float32
    )
    row_grad = lifted_grad.astype(jnp.float32) + ext_grad[:tile_rows]
    halo_grad = ext_grad[tile_rows:].astype(jnp.bfloat16)
    return (near_grad, row_grad, halo_grad)


def route_ranks(owner_tile, count, tiles):
    tile_rows = owner_tile.shape[0]
    index = jnp.arange(tile_rows, dtype=jnp.int32)
    live = index < count
    score = jnp.where(live, owner_tile * tile_rows + index, tiles * tile_rows + index)
    order = jnp.argsort(score, stable=True)
    members = (owner_tile[:, None] == jnp.arange(tiles, dtype=jnp.int32)[None, :]) & live[:, None]
    per_owner = jnp.sum(members.astype(jnp.int32), axis=0)
    starts = jnp.cumsum(per_owner) - per_owner
    sorted_owner = jnp.take(owner_tile, order)
    ranked = index - jnp.take(starts, sorted_owner)
    rank = jnp.zeros((tile_rows,), jnp.int32).at[order].set(ranked)
    return (rank, live)


def route_slots(owner_tile, count, tiles, capacity):
    tile_rows = owner_tile.shape[0]
    live = jnp.arange(tile_rows, dtype=jnp.int32) < count
    owner_ids = lax.broadcasted_iota(jnp.int32, (tile_rows, tiles), 1)
    members = ((owner_tile[:, None] == owner_ids) & live[:, None]).astype(jnp.bfloat16)
    before = (
        lax.broadcasted_iota(jnp.int32, (tile_rows, tile_rows), 1)
        < lax.broadcasted_iota(jnp.int32, (tile_rows, tile_rows), 0)
    ).astype(jnp.bfloat16)
    prefix = jnp.dot(before, members, preferred_element_type=jnp.float32)
    rank = jnp.sum(prefix * members.astype(jnp.float32), axis=1).astype(jnp.int32)
    return jnp.where(live, owner_tile * capacity + rank, tiles * capacity)


def one_hot_rows(ids, size):
    return (lax.broadcasted_iota(jnp.int32, (size, ids.shape[0]), 0) == ids[None, :]).astype(
        jnp.bfloat16
    )


def move_rows(picks, rows, transpose):
    dims = (((0,), (0,)), ((), ())) if transpose else (((1,), (0,)), ((), ()))
    return lax.dot_general(picks, rows, dims, preferred_element_type=jnp.float32).astype(rows.dtype)


def shift_down(rows):
    patches = rows.reshape(-1, PATCH, rows.shape[-1])
    moved = jnp.concatenate([jnp.zeros_like(patches[:, :1]), patches[:, :-1]], axis=1)
    return moved.reshape(rows.shape)


def shift_up(rows):
    patches = rows.reshape(-1, PATCH, rows.shape[-1])
    moved = jnp.concatenate([patches[:, 1:], jnp.zeros_like(patches[:, :1])], axis=1)
    return moved.reshape(rows.shape)


def block_taps(conv_w):
    groups, inner = (conv_w.shape[1], conv_w.shape[2])
    identity_blocks = jnp.eye(groups, dtype=conv_w.dtype)
    full = jnp.einsum("gh,ogab->ogahb", identity_blocks, conv_w)
    return full.reshape(conv_w.shape[0], groups * inner, groups * inner)


def grouped_weight(inputs, outputs, groups, inner):
    length = inputs.shape[0]
    left = inputs.reshape(length, groups, inner)
    right = outputs.reshape(length, groups, inner)
    return jnp.einsum("pga,pgb->gab", left, right, preferred_element_type=jnp.float32)


def tap_back(rows, tap):
    return lax.dot_general(rows, tap, (((1,), (1,)), ((), ())), preferred_element_type=jnp.float32)


def mlp_kernel(
    second_ref, grad_ref, state_ref, up_ref, down_ref, result_ref, sgrad_ref, upg_ref, downg_ref
):
    @pl.when(pl.program_id(0) == 0)
    def _():
        upg_ref[...] = jnp.zeros_like(upg_ref)
        downg_ref[...] = jnp.zeros_like(downg_ref)

    second = second_ref[...]
    out_grad = grad_ref[...]
    hidden_pre = jnp.dot(second, up_ref[...], preferred_element_type=jnp.float32)
    inner = gelu_coef * (hidden_pre + cubic_coef * hidden_pre * hidden_pre * hidden_pre)
    tangent = jnp.tanh(inner)
    hidden = (0.5 * hidden_pre * (1.0 + tangent)).astype(jnp.bfloat16)
    result_ref[...] = (
        state_ref[...] + jnp.dot(hidden, down_ref[...], preferred_element_type=jnp.float32)
    ).astype(jnp.bfloat16)
    downg_ref[...] += lax.dot_general(
        hidden, out_grad, (((0,), (0,)), ((), ())), preferred_element_type=jnp.float32
    )
    hidden_grad = lax.dot_general(
        out_grad, down_ref[...], (((1,), (1,)), ((), ())), preferred_element_type=jnp.float32
    ).astype(jnp.bfloat16)
    slope = 0.5 * (1.0 + tangent) + 0.5 * hidden_pre * (1.0 - tangent * tangent) * gelu_coef * (
        1.0 + 3.0 * cubic_coef * hidden_pre * hidden_pre
    )
    pre_grad = (hidden_grad.astype(jnp.float32) * slope).astype(jnp.bfloat16)
    upg_ref[...] += lax.dot_general(
        second, pre_grad, (((0,), (0,)), ((), ())), preferred_element_type=jnp.float32
    )
    sgrad_ref[...] = lax.dot_general(
        pre_grad, up_ref[...], (((1,), (1,)), ((), ())), preferred_element_type=jnp.float32
    ).astype(jnp.bfloat16)


def mlp_pass(second, out_grad, state, w_up, w_down, block_rows=512):
    rows, width = second.shape
    ffn = w_up.shape[1]
    row_block = pl.BlockSpec((block_rows, width), lambda step: (step, 0))
    whole = lambda shape: pl.BlockSpec(shape, lambda step: (0, 0))
    flops = 2 * rows * width * ffn * 6
    return pl.pallas_call(
        mlp_kernel,
        grid=(rows // block_rows,),
        in_specs=[row_block, row_block, row_block, whole((width, ffn)), whole((ffn, width))],
        out_specs=[row_block, row_block, whole((width, ffn)), whole((ffn, width))],
        out_shape=[
            jax.ShapeDtypeStruct((rows, width), jnp.bfloat16),
            jax.ShapeDtypeStruct((rows, width), jnp.bfloat16),
            jax.ShapeDtypeStruct((width, ffn), jnp.float32),
            jax.ShapeDtypeStruct((ffn, width), jnp.float32),
        ],
        compiler_params=pltpu.CompilerParams(dimension_semantics=("arbitrary",)),
        cost_estimate=pl.CostEstimate(
            flops=flops, transcendentals=rows * ffn, bytes_accessed=rows * width * 10 + 4 * width * ffn * 3
        ),
    )(second, out_grad, state, w_up, w_down)


def patch_pass(serial, out_grad, gain_one, conv_w, taps_full, gain_two, w_up, w_down):
    groups, inner = (conv_w.shape[1], conv_w.shape[2])
    serial_f = serial.astype(jnp.float32)
    scale_one = inverse_rms(serial_f)
    normed = (serial_f * scale_one * gain_one).astype(jnp.bfloat16)
    taps = (shift_down(normed), normed, shift_up(normed))
    mixed = (
        jnp.dot(taps[0], taps_full[0], preferred_element_type=jnp.float32)
        + jnp.dot(taps[1], taps_full[1], preferred_element_type=jnp.float32)
        + jnp.dot(taps[2], taps_full[2], preferred_element_type=jnp.float32)
    )
    state = serial_f + mixed
    scale_two = inverse_rms(state)
    second = (state * scale_two * gain_two).astype(jnp.bfloat16)
    result, second_grad, up_grad, down_grad = mlp_pass(second, out_grad, state, w_up, w_down)
    unit_two = state * scale_two
    weighted_two = second_grad.astype(jnp.float32) * gain_two
    gain_two_grad = jnp.sum(second_grad.astype(jnp.float32) * unit_two, axis=0)
    state_grad = out_grad.astype(jnp.float32) + scale_two * (
        weighted_two - unit_two * jnp.mean(weighted_two * unit_two, axis=-1, keepdims=True)
    )
    mixed_grad = state_grad.astype(jnp.bfloat16)
    conv_grad = jnp.stack(
        [
            grouped_weight(taps[0], mixed_grad, groups, inner),
            grouped_weight(taps[1], mixed_grad, groups, inner),
            grouped_weight(taps[2], mixed_grad, groups, inner),
        ],
        axis=0,
    )
    normed_grad = (
        shift_up(tap_back(mixed_grad, taps_full[0]))
        + tap_back(mixed_grad, taps_full[1])
        + shift_down(tap_back(mixed_grad, taps_full[2]))
    ).astype(jnp.bfloat16)
    unit_one = serial_f * scale_one
    weighted_one = normed_grad.astype(jnp.float32) * gain_one
    gain_one_grad = jnp.sum(normed_grad.astype(jnp.float32) * unit_one, axis=0)
    serial_grad = (
        state_grad
        + scale_one
        * (weighted_one - unit_one * jnp.mean(weighted_one * unit_one, axis=-1, keepdims=True))
    ).astype(jnp.bfloat16)
    return (result, serial_grad, (gain_one_grad, conv_grad, gain_two_grad, up_grad, down_grad))


def all_sum(flat, axes):
    devices = lax.axis_size(axes)
    chunk = -(-flat.shape[0] // (devices * 1024)) * 1024
    padded = jnp.pad(flat, (0, devices * chunk - flat.shape[0])).reshape(devices, chunk // 128, 128)
    pieces = lax.all_to_all(padded, axes, split_axis=0, concat_axis=0, tiled=True)
    part = jnp.sum(pieces, axis=0)
    spread = jnp.broadcast_to(part[None], (devices,) + part.shape)
    whole = lax.all_to_all(spread, axes, split_axis=0, concat_axis=0, tiled=True)
    return whole.reshape(-1)[: flat.shape[0]]


def pair_sum(flat, group):
    devices = lax.axis_size(group)
    chunk = -(-flat.shape[0] // (2 * devices * 1024)) * 1024
    halves = jnp.pad(flat, (0, 2 * devices * chunk - flat.shape[0])).reshape(2, devices * chunk)
    core = lax.axis_index("core")
    swap = [(0, 1), (1, 0)]
    mine = jnp.where(core == 0, halves[0], halves[1])
    theirs = jnp.where(core == 0, halves[1], halves[0])
    half_sum = mine + lax.ppermute(theirs, "core", swap)
    total = all_sum(half_sum, group)
    other = lax.ppermute(total, "core", swap)
    whole = jnp.where(core == 0, jnp.concatenate([total, other]), jnp.concatenate([other, total]))
    return whole[: flat.shape[0]]


def pass_columns(rows, shift_by):
    return shifted(rows, "tx", shift_by)


def pass_lines(rows, shift_by):
    return shifted(rows, LINES, shift_by)


def body(
    points,
    counts,
    owner,
    zorder,
    border,
    near,
    w_near,
    gain_one,
    conv_w,
    gain_two,
    w_up,
    w_down,
    grad_out,
):
    points_tile = points[0]
    tile_rows, width = points_tile.shape
    lists = border[0]
    border_rows = lists.shape[1]
    cols_count = lax.axis_size("tx")
    lines_count = lax.axis_size(LINES)
    tiles = cols_count * lines_count
    recv_rows = zorder.shape[1]
    capacity = recv_rows // tiles
    near_tile = near[0]
    owner_tile = owner[0]
    sent = jnp.take(points_tile, lists.reshape(-1), axis=0).reshape(4, border_rows, width)
    halo = jnp.concatenate(
        [
            pass_columns(sent[0], -1),
            pass_columns(sent[1], 1),
            pass_lines(sent[2], -1),
            pass_lines(sent[3], 1),
        ],
        axis=0,
    )
    count_near = near_tile.shape[0]
    counts_t = near_counts(near_tile, tile_rows + 4 * border_rows)
    average, linear_part, lifted = tile_forward(points_tile, halo, counts_t, w_near, count_near)
    slots = route_slots(owner_tile, counts[0], tiles, capacity)
    slot_picks = one_hot_rows(slots, tiles * capacity)
    order_picks = one_hot_rows(zorder[0], recv_rows).T
    payload = jnp.concatenate([lifted, grad_out[0]], axis=1)
    outgoing = move_rows(slot_picks, payload, False)
    incoming = lax.all_to_all(outgoing, ALL, split_axis=0, concat_axis=0, tiled=True)
    serial_both = move_rows(order_picks, incoming, False)
    taps_full = block_taps(conv_w)

    results, serial_grads, sums = patch_pass(
        serial_both[:, :width], serial_both[:, width:], gain_one, conv_w, taps_full, gain_two, w_up, w_down
    )
    back = jnp.concatenate(
        [results.reshape(recv_rows, width), serial_grads.reshape(recv_rows, width)], axis=1
    )
    back_slots = move_rows(order_picks, back, True)
    returned = lax.all_to_all(back_slots, ALL, split_axis=0, concat_axis=0, tiled=True)
    back_rows = move_rows(slot_picks, returned, True)
    out_rows = back_rows[:, :width]
    lifted_grad = back_rows[:, width:]
    patch_flat = jnp.concatenate(
        [sums[0], sums[2], sums[1].reshape(-1), sums[3].reshape(-1), sums[4].reshape(-1)]
    )
    near_grad, row_grad, halo_grad = tile_backward(
        lifted_grad, average, linear_part, counts_t, w_near, count_near
    )
    came_back = (
        pass_columns(halo_grad[0:border_rows], 1),
        pass_columns(halo_grad[border_rows : 2 * border_rows], -1),
        pass_lines(halo_grad[2 * border_rows : 3 * border_rows], 1),
        pass_lines(halo_grad[3 * border_rows : 4 * border_rows], -1),
    )
    for direction in range(4):
        row_grad = row_grad.at[lists[direction]].add(came_back[direction].astype(jnp.float32))
    grads_flat = jnp.concatenate([near_grad.reshape(-1), patch_flat])
    row_grad, grads_flat = lax.optimization_barrier((row_grad.astype(jnp.bfloat16), grads_flat))
    grads_total = pair_sum(grads_flat, ("tx", "tyc"))
    near_sum = grads_total[: near_grad.size].reshape(near_grad.shape)
    patch_total = grads_total[near_grad.size :]
    sizes = [width, width, conv_w.size, w_up.size, w_down.size]
    shapes = [(width,), (width,), conv_w.shape, w_up.shape, w_down.shape]
    offsets = [sum(sizes[:index]) for index in range(len(sizes))]
    gain_one_sum, gain_two_sum, conv_sum, up_sum, down_sum = [
        patch_total[start : start + size].reshape(shape)
        for start, size, shape in zip(offsets, sizes, shapes)
    ]
    totals = (gain_one_sum, conv_sum, gain_two_sum, up_sum, down_sum)
    scale = 1.0 / math.sqrt(tiles * tile_rows)
    return (
        out_rows[None],
        row_grad.astype(jnp.bfloat16)[None],
        near_sum * scale,
        totals[0] * scale,
        totals[1] * scale,
        totals[2] * scale,
        totals[3] * scale,
        totals[4] * scale,
    )


def solution(mesh):
    placed = (
        P(ALL, None, None),
        P(ALL),
        P(ALL, None),
        P(ALL, None),
        P(ALL, None, None),
        P(ALL, None, None),
        P(),
        P(),
        P(),
        P(),
        P(),
        P(),
        P(ALL, None, None),
    )
    return jax.shard_map(
        body,
        mesh=Mesh(mesh.devices.reshape(mesh.shape["tx"], -1, 2), ALL),
        in_specs=placed,
        out_specs=(
            P(ALL, None, None),
            P(ALL, None, None),
            P(),
            P(),
            P(),
            P(),
            P(),
            P(),
        ),
        check_vma=False,
    )
```

```python
import math

import jax
import jax.numpy as jnp
from jax import lax
from jax.experimental import pallas as pl
from jax.experimental.pallas import tpu as pltpu
from jax.sharding import Mesh, PartitionSpec as P

PATCH = 1024
LINES = ("tyc", "core")
ALL = ("tx",) + LINES


eps_norm = 1e-06
gelu_coef = 0.7978845608028654
cubic_coef = 0.044715


def shifted(value, axis, steps):
    count = lax.axis_size(axis)
    initial, last = (max(0, -steps), min(count, count - steps))
    return lax.ppermute(value, axis, [(source, source + steps) for source in range(initial, last)])


def gelu_tanh(value):
    inner = gelu_coef * (value + cubic_coef * value * value * value)
    return 0.5 * value * (1.0 + jnp.tanh(inner))


def gelu_slope(value):
    inner = gelu_coef * (value + cubic_coef * value * value * value)
    tangent = jnp.tanh(inner)
    return 0.5 * (1.0 + tangent) + 0.5 * value * (1.0 - tangent * tangent) * gelu_coef * (
        1.0 + 3.0 * cubic_coef * value * value
    )


def inverse_rms(value):
    return lax.rsqrt(jnp.mean(value * value, axis=-1, keepdims=True) + eps_norm)


def near_counts(near_tile, ext_count):
    rows = lax.broadcasted_iota(jnp.int32, (ext_count, near_tile.shape[1]), 0)
    total = jnp.zeros((ext_count, near_tile.shape[1]), jnp.float32)
    for index in range(near_tile.shape[0]):
        total = total + (near_tile[index][None, :] == rows).astype(jnp.float32)
    return total.astype(jnp.bfloat16)


def tile_forward(points_tile, halo_rows, counts_t, w_near, count_near):
    extended = jnp.concatenate([points_tile, halo_rows], axis=0)
    total = lax.dot_general(
        counts_t, extended, (((0,), (0,)), ((), ())), preferred_element_type=jnp.float32
    )
    average = (total * (1.0 / count_near)).astype(jnp.bfloat16)
    linear_part = jnp.dot(average, w_near, preferred_element_type=jnp.float32)
    lifted = (points_tile.astype(jnp.float32) + gelu_tanh(linear_part)).astype(jnp.bfloat16)
    return (average, linear_part, lifted)


def tile_backward(lifted_grad, average, linear_part, counts_t, w_near, count_near):
    tile_rows = lifted_grad.shape[0]
    act_grad = (lifted_grad.astype(jnp.float32) * gelu_slope(linear_part)).astype(jnp.bfloat16)
    near_grad = lax.dot_general(
        average, act_grad, (((0,), (0,)), ((), ())), preferred_element_type=jnp.float32
    )
    spread = lax.dot_general(
        act_grad, w_near, (((1,), (1,)), ((), ())), preferred_element_type=jnp.float32
    ) * (1.0 / count_near)
    spread_hi = spread.astype(jnp.bfloat16)
    spread_lo = (spread - spread_hi.astype(jnp.float32)).astype(jnp.bfloat16)
    ext_grad = jnp.dot(counts_t, spread_hi, preferred_element_type=jnp.float32) + jnp.dot(
        counts_t, spread_lo, preferred_element_type=jnp.float32
    )
    row_grad = lifted_grad.astype(jnp.float32) + ext_grad[:tile_rows]
    halo_grad = ext_grad[tile_rows:].astype(jnp.bfloat16)
    return (near_grad, row_grad, halo_grad)


def route_ranks(owner_tile, count, tiles):
    tile_rows = owner_tile.shape[0]
    index = jnp.arange(tile_rows, dtype=jnp.int32)
    live = index < count
    score = jnp.where(live, owner_tile * tile_rows + index, tiles * tile_rows + index)
    order = jnp.argsort(score, stable=True)
    members = (owner_tile[:, None] == jnp.arange(tiles, dtype=jnp.int32)[None, :]) & live[:, None]
    per_owner = jnp.sum(members.astype(jnp.int32), axis=0)
    starts = jnp.cumsum(per_owner) - per_owner
    sorted_owner = jnp.take(owner_tile, order)
    ranked = index - jnp.take(starts, sorted_owner)
    rank = jnp.zeros((tile_rows,), jnp.int32).at[order].set(ranked)
    return (rank, live)


def route_slots(owner_tile, count, tiles, capacity):
    tile_rows = owner_tile.shape[0]
    live = jnp.arange(tile_rows, dtype=jnp.int32) < count
    owner_ids = lax.broadcasted_iota(jnp.int32, (tile_rows, tiles), 1)
    members = ((owner_tile[:, None] == owner_ids) & live[:, None]).astype(jnp.bfloat16)
    before = (
        lax.broadcasted_iota(jnp.int32, (tile_rows, tile_rows), 1)
        < lax.broadcasted_iota(jnp.int32, (tile_rows, tile_rows), 0)
    ).astype(jnp.bfloat16)
    prefix = jnp.dot(before, members, preferred_element_type=jnp.float32)
    rank = jnp.sum(prefix * members.astype(jnp.float32), axis=1).astype(jnp.int32)
    return jnp.where(live, owner_tile * capacity + rank, tiles * capacity)


def one_hot_rows(ids, size):
    return (lax.broadcasted_iota(jnp.int32, (size, ids.shape[0]), 0) == ids[None, :]).astype(
        jnp.bfloat16
    )


def move_rows(picks, rows, transpose):
    dims = (((0,), (0,)), ((), ())) if transpose else (((1,), (0,)), ((), ()))
    return lax.dot_general(picks, rows, dims, preferred_element_type=jnp.float32).astype(rows.dtype)


def shift_down(rows):
    patches = rows.reshape(-1, PATCH, rows.shape[-1])
    moved = jnp.concatenate([jnp.zeros_like(patches[:, :1]), patches[:, :-1]], axis=1)
    return moved.reshape(rows.shape)


def shift_up(rows):
    patches = rows.reshape(-1, PATCH, rows.shape[-1])
    moved = jnp.concatenate([patches[:, 1:], jnp.zeros_like(patches[:, :1])], axis=1)
    return moved.reshape(rows.shape)


def block_taps(conv_w):
    groups, inner = (conv_w.shape[1], conv_w.shape[2])
    identity_blocks = jnp.eye(groups, dtype=conv_w.dtype)
    full = jnp.einsum("gh,ogab->ogahb", identity_blocks, conv_w)
    return full.reshape(conv_w.shape[0], groups * inner, groups * inner)


def grouped_weight(inputs, outputs, groups, inner):
    length = inputs.shape[0]
    left = inputs.reshape(length, groups, inner)
    right = outputs.reshape(length, groups, inner)
    return jnp.einsum("pga,pgb->gab", left, right, preferred_element_type=jnp.float32)


def tap_back(rows, tap):
    return lax.dot_general(rows, tap, (((1,), (1,)), ((), ())), preferred_element_type=jnp.float32)


def mlp_kernel(
    second_ref, grad_ref, state_ref, up_ref, down_ref, result_ref, sgrad_ref, upg_ref, downg_ref
):
    @pl.when(pl.program_id(0) == 0)
    def _():
        upg_ref[...] = jnp.zeros_like(upg_ref)
        downg_ref[...] = jnp.zeros_like(downg_ref)

    second = second_ref[...]
    out_grad = grad_ref[...]
    hidden_pre = jnp.dot(second, up_ref[...], preferred_element_type=jnp.float32)
    inner = gelu_coef * (hidden_pre + cubic_coef * hidden_pre * hidden_pre * hidden_pre)
    tangent = jnp.tanh(inner)
    hidden = (0.5 * hidden_pre * (1.0 + tangent)).astype(jnp.bfloat16)
    result_ref[...] = (
        state_ref[...] + jnp.dot(hidden, down_ref[...], preferred_element_type=jnp.float32)
    ).astype(jnp.bfloat16)
    downg_ref[...] += lax.dot_general(
        hidden, out_grad, (((0,), (0,)), ((), ())), preferred_element_type=jnp.float32
    )
    hidden_grad = lax.dot_general(
        out_grad, down_ref[...], (((1,), (1,)), ((), ())), preferred_element_type=jnp.float32
    ).astype(jnp.bfloat16)
    slope = 0.5 * (1.0 + tangent) + 0.5 * hidden_pre * (1.0 - tangent * tangent) * gelu_coef * (
        1.0 + 3.0 * cubic_coef * hidden_pre * hidden_pre
    )
    pre_grad = (hidden_grad.astype(jnp.float32) * slope).astype(jnp.bfloat16)
    upg_ref[...] += lax.dot_general(
        second, pre_grad, (((0,), (0,)), ((), ())), preferred_element_type=jnp.float32
    )
    sgrad_ref[...] = lax.dot_general(
        pre_grad, up_ref[...], (((1,), (1,)), ((), ())), preferred_element_type=jnp.float32
    ).astype(jnp.bfloat16)


def mlp_pass(second, out_grad, state, w_up, w_down, block_rows=512):
    rows, width = second.shape
    ffn = w_up.shape[1]
    row_block = pl.BlockSpec((block_rows, width), lambda step: (step, 0))
    whole = lambda shape: pl.BlockSpec(shape, lambda step: (0, 0))
    flops = 2 * rows * width * ffn * 6
    return pl.pallas_call(
        mlp_kernel,
        grid=(rows // block_rows,),
        in_specs=[
            row_block,
            pl.BlockSpec((block_rows, width), lambda step: (step, 1)),
            row_block,
            whole((width, ffn)),
            whole((ffn, width)),
        ],
        out_specs=[row_block, row_block, whole((width, ffn)), whole((ffn, width))],
        out_shape=[
            jax.ShapeDtypeStruct((rows, width), jnp.bfloat16),
            jax.ShapeDtypeStruct((rows, width), jnp.bfloat16),
            jax.ShapeDtypeStruct((width, ffn), jnp.float32),
            jax.ShapeDtypeStruct((ffn, width), jnp.float32),
        ],
        compiler_params=pltpu.CompilerParams(dimension_semantics=("arbitrary",)),
        cost_estimate=pl.CostEstimate(
            flops=flops, transcendentals=rows * ffn, bytes_accessed=rows * width * 10 + 4 * width * ffn * 3
        ),
    )(second, out_grad, state, w_up, w_down)


def patch_pass(serial, out_grad, both, gain_one, conv_w, taps_full, gain_two, w_up, w_down):
    groups, inner = (conv_w.shape[1], conv_w.shape[2])
    serial_f = serial.astype(jnp.float32)
    scale_one = inverse_rms(serial_f)
    normed = (serial_f * scale_one * gain_one).astype(jnp.bfloat16)
    taps = (shift_down(normed), normed, shift_up(normed))
    mixed = (
        jnp.dot(taps[0], taps_full[0], preferred_element_type=jnp.float32)
        + jnp.dot(taps[1], taps_full[1], preferred_element_type=jnp.float32)
        + jnp.dot(taps[2], taps_full[2], preferred_element_type=jnp.float32)
    )
    state = serial_f + mixed
    scale_two = inverse_rms(state)
    second = (state * scale_two * gain_two).astype(jnp.bfloat16)
    result, second_grad, up_grad, down_grad = mlp_pass(second, both, state, w_up, w_down)
    unit_two = state * scale_two
    weighted_two = second_grad.astype(jnp.float32) * gain_two
    gain_two_grad = jnp.sum(second_grad.astype(jnp.float32) * unit_two, axis=0)
    state_grad = out_grad.astype(jnp.float32) + scale_two * (
        weighted_two - unit_two * jnp.mean(weighted_two * unit_two, axis=-1, keepdims=True)
    )
    mixed_grad = state_grad.astype(jnp.bfloat16)
    conv_grad = jnp.stack(
        [
            grouped_weight(taps[0], mixed_grad, groups, inner),
            grouped_weight(taps[1], mixed_grad, groups, inner),
            grouped_weight(taps[2], mixed_grad, groups, inner),
        ],
        axis=0,
    )
    normed_grad = (
        shift_up(tap_back(mixed_grad, taps_full[0]))
        + tap_back(mixed_grad, taps_full[1])
        + shift_down(tap_back(mixed_grad, taps_full[2]))
    ).astype(jnp.bfloat16)
    unit_one = serial_f * scale_one
    weighted_one = normed_grad.astype(jnp.float32) * gain_one
    gain_one_grad = jnp.sum(normed_grad.astype(jnp.float32) * unit_one, axis=0)
    serial_grad = (
        state_grad
        + scale_one
        * (weighted_one - unit_one * jnp.mean(weighted_one * unit_one, axis=-1, keepdims=True))
    ).astype(jnp.bfloat16)
    return (result, serial_grad, (gain_one_grad, conv_grad, gain_two_grad, up_grad, down_grad))


def all_sum(flat, axes):
    devices = lax.axis_size(axes)
    chunk = -(-flat.shape[0] // (devices * 1024)) * 1024
    padded = jnp.pad(flat, (0, devices * chunk - flat.shape[0])).reshape(devices, chunk // 128, 128)
    pieces = lax.all_to_all(padded, axes, split_axis=0, concat_axis=0, tiled=True)
    part = jnp.sum(pieces, axis=0)
    spread = jnp.broadcast_to(part[None], (devices,) + part.shape)
    whole = lax.all_to_all(spread, axes, split_axis=0, concat_axis=0, tiled=True)
    return whole.reshape(-1)[: flat.shape[0]]


def pair_sum(flat, group):
    devices = lax.axis_size(group)
    chunk = -(-flat.shape[0] // (2 * devices * 1024)) * 1024
    halves = jnp.pad(flat, (0, 2 * devices * chunk - flat.shape[0])).reshape(2, devices * chunk)
    core = lax.axis_index("core")
    swap = [(0, 1), (1, 0)]
    mine = jnp.where(core == 0, halves[0], halves[1])
    theirs = jnp.where(core == 0, halves[1], halves[0])
    half_sum = mine + lax.ppermute(theirs, "core", swap)
    total = all_sum(half_sum, group)
    other = lax.ppermute(total, "core", swap)
    whole = jnp.where(core == 0, jnp.concatenate([total, other]), jnp.concatenate([other, total]))
    return whole[: flat.shape[0]]


def pass_columns(rows, shift_by):
    return shifted(rows, "tx", shift_by)


def pass_lines(rows, shift_by):
    return shifted(rows, LINES, shift_by)


def body(
    points,
    counts,
    owner,
    zorder,
    border,
    near,
    w_near,
    gain_one,
    conv_w,
    gain_two,
    w_up,
    w_down,
    grad_out,
):
    points_tile = points[0]
    tile_rows, width = points_tile.shape
    lists = border[0]
    border_rows = lists.shape[1]
    cols_count = lax.axis_size("tx")
    lines_count = lax.axis_size(LINES)
    tiles = cols_count * lines_count
    recv_rows = zorder.shape[1]
    capacity = recv_rows // tiles
    near_tile = near[0]
    owner_tile = owner[0]
    sent = jnp.take(points_tile, lists.reshape(-1), axis=0).reshape(4, border_rows, width)
    halo = jnp.concatenate(
        [
            pass_columns(sent[0], -1),
            pass_columns(sent[1], 1),
            pass_lines(sent[2], -1),
            pass_lines(sent[3], 1),
        ],
        axis=0,
    )
    count_near = near_tile.shape[0]
    counts_t = near_counts(near_tile, tile_rows + 4 * border_rows)
    average, linear_part, lifted = tile_forward(points_tile, halo, counts_t, w_near, count_near)
    slots = route_slots(owner_tile, counts[0], tiles, capacity)
    slot_picks = one_hot_rows(slots, tiles * capacity)
    order_picks = one_hot_rows(zorder[0], recv_rows).T
    payload = jnp.concatenate([lifted, grad_out[0]], axis=1)
    outgoing = move_rows(slot_picks, payload, False)
    incoming = lax.all_to_all(outgoing, ALL, split_axis=0, concat_axis=0, tiled=True)
    serial_both = move_rows(order_picks, incoming, False)
    taps_full = block_taps(conv_w)

    results, serial_grads, sums = patch_pass(
        serial_both[:, :width], serial_both[:, width:], serial_both, gain_one, conv_w, taps_full, gain_two, w_up, w_down
    )
    back = jnp.concatenate(
        [results.reshape(recv_rows, width), serial_grads.reshape(recv_rows, width)], axis=1
    )
    back_slots = move_rows(order_picks, back, True)
    returned = lax.all_to_all(back_slots, ALL, split_axis=0, concat_axis=0, tiled=True)
    back_rows = move_rows(slot_picks, returned, True)
    out_rows = back_rows[:, :width]
    lifted_grad = back_rows[:, width:]
    patch_flat = jnp.concatenate(
        [sums[0], sums[2], sums[1].reshape(-1), sums[3].reshape(-1), sums[4].reshape(-1)]
    )
    near_grad, row_grad, halo_grad = tile_backward(
        lifted_grad, average, linear_part, counts_t, w_near, count_near
    )
    came_back = (
        pass_columns(halo_grad[0:border_rows], 1),
        pass_columns(halo_grad[border_rows : 2 * border_rows], -1),
        pass_lines(halo_grad[2 * border_rows : 3 * border_rows], 1),
        pass_lines(halo_grad[3 * border_rows : 4 * border_rows], -1),
    )
    for direction in range(4):
        row_grad = row_grad.at[lists[direction]].add(came_back[direction].astype(jnp.float32))
    grads_total = pair_sum(jnp.concatenate([near_grad.reshape(-1), patch_flat]), ("tx", "tyc"))
    near_sum = grads_total[: near_grad.size].reshape(near_grad.shape)
    patch_total = grads_total[near_grad.size :]
    sizes = [width, width, conv_w.size, w_up.size, w_down.size]
    shapes = [(width,), (width,), conv_w.shape, w_up.shape, w_down.shape]
    offsets = [sum(sizes[:index]) for index in range(len(sizes))]
    gain_one_sum, gain_two_sum, conv_sum, up_sum, down_sum = [
        patch_total[start : start + size].reshape(shape)
        for start, size, shape in zip(offsets, sizes, shapes)
    ]
    totals = (gain_one_sum, conv_sum, gain_two_sum, up_sum, down_sum)
    scale = 1.0 / math.sqrt(tiles * tile_rows)
    return (
        out_rows[None],
        row_grad.astype(jnp.bfloat16)[None],
        near_sum * scale,
        totals[0] * scale,
        totals[1] * scale,
        totals[2] * scale,
        totals[3] * scale,
        totals[4] * scale,
    )


def solution(mesh):
    placed = (
        P(ALL, None, None),
        P(ALL),
        P(ALL, None),
        P(ALL, None),
        P(ALL, None, None),
        P(ALL, None, None),
        P(),
        P(),
        P(),
        P(),
        P(),
        P(),
        P(ALL, None, None),
    )
    return jax.shard_map(
        body,
        mesh=Mesh(mesh.devices.reshape(mesh.shape["tx"], -1, 2), ALL),
        in_specs=placed,
        out_specs=(
            P(ALL, None, None),
            P(ALL, None, None),
            P(),
            P(),
            P(),
            P(),
            P(),
            P(),
        ),
        check_vma=False,
    )
```

```python
import math

import jax
import jax.numpy as jnp
from jax import lax
from jax.experimental import pallas as pl
from jax.experimental.pallas import tpu as pltpu
from jax.sharding import Mesh, PartitionSpec as P

PATCH = 1024
LINES = ("tyc", "core")
ALL = ("tx",) + LINES


eps_norm = 1e-06
gelu_coef = 0.7978845608028654
cubic_coef = 0.044715


def shifted(value, axis, steps):
    count = lax.axis_size(axis)
    initial, last = (max(0, -steps), min(count, count - steps))
    return lax.ppermute(value, axis, [(source, source + steps) for source in range(initial, last)])


def gelu_tanh(value):
    inner = gelu_coef * (value + cubic_coef * value * value * value)
    return 0.5 * value * (1.0 + jnp.tanh(inner))


def gelu_slope(value):
    inner = gelu_coef * (value + cubic_coef * value * value * value)
    tangent = jnp.tanh(inner)
    return 0.5 * (1.0 + tangent) + 0.5 * value * (1.0 - tangent * tangent) * gelu_coef * (
        1.0 + 3.0 * cubic_coef * value * value
    )


def inverse_rms(value):
    return lax.rsqrt(jnp.mean(value * value, axis=-1, keepdims=True) + eps_norm)


def near_counts(near_tile, ext_count):
    rows = lax.broadcasted_iota(jnp.int32, (ext_count, near_tile.shape[1]), 0)
    total = jnp.zeros((ext_count, near_tile.shape[1]), jnp.float32)
    for index in range(near_tile.shape[0]):
        total = total + (near_tile[index][None, :] == rows).astype(jnp.float32)
    return total.astype(jnp.bfloat16)


def tile_forward(points_tile, halo_rows, counts_t, w_near, count_near):
    extended = jnp.concatenate([points_tile, halo_rows], axis=0)
    total = lax.dot_general(
        counts_t, extended, (((0,), (0,)), ((), ())), preferred_element_type=jnp.float32
    )
    average = (total * (1.0 / count_near)).astype(jnp.bfloat16)
    linear_part = jnp.dot(average, w_near, preferred_element_type=jnp.float32)
    lifted = (points_tile.astype(jnp.float32) + gelu_tanh(linear_part)).astype(jnp.bfloat16)
    return (average, linear_part, lifted)


def tile_backward(lifted_grad, average, linear_part, counts_t, w_near, count_near):
    tile_rows = lifted_grad.shape[0]
    act_grad = (lifted_grad.astype(jnp.float32) * gelu_slope(linear_part)).astype(jnp.bfloat16)
    near_grad = lax.dot_general(
        average, act_grad, (((0,), (0,)), ((), ())), preferred_element_type=jnp.float32
    )
    spread = lax.dot_general(
        act_grad, w_near, (((1,), (1,)), ((), ())), preferred_element_type=jnp.float32
    ) * (1.0 / count_near)
    spread_hi = spread.astype(jnp.bfloat16)
    spread_lo = (spread - spread_hi.astype(jnp.float32)).astype(jnp.bfloat16)
    ext_grad = jnp.dot(counts_t, spread_hi, preferred_element_type=jnp.float32) + jnp.dot(
        counts_t, spread_lo, preferred_element_type=jnp.float32
    )
    row_grad = lifted_grad.astype(jnp.float32) + ext_grad[:tile_rows]
    halo_grad = ext_grad[tile_rows:].astype(jnp.bfloat16)
    return (near_grad, row_grad, halo_grad)


def route_ranks(owner_tile, count, tiles):
    tile_rows = owner_tile.shape[0]
    index = jnp.arange(tile_rows, dtype=jnp.int32)
    live = index < count
    score = jnp.where(live, owner_tile * tile_rows + index, tiles * tile_rows + index)
    order = jnp.argsort(score, stable=True)
    members = (owner_tile[:, None] == jnp.arange(tiles, dtype=jnp.int32)[None, :]) & live[:, None]
    per_owner = jnp.sum(members.astype(jnp.int32), axis=0)
    starts = jnp.cumsum(per_owner) - per_owner
    sorted_owner = jnp.take(owner_tile, order)
    ranked = index - jnp.take(starts, sorted_owner)
    rank = jnp.zeros((tile_rows,), jnp.int32).at[order].set(ranked)
    return (rank, live)


def route_slots(owner_tile, count, tiles, capacity):
    tile_rows = owner_tile.shape[0]
    live = jnp.arange(tile_rows, dtype=jnp.int32) < count
    owner_ids = lax.broadcasted_iota(jnp.int32, (tile_rows, tiles), 1)
    members = ((owner_tile[:, None] == owner_ids) & live[:, None]).astype(jnp.bfloat16)
    before = (
        lax.broadcasted_iota(jnp.int32, (tile_rows, tile_rows), 1)
        < lax.broadcasted_iota(jnp.int32, (tile_rows, tile_rows), 0)
    ).astype(jnp.bfloat16)
    prefix = jnp.dot(before, members, preferred_element_type=jnp.float32)
    rank = jnp.sum(prefix * members.astype(jnp.float32), axis=1).astype(jnp.int32)
    return jnp.where(live, owner_tile * capacity + rank, tiles * capacity)


def one_hot_rows(ids, size):
    return (lax.broadcasted_iota(jnp.int32, (size, ids.shape[0]), 0) == ids[None, :]).astype(
        jnp.bfloat16
    )


def move_rows(picks, rows, transpose):
    dims = (((0,), (0,)), ((), ())) if transpose else (((1,), (0,)), ((), ()))
    return lax.dot_general(picks, rows, dims, preferred_element_type=jnp.float32).astype(rows.dtype)


def shift_down(rows):
    patches = rows.reshape(-1, PATCH, rows.shape[-1])
    moved = jnp.concatenate([jnp.zeros_like(patches[:, :1]), patches[:, :-1]], axis=1)
    return moved.reshape(rows.shape)


def shift_up(rows):
    patches = rows.reshape(-1, PATCH, rows.shape[-1])
    moved = jnp.concatenate([patches[:, 1:], jnp.zeros_like(patches[:, :1])], axis=1)
    return moved.reshape(rows.shape)


def block_taps(conv_w):
    groups, inner = (conv_w.shape[1], conv_w.shape[2])
    identity_blocks = jnp.eye(groups, dtype=conv_w.dtype)
    full = jnp.einsum("gh,ogab->ogahb", identity_blocks, conv_w)
    return full.reshape(conv_w.shape[0], groups * inner, groups * inner)


def grouped_weight(inputs, outputs, groups, inner):
    length = inputs.shape[0]
    left = inputs.reshape(length, groups, inner)
    right = outputs.reshape(length, groups, inner)
    return jnp.einsum("pga,pgb->gab", left, right, preferred_element_type=jnp.float32)


def tap_back(rows, tap):
    return lax.dot_general(rows, tap, (((1,), (1,)), ((), ())), preferred_element_type=jnp.float32)


def mlp_kernel(
    second_ref, grad_ref, state_ref, up_ref, down_ref, result_ref, sgrad_ref, upg_ref, downg_ref
):
    @pl.when(pl.program_id(0) == 0)
    def _():
        upg_ref[...] = jnp.zeros_like(upg_ref)
        downg_ref[...] = jnp.zeros_like(downg_ref)

    second = second_ref[...]
    out_grad = grad_ref[...]
    hidden_pre = jnp.dot(second, up_ref[...], preferred_element_type=jnp.float32)
    inner = gelu_coef * (hidden_pre + cubic_coef * hidden_pre * hidden_pre * hidden_pre)
    tangent = jnp.tanh(inner)
    hidden = (0.5 * hidden_pre * (1.0 + tangent)).astype(jnp.bfloat16)
    result_ref[...] = (
        state_ref[...] + jnp.dot(hidden, down_ref[...], preferred_element_type=jnp.float32)
    ).astype(jnp.bfloat16)
    downg_ref[...] += lax.dot_general(
        hidden, out_grad, (((0,), (0,)), ((), ())), preferred_element_type=jnp.float32
    )
    hidden_grad = lax.dot_general(
        out_grad, down_ref[...], (((1,), (1,)), ((), ())), preferred_element_type=jnp.float32
    ).astype(jnp.bfloat16)
    slope = 0.5 * (1.0 + tangent) + 0.5 * hidden_pre * (1.0 - tangent * tangent) * gelu_coef * (
        1.0 + 3.0 * cubic_coef * hidden_pre * hidden_pre
    )
    pre_grad = (hidden_grad.astype(jnp.float32) * slope).astype(jnp.bfloat16)
    upg_ref[...] += lax.dot_general(
        second, pre_grad, (((0,), (0,)), ((), ())), preferred_element_type=jnp.float32
    )
    sgrad_ref[...] = lax.dot_general(
        pre_grad, up_ref[...], (((1,), (1,)), ((), ())), preferred_element_type=jnp.float32
    ).astype(jnp.bfloat16)


def mlp_pass(second, out_grad, state, w_up, w_down, block_rows=512):
    rows, width = second.shape
    ffn = w_up.shape[1]
    row_block = pl.BlockSpec((block_rows, width), lambda step: (step, 0))
    whole = lambda shape: pl.BlockSpec(shape, lambda step: (0, 0))
    flops = 2 * rows * width * ffn * 6
    return pl.pallas_call(
        mlp_kernel,
        grid=(rows // block_rows,),
        in_specs=[
            row_block,
            pl.BlockSpec((block_rows, width), lambda step: (step, 1)),
            row_block,
            whole((width, ffn)),
            whole((ffn, width)),
        ],
        out_specs=[row_block, row_block, whole((width, ffn)), whole((ffn, width))],
        out_shape=[
            jax.ShapeDtypeStruct((rows, width), jnp.bfloat16),
            jax.ShapeDtypeStruct((rows, width), jnp.bfloat16),
            jax.ShapeDtypeStruct((width, ffn), jnp.float32),
            jax.ShapeDtypeStruct((ffn, width), jnp.float32),
        ],
        compiler_params=pltpu.CompilerParams(dimension_semantics=("arbitrary",)),
        cost_estimate=pl.CostEstimate(
            flops=flops, transcendentals=rows * ffn, bytes_accessed=rows * width * 10 + 4 * width * ffn * 3
        ),
    )(second, out_grad, state, w_up, w_down)


def patch_pass(serial, out_grad, both, gain_one, conv_w, taps_full, gain_two, w_up, w_down):
    groups, inner = (conv_w.shape[1], conv_w.shape[2])
    serial_f = serial.astype(jnp.float32)
    scale_one = inverse_rms(serial_f)
    normed = (serial_f * scale_one * gain_one).astype(jnp.bfloat16)
    taps = (shift_down(normed), normed, shift_up(normed))
    mixed = (
        jnp.dot(taps[0], taps_full[0], preferred_element_type=jnp.float32)
        + jnp.dot(taps[1], taps_full[1], preferred_element_type=jnp.float32)
        + jnp.dot(taps[2], taps_full[2], preferred_element_type=jnp.float32)
    )
    state = serial_f + mixed
    scale_two = inverse_rms(state)
    second = (state * scale_two * gain_two).astype(jnp.bfloat16)
    result, second_grad, up_grad, down_grad = mlp_pass(second, both, state, w_up, w_down)
    unit_two = state * scale_two
    weighted_two = second_grad.astype(jnp.float32) * gain_two
    gain_two_grad = jnp.sum(second_grad.astype(jnp.float32) * unit_two, axis=0)
    state_grad = out_grad.astype(jnp.float32) + scale_two * (
        weighted_two - unit_two * jnp.mean(weighted_two * unit_two, axis=-1, keepdims=True)
    )
    mixed_grad = state_grad.astype(jnp.bfloat16)
    conv_grad = jnp.stack(
        [
            grouped_weight(taps[0], mixed_grad, groups, inner),
            grouped_weight(taps[1], mixed_grad, groups, inner),
            grouped_weight(taps[2], mixed_grad, groups, inner),
        ],
        axis=0,
    )
    normed_grad = (
        shift_up(tap_back(mixed_grad, taps_full[0]))
        + tap_back(mixed_grad, taps_full[1])
        + shift_down(tap_back(mixed_grad, taps_full[2]))
    ).astype(jnp.bfloat16)
    unit_one = serial_f * scale_one
    weighted_one = normed_grad.astype(jnp.float32) * gain_one
    gain_one_grad = jnp.sum(normed_grad.astype(jnp.float32) * unit_one, axis=0)
    serial_grad = (
        state_grad
        + scale_one
        * (weighted_one - unit_one * jnp.mean(weighted_one * unit_one, axis=-1, keepdims=True))
    ).astype(jnp.bfloat16)
    return (result, serial_grad, (gain_one_grad, conv_grad, gain_two_grad, up_grad, down_grad))


def all_sum(flat, axes):
    devices = lax.axis_size(axes)
    chunk = -(-flat.shape[0] // (devices * 1024)) * 1024
    padded = jnp.pad(flat, (0, devices * chunk - flat.shape[0])).reshape(devices, chunk // 128, 128)
    pieces = lax.all_to_all(padded, axes, split_axis=0, concat_axis=0, tiled=True)
    part = jnp.sum(pieces, axis=0)
    spread = jnp.broadcast_to(part[None], (devices,) + part.shape)
    whole = lax.all_to_all(spread, axes, split_axis=0, concat_axis=0, tiled=True)
    return whole.reshape(-1)[: flat.shape[0]]


def pair_sum(flat, group):
    devices = lax.axis_size(group)
    chunk = -(-flat.shape[0] // (2 * devices * 1024)) * 1024
    halves = jnp.pad(flat, (0, 2 * devices * chunk - flat.shape[0])).reshape(2, devices * chunk)
    core = lax.axis_index("core")
    swap = [(0, 1), (1, 0)]
    mine = jnp.where(core == 0, halves[0], halves[1])
    theirs = jnp.where(core == 0, halves[1], halves[0])
    half_sum = mine + lax.ppermute(theirs, "core", swap)
    total = all_sum(half_sum, group)
    other = lax.ppermute(total, "core", swap)
    whole = jnp.where(core == 0, jnp.concatenate([total, other]), jnp.concatenate([other, total]))
    return whole[: flat.shape[0]]


def pass_columns(rows, shift_by):
    return shifted(rows, "tx", shift_by)


def pass_lines(rows, shift_by):
    return shifted(rows, LINES, shift_by)


def body(
    points,
    counts,
    owner,
    zorder,
    border,
    near,
    w_near,
    gain_one,
    conv_w,
    gain_two,
    w_up,
    w_down,
    grad_out,
):
    points_tile = points[0]
    tile_rows, width = points_tile.shape
    lists = border[0]
    border_rows = lists.shape[1]
    cols_count = lax.axis_size("tx")
    lines_count = lax.axis_size(LINES)
    tiles = cols_count * lines_count
    recv_rows = zorder.shape[1]
    capacity = recv_rows // tiles
    near_tile = near[0]
    owner_tile = owner[0]
    sent = jnp.take(points_tile, lists.reshape(-1), axis=0).reshape(4, border_rows, width)
    halo = jnp.concatenate(
        [
            pass_columns(sent[0], -1),
            pass_columns(sent[1], 1),
            pass_lines(sent[2], -1),
            pass_lines(sent[3], 1),
        ],
        axis=0,
    )
    count_near = near_tile.shape[0]
    counts_t = near_counts(near_tile, tile_rows + 4 * border_rows)
    average, linear_part, lifted = tile_forward(points_tile, halo, counts_t, w_near, count_near)
    slots = route_slots(owner_tile, counts[0], tiles, capacity)
    slot_picks = one_hot_rows(slots, tiles * capacity)
    order_picks = one_hot_rows(zorder[0], recv_rows).T
    payload = jnp.concatenate([lifted, grad_out[0]], axis=1)
    outgoing = move_rows(slot_picks, payload, False)
    incoming = lax.all_to_all(outgoing, ALL, split_axis=0, concat_axis=0, tiled=True)
    serial_both = move_rows(order_picks, incoming, False)
    taps_full = block_taps(conv_w)

    results, serial_grads, sums = patch_pass(
        serial_both[:, :width], serial_both[:, width:], serial_both, gain_one, conv_w, taps_full, gain_two, w_up, w_down
    )
    back = jnp.concatenate(
        [results.reshape(recv_rows, width), serial_grads.reshape(recv_rows, width)], axis=1
    )
    back_slots = move_rows(order_picks, back, True)
    returned = lax.all_to_all(back_slots, ALL, split_axis=0, concat_axis=0, tiled=True)
    back_rows = move_rows(slot_picks, returned, True)
    out_rows = back_rows[:, :width]
    lifted_grad = back_rows[:, width:]
    patch_flat = jnp.concatenate(
        [sums[0], sums[2], sums[1].reshape(-1), sums[3].reshape(-1), sums[4].reshape(-1)]
    )
    near_grad, row_grad, halo_grad = tile_backward(
        lifted_grad, average, linear_part, counts_t, w_near, count_near
    )
    came_back = (
        pass_columns(halo_grad[0:border_rows], 1),
        pass_columns(halo_grad[border_rows : 2 * border_rows], -1),
        pass_lines(halo_grad[2 * border_rows : 3 * border_rows], 1),
        pass_lines(halo_grad[3 * border_rows : 4 * border_rows], -1),
    )
    for direction in range(4):
        row_grad = row_grad.at[lists[direction]].add(came_back[direction].astype(jnp.float32))
    scale = 1.0 / math.sqrt(tiles * tile_rows)
    grads_total = pair_sum(
        jnp.concatenate([near_grad.reshape(-1), patch_flat]) * scale, ("tx", "tyc")
    )
    near_sum = grads_total[: near_grad.size].reshape(near_grad.shape)
    patch_total = grads_total[near_grad.size :]
    sizes = [width, width, conv_w.size, w_up.size, w_down.size]
    shapes = [(width,), (width,), conv_w.shape, w_up.shape, w_down.shape]
    offsets = [sum(sizes[:index]) for index in range(len(sizes))]
    gain_one_sum, gain_two_sum, conv_sum, up_sum, down_sum = [
        patch_total[start : start + size].reshape(shape)
        for start, size, shape in zip(offsets, sizes, shapes)
    ]
    totals = (gain_one_sum, conv_sum, gain_two_sum, up_sum, down_sum)
    return (
        out_rows[None],
        row_grad.astype(jnp.bfloat16)[None],
        near_sum,
        totals[0],
        totals[1],
        totals[2],
        totals[3],
        totals[4],
    )


def solution(mesh):
    placed = (
        P(ALL, None, None),
        P(ALL),
        P(ALL, None),
        P(ALL, None),
        P(ALL, None, None),
        P(ALL, None, None),
        P(),
        P(),
        P(),
        P(),
        P(),
        P(),
        P(ALL, None, None),
    )
    return jax.shard_map(
        body,
        mesh=Mesh(mesh.devices.reshape(mesh.shape["tx"], -1, 2), ALL),
        in_specs=placed,
        out_specs=(
            P(ALL, None, None),
            P(ALL, None, None),
            P(),
            P(),
            P(),
            P(),
            P(),
            P(),
        ),
        check_vma=False,
    )
```
